32 devices in a mesh: ctx: 8 (over z, y), fsdp: 4 (over x, core).
Axes of the slice: x: 2, y: 2, z: 4, core: 2. Of those that a mesh axis runs over, the one named last changes fastest.
Arguments:
- tokens: bfloat16 [4, 1024, 576], P('fsdp', 'ctx'), may hold values from -6 to 6
- pair_of: int32 [4, 8], P('fsdp'), may hold values from 0 to 7, each once within a row
- gain_attn: bfloat16 [576], P('ctx'), may hold values from 0.099609375 to 1.8984375
- w_query: bfloat16 [576, 576], P('fsdp', 'ctx'), may hold values from -0.25 to 0.25
- key_weight: bfloat16 [576, 192], P('fsdp', 'ctx'), may hold values from -0.25 to 0.25
- value_weight: bfloat16 [576, 192], P('fsdp', 'ctx'), may hold values from -0.25 to 0.25
- w_out: bfloat16 [576, 576], P('fsdp', 'ctx'), may hold values from -6 to 6
- gain_ffn: bfloat16 [576], P('ctx'), may hold values from 0.099609375 to 1.8984375
- w_gate: bfloat16 [576, 1536], P('fsdp', 'ctx'), may hold values from -0.25 to 0.25
- w_up: bfloat16 [576, 1536], P('fsdp', 'ctx'), may hold values from -0.25 to 0.25
- w_down: bfloat16 [1536, 576], P('fsdp', 'ctx'), may hold values from -0.15625 to 0.15625
- cotangent: bfloat16 [4, 1024, 576], P('fsdp', 'ctx'), may hold values from -6 to 6
Outputs:
- output: bfloat16 [4, 1024, 576], P('fsdp', 'ctx')
- grad_input: float32 [4, 1024, 576], P('fsdp', 'ctx')
- grad_gain_attn: float32 [576], P('ctx')
- grad_w_query: float32 [576, 576], P('fsdp', 'ctx')
- grad_w_key: float32 [576, 192], P('fsdp', 'ctx')
- grad_w_value: float32 [576, 192], P('fsdp', 'ctx')
- grad_w_out: float32 [576, 576], P('fsdp', 'ctx')
- grad_gain_ffn: float32 [576], P('ctx')
- grad_w_gate: float32 [576, 1536], P('fsdp', 'ctx')
- grad_w_up: float32 [576, 1536], P('fsdp', 'ctx')
- grad_w_down: float32 [1536, 576], P('fsdp', 'ctx')
The draws below stay inside these ranges and needn't reach their ends.
Inputs may be any that keep to these rules, and one draw needn't show every extreme that they name: Each row of pair_of holds every number from 0 to 7 once.
All inputs are finite; a program needn't handle non-finite values.
Results may differ from the reference program's by a relative error of at most 0.02.
Values may be sent and summed in bfloat16 or wider, within the bound.
No kernel may reach another device: no remote copies, remote signals or barrier semaphores. Data moves between devices by JAX's collectives and lax.ppermute only.
A program may use at most 128 MiB of HBM per device.

```python
import math
from functools import partial
import jax
import jax.numpy as jnp
from jax import lax

MODEL_DIM = 576
QUERY_HEADS = 9
KEY_VALUE_HEADS = 3
HEAD_DIM = 64
FF = 1536
BLK = 64
SEQS = 4
SEQ_LEN = 1024
N_CTX = 8


def steps_of(key, extent, shards, smallest, largest):
    def one(axis_at, shards_of):
        heights = jax.random.uniform(jax.random.fold_in(jax.random.fold_in(key, 6), axis_at), (shards_of,), jnp.float32, smallest / len(shards), largest / len(shards))
        return jnp.repeat(jnp.exp(heights), extent[axis_at] // shards_of).reshape((-1,) + (1,) * (len(extent) - axis_at - 1))

    factor_of = one(*shards[0])
    for cut in shards[1:]:
        factor_of = factor_of * one(*cut)
    return factor_of


def scatter_about(rng, shape, scale, reach, cuts=(), kind=jnp.bfloat16):
    array = scale * jax.random.normal(rng, shape, jnp.float32)
    if cuts:
        array = array * steps_of(rng, shape, cuts, -0.22, 0.18)
    return jnp.clip(array, -reach, reach).astype(kind)


def setup_inputs(seed: int = 0) -> dict:
    streams_of = jax.random.split(jax.random.key(seed), 13)
    return {
        "tokens": scatter_about(streams_of[0], (SEQS, SEQ_LEN, MODEL_DIM), 1.0, 6.0, ((0, 4), (1, 8))),
        "pair_of": jax.vmap(lambda own: jax.random.permutation(own, N_CTX))(jax.random.split(streams_of[1], SEQS)).reshape((SEQS, N_CTX)).astype(jnp.int32),
        "gain_attn": jnp.clip(1.0 + 0.18 * jax.random.normal(streams_of[2], (MODEL_DIM,), jnp.float32), 0.099609375, 1.8984375).astype(jnp.bfloat16),
        "w_query": scatter_about(streams_of[3], (MODEL_DIM, QUERY_HEADS * HEAD_DIM), MODEL_DIM ** -0.5, 0.25, ((0, 4), (1, 8))),
        "key_weight": scatter_about(streams_of[4], (MODEL_DIM, KEY_VALUE_HEADS * HEAD_DIM), MODEL_DIM ** -0.5, 0.25, ((0, 4), (1, 8))),
        "value_weight": scatter_about(streams_of[5], (MODEL_DIM, KEY_VALUE_HEADS * HEAD_DIM), MODEL_DIM ** -0.5, 0.25, ((0, 4), (1, 8))),
        "w_out": scatter_about(streams_of[6], (QUERY_HEADS * HEAD_DIM, MODEL_DIM), ((SEQ_LEN // 8) ** 0.5 * (QUERY_HEADS * HEAD_DIM) ** -0.5), 6.0, ((0, 4), (1, 8))),
        "gain_ffn": jnp.clip(1.0 + 0.18 * jax.random.normal(streams_of[7], (MODEL_DIM,), jnp.float32), 0.099609375, 1.8984375).astype(jnp.bfloat16),
        "w_gate": scatter_about(streams_of[8], (MODEL_DIM, FF), MODEL_DIM ** -0.5, 0.25, ((0, 4), (1, 8))),
        "w_up": scatter_about(streams_of[9], (MODEL_DIM, FF), MODEL_DIM ** -0.5, 0.25, ((0, 4), (1, 8))),
        "w_down": scatter_about(streams_of[10], (FF, MODEL_DIM), FF ** -0.5, 0.15625, ((0, 4), (1, 8))),
        "cotangent": scatter_about(streams_of[11], (SEQS, SEQ_LEN, MODEL_DIM), 1.0, 6.0, ((0, 4), (1, 8))),
    }


theta_base = 100000.0
norm_eps = 1e-05
masked_fill = -1e+30

@jax.custom_vjp
def lower_block(v):
    return lax.optimization_barrier(v.astype(jnp.bfloat16)).astype(jnp.float32)

@jax.custom_vjp
def low_back(v):
    return v

def low_keep(v):
    return (lower_block(v), None)

def low_pass(kept, grad):
    return (grad,)

def back_keep(v):
    return (v, None)

def back_low(kept, grad):
    return (lower_block(grad),)
lower_block.defvjp(low_keep, low_pass)
low_back.defvjp(back_keep, back_low)

def positions_of(pair_of):
    offsets = jnp.arange(BLK, dtype=jnp.int32)
    low_pos = pair_of[:, :, None] * BLK + offsets[None, None, :]
    high_pos = (2 * N_CTX - 1 - pair_of[:, :, None]) * BLK + offsets[None, None, :]
    joined = jnp.concatenate([low_pos, high_pos], axis=2)
    return joined.reshape(pair_of.shape[0], 2 * N_CTX * BLK).astype(jnp.int32)

def rms_norm(values, gain):
    return values * lax.rsqrt(lax.optimization_barrier(jnp.mean(values * values, axis=-1, keepdims=True)) + norm_eps) * gain

def rotary_tables(positions):
    half_dim = HEAD_DIM // 2
    frequency = theta_base ** (-jnp.arange(half_dim, dtype=jnp.float32) * 2.0 / HEAD_DIM)
    angles = positions.astype(jnp.float32)[:, None] * frequency[None, :]
    return (jnp.cos(angles), jnp.sin(angles))

def apply_rotary(values, cosine_table, sine_values):
    half_dim = values.shape[-1] // 2
    first_half = values[..., :half_dim]
    second_half = values[..., half_dim:]
    cos_rows = cosine_table[:, None, :]
    sin_rows = sine_values[:, None, :]
    return jnp.concatenate([first_half * cos_rows - second_half * sin_rows, second_half * cos_rows + first_half * sin_rows], axis=-1)

def forward(tokens, gain_attn, w_query, key_weight, value_weight, w_out, gain_ffn, w_gate, w_up, w_down, positions):
    highest = lax.Precision.HIGHEST
    sequence_count = tokens.shape[0]
    sequence_length = tokens.shape[1]
    query_group_width = QUERY_HEADS // KEY_VALUE_HEADS
    score_scale = 1.0 / math.sqrt(HEAD_DIM)
    normed_attn = lower_block(rms_norm(tokens, gain_attn))
    query_pre = low_back(jnp.dot(normed_attn, w_query, precision=highest))
    key_unrotated = low_back(jnp.dot(normed_attn, key_weight, precision=highest))
    every_value = lower_block(low_back(jnp.dot(normed_attn, value_weight, precision=highest)))
    cosine_table, sine_values = rotary_tables(positions.reshape(-1))
    query_matrix = lower_block(apply_rotary(query_pre.reshape(-1, QUERY_HEADS, HEAD_DIM), cosine_table, sine_values))
    every_key = lower_block(apply_rotary(key_unrotated.reshape(-1, KEY_VALUE_HEADS, HEAD_DIM), cosine_table, sine_values))
    every_key = every_key.reshape(sequence_count, sequence_length, KEY_VALUE_HEADS, HEAD_DIM)
    every_value = every_value.reshape(sequence_count, sequence_length, KEY_VALUE_HEADS, HEAD_DIM)
    rows_of_query = min(512, sequence_length)
    blocks_each_sequence = sequence_length // rows_of_query
    query_entries = query_matrix.reshape(sequence_count * blocks_each_sequence, rows_of_query, KEY_VALUE_HEADS, query_group_width, HEAD_DIM)
    query_pos = positions.reshape(sequence_count * blocks_each_sequence, rows_of_query)
    seq_ids = jnp.repeat(jnp.arange(sequence_count, dtype=jnp.int32), blocks_each_sequence)

    def attend(query_item):
        block_queries, block_pos, seq_id = query_item
        seq_keys = every_key[seq_id]
        seq_values = every_value[seq_id]
        key_pos = positions[seq_id]
        raw_scores = low_back(jnp.einsum('rgjd,kgd->gjrk', block_queries, seq_keys, precision=highest))
        allowed = key_pos[None, None, None, :] <= block_pos[None, None, :, None]
        scores = jnp.where(allowed, raw_scores * score_scale, masked_fill)
        weights = jax.nn.softmax(scores, axis=-1)
        return jnp.einsum('gjrk,kgd->rgjd', lower_block(weights), seq_values, precision=highest)
    attended = lax.map(jax.checkpoint(attend), (query_entries, query_pos, seq_ids))
    attended = lower_block(low_back(attended.reshape(sequence_count, sequence_length, QUERY_HEADS * HEAD_DIM)))
    branch = low_back(jnp.dot(attended, w_out, precision=highest))
    middle = tokens + branch
    normed_ffn = lower_block(rms_norm(middle, gain_ffn))
    gate = low_back(jnp.dot(normed_ffn, w_gate, precision=highest))
    up_part = low_back(jnp.dot(normed_ffn, w_up, precision=highest))
    hidden = lower_block(jax.nn.silu(gate) * up_part)
    return middle + low_back(jnp.dot(hidden, w_down, precision=highest))

def reference(tokens, pair_of, gain_attn, w_query, key_weight, value_weight, w_out, gain_ffn, w_gate, w_up, w_down, cotangent):
    positions = positions_of(pair_of)
    params = (tokens.astype(jnp.float32), gain_attn.astype(jnp.float32), w_query.astype(jnp.float32), key_weight.astype(jnp.float32), value_weight.astype(jnp.float32), w_out.astype(jnp.float32), gain_ffn.astype(jnp.float32), w_gate.astype(jnp.float32), w_up.astype(jnp.float32), w_down.astype(jnp.float32))
    result, pullback = jax.vjp(partial(forward, positions=positions), *params)
    grads = pullback(cotangent.astype(jnp.float32))
    return (result.astype(jnp.bfloat16), grads[0], grads[1], grads[2], grads[3], grads[4], grads[5], grads[6], grads[7], grads[8], grads[9])
```

```python
import functools
import math

import jax
import jax.numpy as jnp
from jax import lax
from jax.experimental import pallas as pl
from jax.experimental.pallas import tpu as pltpu
from jax.sharding import PartitionSpec as P

QUERY_HEADS = 9
KEY_VALUE_HEADS = 3
HEAD_DIM = 64
GROUP = QUERY_HEADS // KEY_VALUE_HEADS

THETA = 100000.0
EPS = 1e-05
MASKED = -1e30
SCALE = 1.0 / math.sqrt(HEAD_DIM)
F32 = jnp.float32
BF16 = jnp.bfloat16
VMEM_BYTES = 56 * 1024 * 1024

K_TILE, K_HALF = (0, 0, 1), (0, 1, 0)
V_TILE, V_HALF = (1, 2, 2), (1, 0, 1)


def round_up(n, m):
    return -(-n // m) * m


def swap(x, axis, mask):
    size = lax.axis_size(axis)
    return lax.ppermute(x, axis, [(i, i ^ mask) for i in range(size)])


def add_low(a, b):
    return (a.astype(F32) + b.astype(F32)).astype(BF16)


def outer_digits(shards):
    bits = list(range(1, shards.bit_length() - 1))
    return [tuple(bits[i : i + 2]) for i in range(0, len(bits), 2)]


def masks_of(digit):
    return [sum(1 << b for k, b in enumerate(digit) if n >> k & 1) for n in range(1 << len(digit))]


def gather_outer(x, shards):
    for digit in outer_digits(shards):
        x = jnp.concatenate([x] + [swap(x, "ctx", m) for m in masks_of(digit)[1:]], 0)
    return x


def scatter_outer(x, shards):
    digits = outer_digits(shards)[::-1]
    for at, digit in enumerate(digits):
        masks = masks_of(digit)
        parts = x.reshape((len(masks), -1) + x.shape[1:])
        total = parts[0].astype(F32)
        for n, m in enumerate(masks[1:]):
            total = total + swap(parts[n + 1], "ctx", m).astype(F32)
        x = total if at == len(digits) - 1 else total.astype(BF16)
    return x


def both(x, axis, mask):
    return jnp.concatenate([x, swap(x, axis, mask)], 0)


def gather_tree(x, rows, shards):
    z = gather_outer(x[None], shards)
    a, b = z[:, :rows], z[:, rows:]
    a, b = both(a, "ctx", 1), both(b, "fsdp", 2)
    a, b = both(a, "fsdp", 2), both(b, "ctx", 1)
    return both(a, "fsdp", 1), both(b, "fsdp", 1)


def scatter_tree(g, rows, shards):
    s = add_low(g[: 2 * shards], swap(g[2 * shards :], "fsdp", 1))
    a, b = s[:, :rows], s[:, rows:]
    a = add_low(a[:shards], swap(a[shards:], "fsdp", 2))
    b = b.reshape((2, 2, shards // 2) + b.shape[1:])
    b = add_low(b[:, 0], swap(b[:, 1], "ctx", 1))
    a = add_low(a[: shards // 2], swap(a[shards // 2 :], "ctx", 1))
    b = add_low(b[0], swap(b[1], "fsdp", 2))
    return scatter_outer(jnp.concatenate([a, b], 1), shards)[0]


def ctx_place(mask, shards):
    return (mask >> 1) + (shards // 2) * (mask & 1)


def place_yx(cm, fm, shards):
    return ctx_place(cm, shards) + shards * (fm >> 1) + 2 * shards * (fm & 1)


def place_xy(cm, fm, shards):
    half = shards // 2
    return (cm >> 1) + half * (fm >> 1) + shards * (cm & 1) + 2 * shards * (fm & 1)


def dot(a, b):
    return lax.dot_general(a, b, (((1,), (0,)), ((), ())), preferred_element_type=F32)


def dot_nt(a, b):
    return lax.dot_general(a, b, (((1,), (1,)), ((), ())), preferred_element_type=F32)


def dot_tn(a, b):
    return lax.dot_general(a, b, (((0,), (0,)), ((), ())), preferred_element_type=F32)


def lane_ids():
    return lax.broadcasted_iota(jnp.int32, (1, 128), 1)


def turned(u):
    lane = lane_ids()
    first = (lane & (HEAD_DIM - 1)) < HEAD_DIM // 2
    return jnp.where(first, pltpu.roll(u, 96, 1), pltpu.roll(u, 32, 1))


def to_half(tile, source, target):
    return tile if source == target else pltpu.roll(tile, 64, 1)


def only_half(tile, half):
    lane = lane_ids()
    keep = lane >= 64 if half else lane < 64
    return jnp.where(keep, tile, 0.0)


def head_rows(h):
    return slice(h * 128, (h + 1) * 128)


def qkv_kernel(dims, meta, x_ref, a1_ref, a2_ref, cos_ref, sin_ref, qp_ref, kv_ref, an_ref, gain_ref, q_s, kv_s):
    shards, fsdp, cq, ck, split, feat = dims
    mc, mf = meta[shards], meta[shards + 1]
    kvw = KEY_VALUE_HEADS * HEAD_DIM
    for c in range(shards):
        tail = a2_ref[place_xy(c ^ mc, mf ^ mf, shards)]
        row = tail[feat - split :, :].astype(F32)
        gain_ref[:, c * cq : (c + 1) * cq] = row[:, :cq]
        gain_ref[:, 640 + c * cq : 640 + (c + 1) * cq] = row[:, 128 : 128 + cq]
    x = x_ref[...].astype(F32)
    width = x.shape[1]
    rr = lax.rsqrt(jnp.mean(x * x, axis=-1, keepdims=True) + EPS)
    normed = (x * rr * gain_ref[0:1, :width]).astype(BF16)
    for c in range(shards):
        pieces = []
        for f in range(fsdp):
            pieces.append(a1_ref[place_yx(c ^ mc, f ^ mf, shards)])
            pieces.append(a2_ref[place_xy(c ^ mc, f ^ mf, shards)][: feat - split])
        w = jnp.concatenate(pieces, 0)
        an_ref[c] = w
        y = dot(normed, w[:, :128])
        q_s[:, c * cq : (c + 1) * cq] = y[:, :cq]
        kv_s[:, c * ck : (c + 1) * ck] = y[:, cq : cq + ck]
        kv_s[:, kvw + c * ck : kvw + (c + 1) * ck] = y[:, cq + ck : cq + 2 * ck]
    cos, sin = cos_ref[...], sin_ref[...]
    for t in range(5):
        u = q_s[:, t * 128 : (t + 1) * 128]
        u = u * cos + turned(u) * sin
        for h in (2 * t, 2 * t + 1):
            if h < QUERY_HEADS:
                half = K_HALF[h // GROUP]
                qp_ref[head_rows(h), :] = only_half(to_half(u, h % 2, half), half).astype(BF16)
    for t in range(3):
        u = kv_s[:, t * 128 : (t + 1) * 128]
        if t < 2:
            r = u * cos + turned(u) * sin
            u = r if t == 0 else jnp.where(lane_ids() < 64, r, u)
        kv_ref[:, t * 128 : (t + 1) * 128] = u.astype(BF16)


def score_mask(meta, shards, block, chunks, blk):
    mc = meta[shards]
    mine = meta[mc]
    r = lax.broadcasted_iota(jnp.int32, (blk, GROUP * 2 * blk), 1) & (2 * blk - 1)
    qpos = jnp.where(r < blk, mine * blk + r, (2 * shards - 1 - mine) * blk + r - blk)
    gap = qpos - lax.broadcasted_iota(jnp.int32, qpos.shape, 0)
    out = []
    half = shards // 2
    for i in range(chunks):
        place = block * chunks + i
        mask = 2 * lax.rem(place, half) + lax.div(place, half)
        pair = meta[mc ^ mask]
        out.append(gap >= pair * blk)
        out.append(gap >= (2 * shards - 1 - pair) * blk)
    return out


def masked(s, mask, blk):
    return jnp.concatenate(
        [jnp.where(m, s[i * blk : (i + 1) * blk], MASKED) for i, m in enumerate(mask)], 0
    )


def attend_kernel(dims, meta, qp_ref, kv_ref, att_ref, ot_ref, lse_ref, m_s, l_s):
    shards, chunks, blk = dims
    blocks = shards // chunks
    rows = chunks * 2 * blk
    span = GROUP * 2 * blk

    def block_step(b, first):
        mask = score_mask(meta, shards, b, chunks, blk)
        kv = kv_ref[pl.ds(b * chunks, chunks)].reshape(rows, -1)
        for g in range(KEY_VALUE_HEADS):
            keys = kv[:, K_TILE[g] * 128 : (K_TILE[g] + 1) * 128]
            vals = kv[:, V_TILE[g] * 128 : (V_TILE[g] + 1) * 128]
            s = masked(dot_nt(keys, qp_ref[g * span : (g + 1) * span, :]) * SCALE, mask, blk)
            top = jnp.max(s, axis=0, keepdims=True)
            if not first:
                top = jnp.maximum(top, m_s[g : g + 1, :])
            p = jnp.exp(s - top)
            total = jnp.sum(p, axis=0, keepdims=True)
            out = dot_tn(vals, p.astype(BF16))
            if not first:
                fade = jnp.exp(m_s[g : g + 1, :] - top)
                total = total + l_s[g : g + 1, :] * fade
                out = out + ot_ref[g] * fade
            m_s[g : g + 1, :] = top
            l_s[g : g + 1, :] = total
            ot_ref[g] = out

    block_step(0, True)
    if blocks > 1:

        @pl.loop(1, blocks)
        def _(b):
            block_step(b, False)

    tiles = {}
    for g in range(KEY_VALUE_HEADS):
        o = ot_ref[g] / l_s[g : g + 1, :]
        ot_ref[g] = o
        lse_ref[g : g + 1, :] = m_s[g : g + 1, :] + jnp.log(l_s[g : g + 1, :])
        for j in range(GROUP):
            h = g * GROUP + j
            tile = jnp.transpose(o[:, j * 128 : (j + 1) * 128])
            tiles[h] = to_half(tile, V_HALF[g], h % 2)
    for t in range(5):
        if 2 * t + 1 < QUERY_HEADS:
            tile = jnp.where(lane_ids() < 64, tiles[2 * t], tiles[2 * t + 1])
            att_ref[:, t * 128 : (t + 1) * 128] = tile.astype(BF16)
        else:
            att_ref[:, t * 128 : t * 128 + 64] = tiles[2 * t][:, :64].astype(BF16)


def ffn_kernel(
    dims, meta, att_ref, x_ref, dy_ref, wo_ref, gain_ref, gu_ref, dt_ref,
    out_ref, gout_ref, dmid_ref, ggain_ref, gp_ref, gu_s, hid_s, dh_s, dgu_s, ga_s,
):
    shards, fsdp, cq, cg, feat, ffr = dims
    mc, mf = meta[shards], meta[shards + 1]
    att = att_ref[...]
    x = x_ref[...].astype(F32)
    width = x.shape[1]
    dyl = dy_ref[...]
    gain = gain_ref[0:1, :width]
    mid = x + dot(att, wo_ref[...])
    rr = lax.rsqrt(jnp.mean(mid * mid, axis=-1, keepdims=True) + EPS)
    z = mid * rr
    normed = (z * gain).astype(BF16)

    def weights(c):
        return jnp.concatenate([gu_ref[c * fsdp + f, :feat, :] for f in range(fsdp)], 0)

    for c in range(shards):
        gu = dot(normed, weights(c))
        gu_s[c] = gu
        gate, up = gu[:, :cg], gu[:, cg : 2 * cg]
        hid_s[:, c * cg : (c + 1) * cg] = gate * jax.nn.sigmoid(gate) * up
    out = mid
    for f in range(fsdp):
        hid = hid_s[:, f * ffr : (f + 1) * ffr].astype(BF16)
        out = out + dot_nt(hid, dt_ref[f])
        dh_s[:, f * ffr : (f + 1) * ffr] = dot(dyl, dt_ref[f])
        g = dot_tn(dyl, hid)
        for c in range(shards):
            piece = g[c * cq : (c + 1) * cq, :].astype(BF16)
            gout_ref[place_yx(c ^ mc, f ^ mf, shards), feat : feat + cq, :] = piece
    out_ref[...] = out.astype(BF16)
    dn = jnp.zeros_like(mid)
    for c in range(shards):
        gu = gu_s[c]
        gate, up = gu[:, :cg], gu[:, cg : 2 * cg]
        dh = dh_s[:, c * cg : (c + 1) * cg]
        sg = jax.nn.sigmoid(gate)
        if 2 * cg < dgu_s.shape[1]:
            dgu_s[...] = jnp.zeros_like(dgu_s)
        dgu_s[:, :cg] = dh * up * sg * (1.0 + gate * (1.0 - sg))
        dgu_s[:, cg : 2 * cg] = dh * gate * sg
        dgu = dgu_s[...].astype(BF16)
        g = dot_tn(normed, dgu)
        for f in range(fsdp):
            piece = g[f * feat : (f + 1) * feat, :].astype(BF16)
            gout_ref[place_yx(c ^ mc, f ^ mf, shards), :feat, : dgu.shape[1]] = piece
        dn = dn + dot_nt(dgu, weights(c))
    e = dn * gain
    dmid = dyl.astype(F32) + rr * (e - z * jnp.mean(e * z, axis=-1, keepdims=True))
    dmid_ref[...] = dmid
    ggain_ref[...] = jnp.broadcast_to(jnp.sum(dn * z, axis=0, keepdims=True), ggain_ref.shape)
    ga_s[:, :width] = dot_nt(dmid.astype(BF16), wo_ref[...])
    for h in range(QUERY_HEADS):
        half = V_HALF[h // GROUP]
        tile = ga_s[:, (h // 2) * 128 : (h // 2 + 1) * 128]
        gp_ref[head_rows(h), :] = only_half(to_half(tile, h % 2, half), half).astype(BF16)


def attend_back_kernel(
    dims, meta, qp_ref, gp_ref, kv_ref, ot_ref, lse_ref, cos_ref, sin_ref, dq_ref, dkv_ref, dq_s
):
    shards, chunks, blk = dims
    blocks = shards // chunks
    rows = chunks * 2 * blk
    span = GROUP * 2 * blk
    deltas = []
    for g in range(KEY_VALUE_HEADS):
        gt = jnp.transpose(gp_ref[g * span : (g + 1) * span, :].astype(F32))
        deltas.append(jnp.sum(gt * ot_ref[g], axis=0, keepdims=True))

    def block_step(b, first):
        mask = score_mask(meta, shards, b, chunks, blk)
        kv = kv_ref[pl.ds(b * chunks, chunks)].reshape(rows, -1)
        tiles = [None, None, None]

        def put(t, value):
            tiles[t] = value if tiles[t] is None else tiles[t] + value

        for g in range(KEY_VALUE_HEADS):
            keys = kv[:, K_TILE[g] * 128 : (K_TILE[g] + 1) * 128]
            vals = kv[:, V_TILE[g] * 128 : (V_TILE[g] + 1) * 128]
            qg = qp_ref[g * span : (g + 1) * span, :]
            gg = gp_ref[g * span : (g + 1) * span, :]
            s = masked(dot_nt(keys, qg) * SCALE, mask, blk)
            p = jnp.exp(s - lse_ref[g : g + 1, :])
            ds = (p * (dot_nt(vals, gg) - deltas[g]) * SCALE).astype(BF16)
            put(V_TILE[g], dot(p.astype(BF16), gg))
            put(K_TILE[g], dot(ds, qg))
            dq = dot_tn(ds, keys)
            if first:
                dq_s[g * span : (g + 1) * span, :] = dq
            else:
                dq_s[g * span : (g + 1) * span, :] += dq
        for t in range(3):
            dkv_ref[pl.ds(b * chunks, chunks), :, t * 128 : (t + 1) * 128] = (
                tiles[t].astype(BF16).reshape(chunks, 2 * blk, 128)
            )

    block_step(0, True)
    if blocks > 1:

        @pl.loop(1, blocks)
        def _(b):
            block_step(b, False)

    cos, sin = cos_ref[...], sin_ref[...]
    tiles = {}
    for h in range(QUERY_HEADS):
        u = dq_s[head_rows(h), :]
        tiles[h] = to_half(u * cos - turned(u) * sin, K_HALF[h // GROUP], h % 2)
    for t in range(5):
        if 2 * t + 1 < QUERY_HEADS:
            tile = jnp.where(lane_ids() < 64, tiles[2 * t], tiles[2 * t + 1])
            dq_ref[:, t * 128 : (t + 1) * 128] = tile.astype(BF16)
        else:
            dq_ref[:, t * 128 : t * 128 + 64] = tiles[2 * t][:, :64].astype(BF16)


def qkv_back_kernel(
    dims, meta, x_ref, dq_ref, dkv_ref, att_ref, dmid_ref, wq_ref, wkv_ref, gain_ref, gg_ref,
    cos_ref, sin_ref, gin_ref, gout_ref, dq_s, dkv_s, gb_s, d_s, gg_s,
):
    shards, fsdp, cq, ck, feat = dims
    mc, mf = meta[shards], meta[shards + 1]
    kvw = KEY_VALUE_HEADS * HEAD_DIM
    x = x_ref[...].astype(F32)
    width = x.shape[1]
    gain = gain_ref[0:1, :width]
    rr = lax.rsqrt(jnp.mean(x * x, axis=-1, keepdims=True) + EPS)
    z = x * rr
    normed = (z * gain).astype(BF16)
    cos, sin = cos_ref[...], sin_ref[...]
    for t in range(3):
        u = dkv_ref[:, t * 128 : (t + 1) * 128]
        if t < 2:
            r = u * cos - turned(u) * sin
            u = r if t == 0 else jnp.where(lane_ids() < 64, r, u)
        dkv_s[:, t * 128 : (t + 1) * 128] = u
    dq_s[...] = dq_ref[...].astype(F32)
    dmid = dmid_ref[...]
    gb_s[...] = dmid
    dn = dot_nt(dq_ref[...], wq_ref[...]) + dot_nt(dkv_s[...].astype(BF16), wkv_ref[...])
    e = dn * gain
    gin_ref[...] = dmid + rr * (e - z * jnp.mean(e * z, axis=-1, keepdims=True))
    gg_s[...] = jnp.broadcast_to(jnp.sum(dn * z, axis=0, keepdims=True), gg_s.shape)
    att = att_ref[...]
    d_s[...] = jnp.zeros_like(d_s)
    for c in range(shards):
        d_s[:, :cq] = dq_s[:, c * cq : (c + 1) * cq]
        d_s[:, cq : cq + ck] = dkv_s[:, c * ck : (c + 1) * ck]
        d_s[:, cq + ck : cq + 2 * ck] = dkv_s[:, kvw + c * ck : kvw + (c + 1) * ck]
        d_s[:, 128 : 128 + cq] = gb_s[:, c * cq : (c + 1) * cq]
        g = jnp.concatenate(
            [dot_tn(normed, d_s[:, :128].astype(BF16)), dot_tn(att, d_s[:, 128:].astype(BF16))], 1
        )
        d_s[0:8, 0:cq] = gg_s[:, c * cq : (c + 1) * cq]
        d_s[0:8, 128 : 128 + cq] = gg_ref[:, c * cq : (c + 1) * cq]
        gains = d_s[0:8, :].astype(BF16)
        for f in range(fsdp):
            at = place_yx(c ^ mc, f ^ mf, shards)
            gout_ref[at, :feat, :] = g[f * feat : (f + 1) * feat, :].astype(BF16)
            gout_ref[at, feat : feat + 8, :] = gains


def call(kernel, outs, scratch, flops, moved, *args):
    smem = pl.BlockSpec(memory_space=pltpu.SMEM)
    vmem = pl.BlockSpec(memory_space=pltpu.VMEM)
    return pl.pallas_call(
        kernel,
        out_shape=outs,
        in_specs=[smem] + [vmem] * (len(args) - 1),
        out_specs=[vmem] * len(outs),
        scratch_shapes=scratch,
        cost_estimate=pl.CostEstimate(flops=flops, bytes_accessed=moved, transcendentals=0),
        compiler_params=pltpu.CompilerParams(vmem_limit_bytes=VMEM_BYTES),
    )(*args)


def arr(shape, dtype):
    return jax.ShapeDtypeStruct(shape, dtype)


def on_device(
    tokens, pair_of, gain_attn, w_query, key_weight, value_weight, w_out, gain_ffn,
    w_gate, w_up, w_down, cotangent,
):
    rows, width = tokens.shape[1:]
    blk = rows // 2
    shards, fsdp = lax.axis_size("ctx"), lax.axis_size("fsdp")
    feat, cq = w_query.shape
    ck, cg, ffr = key_weight.shape[1], w_gate.shape[1], w_down.shape[0]
    ff = cg * shards
    x, dy = tokens[0], cotangent[0]
    meta = jnp.concatenate(
        [pair_of[0], jnp.stack([lax.axis_index("ctx"), lax.axis_index("fsdp")]).astype(jnp.int32)]
    )

    def fill(parts, total):
        used = sum(p.shape[1] for p in parts)
        return parts + [jnp.zeros((parts[0].shape[0], total - used), BF16)]

    lanes = 256
    body = jnp.concatenate(
        fill([w_query, key_weight, value_weight], 128) + fill([w_out], 128), 1
    )
    gains_row = jnp.concatenate(fill([gain_attn[None]], 128) + fill([gain_ffn[None]], 128), 1)
    own = jnp.concatenate([body, jnp.broadcast_to(gains_row, (8, lanes))], 0)
    split = 80

    cgl = round_up(2 * cg, 128)
    gu_own = jnp.concatenate(fill([w_gate, w_up], cgl), 1)
    dt_own = w_down.T
    if cgl == ffr:
        ffn_all = lax.all_gather(jnp.concatenate([gu_own, dt_own], 0), ("ctx", "fsdp"), axis=0)
        gu_all, dt_all = ffn_all, ffn_all[:, feat:]
    else:
        gu_all = lax.all_gather(gu_own, ("ctx", "fsdp"), axis=0)
        dt_all = lax.all_gather(dt_own, ("ctx", "fsdp"), axis=0)
    dt_all = dt_all.reshape(shards, fsdp, cq, ffr).transpose(1, 0, 2, 3).reshape(fsdp, width, ffr)

    a1, a2 = gather_tree(own, split, shards)

    my_pair = pair_of[0, lax.axis_index("ctx")]
    offsets = jnp.arange(blk, dtype=jnp.int32)
    pos = jnp.concatenate([my_pair * blk + offsets, (2 * shards - 1 - my_pair) * blk + offsets])
    freq = THETA ** (-jnp.arange(HEAD_DIM // 2, dtype=F32) * 2.0 / HEAD_DIM)
    angles = pos.astype(F32)[:, None] * freq[None, :]
    cos, sin = jnp.cos(angles), jnp.sin(angles)
    cos_t = jnp.concatenate([cos] * 4, 1)
    sin_t = jnp.concatenate([-sin, sin] * 2, 1)

    kvl = 2 * KEY_VALUE_HEADS * HEAD_DIM
    hrows = QUERY_HEADS * rows
    qp, kv, a_nat, gains = call(
        functools.partial(qkv_kernel, (shards, fsdp, cq, ck, split, feat)),
        [
            arr((hrows, 128), BF16), arr((rows, kvl), BF16),
            arr((shards, width, lanes), BF16), arr((8, 1280), F32),
        ],
        [pltpu.VMEM((rows, 640), F32), pltpu.VMEM((rows, kvl), F32)],
        2 * rows * width * 128 * shards, 6_000_000,
        meta, x, a1, a2, cos_t, sin_t,
    )
    gain_first, gain_second = gains[:, :640], gains[:, 640:]

    def natural(lo, n):
        return a_nat[:, :, lo : lo + n].transpose(1, 0, 2).reshape(width, n * shards)

    wq_n = natural(0, cq)
    wkv_n = jnp.concatenate([natural(cq, ck), natural(cq + ck, ck)], 1)
    wo_n = natural(128, cq)

    kv_all = both(gather_outer(kv[None], shards), "ctx", 1)
    chunks = min(8, shards)
    span = GROUP * rows
    att, ot, lse = call(
        functools.partial(attend_kernel, (shards, chunks, blk)),
        [arr((rows, width), BF16), arr((KEY_VALUE_HEADS, 128, span), F32), arr((8, span), F32)],
        [pltpu.VMEM((8, span), F32), pltpu.VMEM((8, span), F32)],
        4 * hrows * shards * rows * 128, 3_000_000,
        meta, qp, kv_all,
    )

    grows = feat + cq
    glanes = max(cgl, ffr)
    out, g_ffn, dmid, ggain, gp = call(
        functools.partial(ffn_kernel, (shards, fsdp, cq, cg, feat, ffr)),
        [
            arr((rows, width), BF16), arr((fsdp * shards, grows, glanes), BF16),
            arr((rows, width), F32), arr((8, width), F32), arr((hrows, 128), BF16),
        ],
        [
            pltpu.VMEM((shards, rows, cgl), F32), pltpu.VMEM((rows, ff), F32),
            pltpu.VMEM((rows, ff), F32), pltpu.VMEM((rows, cgl), F32), pltpu.VMEM((rows, 640), F32),
        ],
        18 * rows * width * ff, 14_000_000,
        meta, att, x, dy, wo_n, gain_second, gu_all, dt_all,
    )
    ffn_own = scatter_tree(g_ffn, 112, shards)

    dq, dkv = call(
        functools.partial(attend_back_kernel, (shards, chunks, blk)),
        [arr((rows, width), BF16), arr((shards, rows, kvl), BF16)],
        [pltpu.VMEM((hrows, 128), F32)],
        10 * hrows * shards * rows * 128, 5_000_000,
        meta, qp, gp, kv_all, ot, lse, cos_t, sin_t,
    )
    half = shards // 2
    dkv = scatter_outer(add_low(dkv[:half], swap(dkv[half:], "ctx", 1)), shards)[0]

    grad_input, g_attn = call(
        functools.partial(qkv_back_kernel, (shards, fsdp, cq, ck, feat)),
        [arr((rows, width), F32), arr((fsdp * shards, feat + 8, lanes), BF16)],
        [
            pltpu.VMEM((rows, width), F32), pltpu.VMEM((rows, kvl), F32),
            pltpu.VMEM((rows, width), F32), pltpu.VMEM((rows, lanes), F32),
            pltpu.VMEM((8, width), F32),
        ],
        6 * rows * width * 256 * shards, 6_000_000,
        meta, x, dq, dkv, att, dmid, wq_n, wkv_n, gain_first, ggain, cos_t, sin_t,
    )
    attn_own = scatter_tree(g_attn, split, shards)
    return (
        out[None],
        grad_input[None],
        attn_own[feat, :cq],
        attn_own[:feat, :cq],
        attn_own[:feat, cq : cq + ck],
        attn_own[:feat, cq + ck : cq + 2 * ck],
        attn_own[:feat, 128 : 128 + cq],
        attn_own[feat, 128 : 128 + cq],
        ffn_own[:feat, :cg],
        ffn_own[:feat, cg : 2 * cg],
        ffn_own[feat:, :ffr].T,
    )


def solution(mesh):
    weights = (P("fsdp", "ctx"),) * 4
    data = P("fsdp", "ctx", None)
    in_specs = (
        (data, P("fsdp", None), P("ctx")) + weights + (P("ctx"),) + weights[:3] + (data,)
    )
    out_specs = (data, data, P("ctx")) + weights + (P("ctx"),) + weights[:3]
    return jax.shard_map(
        on_device, mesh=mesh, in_specs=in_specs, out_specs=out_specs, check_vma=False
    )
```

```python
import functools
import math

import jax
import jax.numpy as jnp
from jax import lax
from jax.experimental import pallas as pl
from jax.experimental.pallas import tpu as pltpu
from jax.sharding import PartitionSpec as P

QUERY_HEADS = 9
KEY_VALUE_HEADS = 3
HEAD_DIM = 64
GROUP = QUERY_HEADS // KEY_VALUE_HEADS

THETA = 100000.0
EPS = 1e-05
MASKED = -1e30
SCALE = 1.0 / math.sqrt(HEAD_DIM)
F32 = jnp.float32
BF16 = jnp.bfloat16
VMEM_BYTES = 56 * 1024 * 1024

K_TILE, K_HALF = (0, 0, 1), (0, 1, 0)
V_TILE, V_HALF = (1, 2, 2), (1, 0, 1)


def round_up(n, m):
    return -(-n // m) * m


def swap(x, axis, mask):
    size = lax.axis_size(axis)
    return lax.ppermute(x, axis, [(i, i ^ mask) for i in range(size)])


def add_low(a, b):
    return (a.astype(F32) + b.astype(F32)).astype(BF16)


def outer_digits(shards):
    bits = list(range(1, shards.bit_length() - 1))
    return [tuple(bits[i : i + 2]) for i in range(0, len(bits), 2)]


def masks_of(digit):
    return [sum(1 << b for k, b in enumerate(digit) if n >> k & 1) for n in range(1 << len(digit))]


def join(pieces, *before):
    held = lax.optimization_barrier((*pieces, *before))[: len(pieces)]
    return jnp.concatenate(held, 0)


def gather_outer(x, shards):
    pieces = [x]
    for digit in outer_digits(shards):
        x = jnp.concatenate(pieces, 0)
        pieces = [x] + [swap(x, "ctx", m) for m in masks_of(digit)[1:]]
    return pieces


def scatter_outer(x, shards):
    for digit in outer_digits(shards)[::-1]:
        masks = masks_of(digit)
        parts = x.reshape((len(masks), -1) + x.shape[1:])
        terms = [parts[0]] + [swap(parts[n + 1], "ctx", m) for n, m in enumerate(masks[1:])]
        x = add_terms(terms).astype(BF16)
    return terms


def add_terms(terms, *before):
    held = lax.optimization_barrier((*terms, *before))[: len(terms)]
    return functools.reduce(lambda a, b: a + b, [t.astype(F32) for t in held])


def after(x, *before):
    return lax.optimization_barrier((x, *before))[0]


class Gather:
    def __init__(self, block, rows, shards):
        self.block, self.rows, self.shards = block, rows, shards

    def outer(self, *before):
        pieces = gather_outer(after(self.block[None], *before), self.shards)
        self.a = [p[:, : self.rows] for p in pieces]
        self.b = [p[:, self.rows :] for p in pieces]

    def phase(self, axis_a, mask_a, axis_b, mask_b, *before):
        a, b = join(self.a, *before), join(self.b, *before)
        self.now = a, b
        self.a, self.b = [a, swap(a, axis_a, mask_a)], [b, swap(b, axis_b, mask_b)]

    def second(self, *before):
        self.phase("ctx", 1, "fsdp", 2, *before)

    def third(self, *before):
        self.phase("fsdp", 2, "ctx", 1, *before)

    def cores(self, *before):
        self.phase("fsdp", 1, "fsdp", 1, *before)
        return *self.a, *self.b


class Scatter:
    def __init__(self, keep_a, send_a, keep_b, send_b, shards, *before):
        self.a, self.b, self.shards = keep_a, keep_b, shards
        send_a, send_b = after(send_a, *before), after(send_b, *before)
        self.got_a, self.got_b = swap(send_a, "fsdp", 1), swap(send_b, "fsdp", 1)

    def fold(self, size, *before):
        a, b, got_a, got_b = lax.optimization_barrier(
            (self.a, self.b, self.got_a, self.got_b, *before)
        )[:4]
        self.a, self.b = add_low(a[:size], got_a[:size]), add_low(b[:size], got_b[:size])
        self.out = add_low(a[size:], got_a[size:]), add_low(b[size:], got_b[size:])
        return self.out

    def second(self, *before):
        a, b = self.fold(self.shards, *before)
        self.got_a, self.got_b = swap(a, "fsdp", 2), swap(b, "ctx", 1)

    def third(self, *before):
        a, b = self.fold(self.shards // 2, *before)
        self.got_a, self.got_b = swap(a, "ctx", 1), swap(b, "fsdp", 2)

    def outer(self, *before):
        a, b, got_a, got_b = lax.optimization_barrier(
            (self.a, self.b, self.got_a, self.got_b, *before)
        )[:4]
        self.terms = scatter_outer(
            jnp.concatenate([add_low(a, got_a), add_low(b, got_b)], 1), self.shards
        )

    def total(self, *before):
        return add_terms(self.terms, *before)[0]


def ctx_place(mask, shards):
    return (mask >> 1) + (shards // 2) * (mask & 1)


def place_a(cm, x_bit, shards):
    return ctx_place(cm, shards) + shards * x_bit


def place_b(cm, x_bit, shards):
    return (cm >> 1) + (shards // 2) * x_bit + shards * (cm & 1)


def arrange(out_ref, value, mine, feat):
    for k in range(value.shape[1] // feat):

        @pl.when(mine == k)
        def _():
            for m in range(value.shape[1] // feat):
                out_ref[:, m * feat : (m + 1) * feat] = value[:, (m ^ k) * feat : ((m ^ k) + 1) * feat]


def dot(a, b):
    return lax.dot_general(a, b, (((1,), (0,)), ((), ())), preferred_element_type=F32)


def dot_nt(a, b):
    return lax.dot_general(a, b, (((1,), (1,)), ((), ())), preferred_element_type=F32)


def dot_tn(a, b):
    return lax.dot_general(a, b, (((0,), (0,)), ((), ())), preferred_element_type=F32)


def lane_ids():
    return lax.broadcasted_iota(jnp.int32, (1, 128), 1)


def turned(u):
    lane = lane_ids()
    first = (lane & (HEAD_DIM - 1)) < HEAD_DIM // 2
    return jnp.where(first, pltpu.roll(u, 96, 1), pltpu.roll(u, 32, 1))


def to_half(tile, source, target):
    return tile if source == target else pltpu.roll(tile, 64, 1)


def only_half(tile, half):
    lane = lane_ids()
    keep = lane >= 64 if half else lane < 64
    return jnp.where(keep, tile, 0.0)


def head_rows(h):
    return slice(h * 128, (h + 1) * 128)


def qkv_kernel(
    dims, meta, x_ref, ao_ref, as_ref, bo_ref, bs_ref, cos_ref, sin_ref,
    qp_ref, kv_ref, an_ref, gain_ref, q_s, kv_s, n_s,
):
    shards, fsdp, cq, ck, split, feat = dims
    mc, mf = meta[shards], meta[shards + 1]
    kvw = KEY_VALUE_HEADS * HEAD_DIM
    for c in range(shards):
        row = bo_ref[place_b(c ^ mc, 0, shards)][feat - split :, :].astype(F32)
        gain_ref[:, c * cq : (c + 1) * cq] = row[:, :cq]
        gain_ref[:, 640 + c * cq : 640 + (c + 1) * cq] = row[:, 128 : 128 + cq]
    x = x_ref[...].astype(F32)
    width = x.shape[1]
    rr = lax.rsqrt(jnp.mean(x * x, axis=-1, keepdims=True) + EPS)
    arrange(n_s, x * rr * gain_ref[0:1, :width], mf, feat)
    normed = n_s[...].astype(BF16)
    for c in range(shards):
        for m in range(fsdp):
            a_ref, b_ref = ((ao_ref, bo_ref), (as_ref, bs_ref))[m & 1]
            cut = m * feat + split
            an_ref[c, m * feat : cut, :] = a_ref[place_a(c ^ mc, m >> 1, shards)]
            an_ref[c, cut : (m + 1) * feat, :] = b_ref[place_b(c ^ mc, m >> 1, shards)][: feat - split]
        y = dot(normed, an_ref[c, :, :128])
        q_s[:, c * cq : (c + 1) * cq] = y[:, :cq]
        kv_s[:, c * ck : (c + 1) * ck] = y[:, cq : cq + ck]
        kv_s[:, kvw + c * ck : kvw + (c + 1) * ck] = y[:, cq + ck : cq + 2 * ck]
    cos, sin = cos_ref[...], sin_ref[...]
    for t in range(5):
        u = q_s[:, t * 128 : (t + 1) * 128]
        u = u * cos + turned(u) * sin
        for h in (2 * t, 2 * t + 1):
            if h < QUERY_HEADS:
                half = K_HALF[h // GROUP]
                qp_ref[head_rows(h), :] = only_half(to_half(u, h % 2, half), half).astype(BF16)
    for t in range(3):
        u = kv_s[:, t * 128 : (t + 1) * 128]
        if t < 2:
            r = u * cos + turned(u) * sin
            u = r if t == 0 else jnp.where(lane_ids() < 64, r, u)
        kv_ref[:, t * 128 : (t + 1) * 128] = u.astype(BF16)


def score_mask(meta, shards, block, chunks, blk):
    mc = meta[shards]
    mine = meta[mc]
    r = lax.broadcasted_iota(jnp.int32, (blk, GROUP * 2 * blk), 1) & (2 * blk - 1)
    qpos = jnp.where(r < blk, mine * blk + r, (2 * shards - 1 - mine) * blk + r - blk)
    gap = qpos - lax.broadcasted_iota(jnp.int32, qpos.shape, 0)
    out = []
    for i in range(chunks):
        pair = meta[mc ^ (2 * (block * (chunks // 2) + i % (chunks // 2)) + i // (chunks // 2))]
        out.append(gap >= pair * blk)
        out.append(gap >= (2 * shards - 1 - pair) * blk)
    return out


def block_rows(near_ref, far_ref, block, chunks):
    here = pl.ds(block * (chunks // 2), chunks // 2)
    return jnp.concatenate(
        [r[here].reshape(-1, r.shape[2]) for r in (near_ref, far_ref)], 0
    )


def masked(s, mask, blk):
    return jnp.concatenate(
        [jnp.where(m, s[i * blk : (i + 1) * blk], MASKED) for i, m in enumerate(mask)], 0
    )


def attend_kernel(dims, meta, qp_ref, near_ref, far_ref, att_ref, ot_ref, lse_ref, m_s, l_s):
    shards, chunks, blk = dims
    blocks = shards // chunks
    rows = chunks * 2 * blk
    span = GROUP * 2 * blk

    def block_step(b, first):
        mask = score_mask(meta, shards, b, chunks, blk)
        kv = block_rows(near_ref, far_ref, b, chunks)
        for g in range(KEY_VALUE_HEADS):
            keys = kv[:, K_TILE[g] * 128 : (K_TILE[g] + 1) * 128]
            vals = kv[:, V_TILE[g] * 128 : (V_TILE[g] + 1) * 128]
            s = masked(dot_nt(keys, qp_ref[g * span : (g + 1) * span, :]) * SCALE, mask, blk)
            top = jnp.max(s, axis=0, keepdims=True)
            if not first:
                top = jnp.maximum(top, m_s[g : g + 1, :])
            p = jnp.exp(s - top)
            total = jnp.sum(p, axis=0, keepdims=True)
            out = dot_tn(vals, p.astype(BF16))
            if not first:
                fade = jnp.exp(m_s[g : g + 1, :] - top)
                total = total + l_s[g : g + 1, :] * fade
                out = out + ot_ref[g] * fade
            m_s[g : g + 1, :] = top
            l_s[g : g + 1, :] = total
            ot_ref[g] = out

    block_step(0, True)
    if blocks > 1:

        @pl.loop(1, blocks)
        def _(b):
            block_step(b, False)

    tiles = {}
    for g in range(KEY_VALUE_HEADS):
        o = ot_ref[g] / l_s[g : g + 1, :]
        ot_ref[g] = o
        lse_ref[g : g + 1, :] = m_s[g : g + 1, :] + jnp.log(l_s[g : g + 1, :])
        for j in range(GROUP):
            h = g * GROUP + j
            tile = jnp.transpose(o[:, j * 128 : (j + 1) * 128])
            tiles[h] = to_half(tile, V_HALF[g], h % 2)
    for t in range(5):
        if 2 * t + 1 < QUERY_HEADS:
            tile = jnp.where(lane_ids() < 64, tiles[2 * t], tiles[2 * t + 1])
            att_ref[:, t * 128 : (t + 1) * 128] = tile.astype(BF16)
        else:
            att_ref[:, t * 128 : t * 128 + 64] = tiles[2 * t][:, :64].astype(BF16)


def ffn_kernel(
    dims, meta, att_ref, x_ref, dy_ref, an_ref, gain_ref, *refs
):
    shards, fsdp, cq, cg, feat, ffr, split, packed = dims
    ins = refs[:4] if packed else refs[:2]
    (
        out_ref, ak_ref, as_ref, bk_ref, bs_ref, dmid_ref, ggain_ref, gp_ref,
        gu_s, hid_s, dh_s, dgu_s, wide_s, p_s, w_s, dt_s,
    ) = refs[len(ins) :]
    mc, mf = meta[shards], meta[shards + 1]
    lanes = ak_ref.shape[2]
    if packed:
        for c in range(0, shards, 2):
            for m in range(fsdp):
                tails = []
                for d in (c, c + 1):
                    a_ref, b_ref = ins[m & 1], ins[2 + (m & 1)]
                    w_s[d, m * feat : m * feat + split, :] = a_ref[place_a(d ^ mc, m >> 1, shards)]
                    tail = b_ref[place_b(d ^ mc, m >> 1, shards)]
                    w_s[d, m * feat + split : (m + 1) * feat, :] = tail[: feat - split]
                    tails.append(tail[feat - split :].astype(F32))
                dt_s[m, c * cq : (c + 2) * cq, :] = jnp.concatenate(tails, 0).astype(BF16)
    else:
        for m in range(fsdp):
            dt_s[m] = ins[1][mf ^ m]

    def weights(c):
        if packed:
            return w_s[c]
        return jnp.concatenate([ins[0][c, mf ^ m] for m in range(fsdp)], 0)

    x = x_ref[...].astype(F32)
    width = x.shape[1]
    dyl = dy_ref[...]
    gain = gain_ref[0:1, :width]
    arrange(p_s, att_ref[...].astype(F32), mf, feat)
    attp = p_s[...].astype(BF16)
    for c in range(shards):
        wide_s[:, c * cq : (c + 1) * cq] = dot(attp, an_ref[c, :, -128:])[:, :cq]
    mid = x + wide_s[:, :width]
    rr = lax.rsqrt(jnp.mean(mid * mid, axis=-1, keepdims=True) + EPS)
    z = mid * rr
    arrange(p_s, z * gain, mf, feat)
    normed = p_s[...].astype(BF16)

    def store_grad(c, m, row, value):
        end = row + value.shape[0]
        here = slice(0, value.shape[1])
        if row < split:
            stop = min(end, split)
            ref = (ak_ref, as_ref)[m & 1]
            ref[place_a(c ^ mc, m >> 1, shards), row:stop, here] = value[: stop - row]
        if end > split:
            start = max(row, split)
            ref = (bk_ref, bs_ref)[m & 1]
            ref[place_b(c ^ mc, m >> 1, shards), start - split : end - split, here] = value[start - row :]

    for c in range(shards):
        gu = dot(normed, weights(c))
        gu_s[c] = gu
        gate, up = gu[:, :cg], gu[:, cg : 2 * cg]
        hid_s[:, c * cg : (c + 1) * cg] = gate * jax.nn.sigmoid(gate) * up
    out = mid
    for m in range(fsdp):
        here = pl.ds(pl.multiple_of((mf ^ m) * ffr, 128), ffr)
        hid = hid_s[:, here].astype(BF16)
        out = out + dot_nt(hid, dt_s[m])
        dh_s[:, here] = dot(dyl, dt_s[m])
        g = dot_tn(dyl, hid)
        for c in range(shards):
            piece = g[c * cq : (c + 1) * cq, :].astype(BF16)
            for t in range(ffr // lanes):
                store_grad(c, m, feat + t * cq, piece[:, t * lanes : (t + 1) * lanes])
    out_ref[...] = out.astype(BF16)
    dn = jnp.zeros_like(mid)
    for c in range(shards):
        gu = gu_s[c]
        gate, up = gu[:, :cg], gu[:, cg : 2 * cg]
        dh = dh_s[:, c * cg : (c + 1) * cg]
        sg = jax.nn.sigmoid(gate)
        if 2 * cg < dgu_s.shape[1]:
            dgu_s[...] = jnp.zeros_like(dgu_s)
        dgu_s[:, :cg] = dh * up * sg * (1.0 + gate * (1.0 - sg))
        dgu_s[:, cg : 2 * cg] = dh * gate * sg
        dgu = dgu_s[...].astype(BF16)
        g = dot_tn(normed, dgu)
        for m in range(fsdp):
            store_grad(c, m, 0, g[m * feat : (m + 1) * feat, :].astype(BF16))
        dn = dn + dot_nt(dgu, weights(c))
    arrange(p_s, dn, mf, feat)
    dn = p_s[...]
    e = dn * gain
    dmid = dyl.astype(F32) + rr * (e - z * jnp.mean(e * z, axis=-1, keepdims=True))
    dmid_ref[...] = dmid
    ggain_ref[...] = jnp.broadcast_to(jnp.sum(dn * z, axis=0, keepdims=True), ggain_ref.shape)
    wide_s[...] = jnp.zeros_like(wide_s)
    wide_s[:, :width] = dmid
    ga = jnp.zeros_like(mid)
    for c in range(shards):
        gb = wide_s[:, c * cq : c * cq + 128].astype(BF16)
        ga = ga + dot_nt(gb, an_ref[c, :, -128:])
    arrange(p_s, ga, mf, feat)
    wide_s[:, :width] = p_s[...]
    for h in range(QUERY_HEADS):
        half = V_HALF[h // GROUP]
        tile = wide_s[:, (h // 2) * 128 : (h // 2 + 1) * 128]
        gp_ref[head_rows(h), :] = only_half(to_half(tile, h % 2, half), half).astype(BF16)


def attend_back_kernel(
    dims, meta, qp_ref, gp_ref, near_ref, far_ref, ot_ref, lse_ref, cos_ref, sin_ref,
    dq_ref, dnear_ref, dfar_ref, dq_s,
):
    shards, chunks, blk = dims
    blocks = shards // chunks
    rows = chunks * 2 * blk
    span = GROUP * 2 * blk
    deltas = []
    for g in range(KEY_VALUE_HEADS):
        gt = jnp.transpose(gp_ref[g * span : (g + 1) * span, :].astype(F32))
        deltas.append(jnp.sum(gt * ot_ref[g], axis=0, keepdims=True))

    def block_step(b, first):
        mask = score_mask(meta, shards, b, chunks, blk)
        kv = block_rows(near_ref, far_ref, b, chunks)
        tiles = [None, None, None]

        def put(t, value):
            tiles[t] = value if tiles[t] is None else tiles[t] + value

        for g in range(KEY_VALUE_HEADS):
            keys = kv[:, K_TILE[g] * 128 : (K_TILE[g] + 1) * 128]
            vals = kv[:, V_TILE[g] * 128 : (V_TILE[g] + 1) * 128]
            qg = qp_ref[g * span : (g + 1) * span, :]
            gg = gp_ref[g * span : (g + 1) * span, :]
            s = masked(dot_nt(keys, qg) * SCALE, mask, blk)
            p = jnp.exp(s - lse_ref[g : g + 1, :])
            ds = (p * (dot_nt(vals, gg) - deltas[g]) * SCALE).astype(BF16)
            put(V_TILE[g], dot(p.astype(BF16), gg))
            put(K_TILE[g], dot(ds, qg))
            dq = dot_tn(ds, keys)
            if first:
                dq_s[g * span : (g + 1) * span, :] = dq
            else:
                dq_s[g * span : (g + 1) * span, :] += dq
        for t in range(3):
            tile = tiles[t].astype(BF16).reshape(2, chunks // 2, 2 * blk, 128)
            for n, ref in enumerate((dnear_ref, dfar_ref)):
                ref[pl.ds(b * (chunks // 2), chunks // 2), :, t * 128 : (t + 1) * 128] = tile[n]

    block_step(0, True)
    if blocks > 1:

        @pl.loop(1, blocks)
        def _(b):
            block_step(b, False)

    cos, sin = cos_ref[...], sin_ref[...]
    tiles = {}
    for h in range(QUERY_HEADS):
        u = dq_s[head_rows(h), :]
        tiles[h] = to_half(u * cos - turned(u) * sin, K_HALF[h // GROUP], h % 2)
    for t in range(5):
        if 2 * t + 1 < QUERY_HEADS:
            tile = jnp.where(lane_ids() < 64, tiles[2 * t], tiles[2 * t + 1])
            dq_ref[:, t * 128 : (t + 1) * 128] = tile.astype(BF16)
        else:
            dq_ref[:, t * 128 : t * 128 + 64] = tiles[2 * t][:, :64].astype(BF16)


def qkv_back_kernel(
    dims, meta, x_ref, dq_ref, dkv_ref, att_ref, dmid_ref, an_ref, gain_ref, gg_ref,
    cos_ref, sin_ref, gin_ref, ak_ref, as_ref, bk_ref, bs_ref, dq_s, dkv_s, d_s, p_s, gg_s,
):
    shards, fsdp, cq, ck, split, feat = dims
    mc, mf = meta[shards], meta[shards + 1]
    kvw = KEY_VALUE_HEADS * HEAD_DIM
    x = x_ref[...].astype(F32)
    width = x.shape[1]
    gain = gain_ref[0:1, :width]
    rr = lax.rsqrt(jnp.mean(x * x, axis=-1, keepdims=True) + EPS)
    z = x * rr
    arrange(p_s, z * gain, mf, feat)
    normed = p_s[...].astype(BF16)
    arrange(p_s, att_ref[...].astype(F32), mf, feat)
    att = p_s[...].astype(BF16)
    cos, sin = cos_ref[...], sin_ref[...]
    for t in range(3):
        u = dkv_ref[:, t * 128 : (t + 1) * 128]
        if t < 2:
            r = u * cos - turned(u) * sin
            u = r if t == 0 else jnp.where(lane_ids() < 64, r, u)
        dkv_s[:, t * 128 : (t + 1) * 128] = u
    dq_s[...] = dq_ref[...].astype(F32)
    d_s[...] = jnp.zeros_like(d_s)
    dn = jnp.zeros_like(x)
    for c in range(shards):
        d_s[:, :cq] = dq_s[:, c * cq : (c + 1) * cq]
        d_s[:, cq : cq + ck] = dkv_s[:, c * ck : (c + 1) * ck]
        d_s[:, cq + ck : cq + 2 * ck] = dkv_s[:, kvw + c * ck : kvw + (c + 1) * ck]
        d_s[:, 128 : 128 + cq] = dmid_ref[:, c * cq : (c + 1) * cq]
        d = d_s[...].astype(BF16)
        dn = dn + dot_nt(d[:, :128], an_ref[c, :, :128])
        g = jnp.concatenate([dot_tn(normed, d[:, :128]), dot_tn(att, d[:, 128:])], 1).astype(BF16)
        for m in range(fsdp):
            part = g[m * feat : (m + 1) * feat, :]
            (ak_ref, as_ref)[m & 1][place_a(c ^ mc, m >> 1, shards)] = part[:split]
            (bk_ref, bs_ref)[m & 1][place_b(c ^ mc, m >> 1, shards), : feat - split] = part[split:]
    arrange(p_s, dn, mf, feat)
    dn = p_s[...]
    e = dn * gain
    gin_ref[...] = dmid_ref[...] + rr * (e - z * jnp.mean(e * z, axis=-1, keepdims=True))
    gg_s[...] = jnp.broadcast_to(jnp.sum(dn * z, axis=0, keepdims=True), gg_s.shape)
    for c in range(shards):
        d_s[0:8, 0:cq] = gg_s[:, c * cq : (c + 1) * cq]
        d_s[0:8, 128 : 128 + cq] = gg_ref[:, c * cq : (c + 1) * cq]
        gains = d_s[0:8, :].astype(BF16)
        for m in range(fsdp):
            (bk_ref, bs_ref)[m & 1][place_b(c ^ mc, m >> 1, shards), feat - split :] = gains


def call(kernel, outs, scratch, flops, moved, *args):
    smem = pl.BlockSpec(memory_space=pltpu.SMEM)
    vmem = pl.BlockSpec(memory_space=pltpu.VMEM)
    return pl.pallas_call(
        kernel,
        out_shape=outs,
        in_specs=[smem] + [vmem] * (len(args) - 1),
        out_specs=[vmem] * len(outs),
        scratch_shapes=scratch,
        cost_estimate=pl.CostEstimate(flops=flops, bytes_accessed=moved, transcendentals=0),
        compiler_params=pltpu.CompilerParams(vmem_limit_bytes=VMEM_BYTES),
    )(*args)


def arr(shape, dtype):
    return jax.ShapeDtypeStruct(shape, dtype)


def on_device(
    tokens, pair_of, gain_attn, w_query, key_weight, value_weight, w_out, gain_ffn,
    w_gate, w_up, w_down, cotangent,
):
    rows, width = tokens.shape[1:]
    blk = rows // 2
    shards, fsdp = lax.axis_size("ctx"), lax.axis_size("fsdp")
    feat, cq = w_query.shape
    ck, cg, ffr = key_weight.shape[1], w_gate.shape[1], w_down.shape[0]
    ff = cg * shards
    x, dy = tokens[0], cotangent[0]
    meta = jnp.concatenate(
        [pair_of[0], jnp.stack([lax.axis_index("ctx"), lax.axis_index("fsdp")]).astype(jnp.int32)]
    )

    def fill(parts, total):
        used = sum(p.shape[1] for p in parts)
        return parts + [jnp.zeros((parts[0].shape[0], total - used), BF16)]

    lanes = 256
    body = jnp.concatenate(
        fill([w_query, key_weight, value_weight], 128) + fill([w_out], 128), 1
    )
    gains_row = jnp.concatenate(fill([gain_attn[None]], 128) + fill([gain_ffn[None]], 128), 1)
    own = jnp.concatenate([body, jnp.broadcast_to(gains_row, (8, lanes))], 0)
    split = 80

    cgl = round_up(2 * cg, 128)
    gu_own = jnp.concatenate(fill([w_gate, w_up], cgl), 1)
    dt_own = w_down.T
    packed = cgl == ffr and cq % 8 == 0
    ffn_split = 112
    if packed:
        ffn = Gather(jnp.concatenate([gu_own, dt_own], 0), ffn_split, shards)
    else:
        gu_all = lax.all_gather(gu_own, ("ctx", "fsdp"), axis=0).reshape(shards, fsdp, feat, cgl)
        dt_all = lax.all_gather(dt_own, ("ctx", "fsdp"), axis=0).reshape(shards, fsdp, cq, ffr)
        ffn_in = (gu_all, dt_all.transpose(1, 0, 2, 3).reshape(fsdp, width, ffr))

    attn = Gather(own, split, shards)
    attn.outer()
    if packed:
        ffn.outer(*attn.a, *attn.b)
    attn.second()
    attn.third()
    if packed:
        attn_in = attn.cores(*ffn.a, *ffn.b)
        ffn.second()
    else:
        attn_in = attn.cores()

    my_pair = pair_of[0, lax.axis_index("ctx")]
    offsets = jnp.arange(blk, dtype=jnp.int32)
    pos = jnp.concatenate([my_pair * blk + offsets, (2 * shards - 1 - my_pair) * blk + offsets])
    freq = THETA ** (-jnp.arange(HEAD_DIM // 2, dtype=F32) * 2.0 / HEAD_DIM)
    angles = pos.astype(F32)[:, None] * freq[None, :]
    cos, sin = jnp.cos(angles), jnp.sin(angles)
    cos_t = jnp.concatenate([cos] * 4, 1)
    sin_t = jnp.concatenate([-sin, sin] * 2, 1)

    kvl = 2 * KEY_VALUE_HEADS * HEAD_DIM
    hrows = QUERY_HEADS * rows
    qp, kv, a_nat, gains = call(
        functools.partial(qkv_kernel, (shards, fsdp, cq, ck, split, feat)),
        [
            arr((hrows, 128), BF16), arr((rows, kvl), BF16),
            arr((shards, width, lanes), BF16), arr((8, 1280), F32),
        ],
        [pltpu.VMEM((rows, 640), F32), pltpu.VMEM((rows, kvl), F32), pltpu.VMEM((rows, width), F32)],
        2 * rows * width * 128 * shards, 6_000_000,
        meta, x, *attn_in, cos_t, sin_t,
    )
    gain_first, gain_second = gains[:, :640], gains[:, 640:]

    kv_near = join(gather_outer(kv[None], shards))
    kv_far = swap(kv_near, "ctx", 1)
    if packed:
        ffn.third(kv)
    chunks = min(8, shards)
    span = GROUP * rows
    att, ot, lse = call(
        functools.partial(attend_kernel, (shards, chunks, blk)),
        [arr((rows, width), BF16), arr((KEY_VALUE_HEADS, 128, span), F32), arr((8, span), F32)],
        [pltpu.VMEM((8, span), F32), pltpu.VMEM((8, span), F32)],
        4 * hrows * shards * rows * 128, 3_000_000,
        meta, qp, kv_near, kv_far,
    )

    if packed:
        ffn_in = ffn.cores(kv_near)
    glanes = cgl
    tiles = ffr // glanes
    parts = [arr((2 * shards, ffn_split, glanes), BF16)] * 2
    parts += [arr((2 * shards, feat + tiles * cq - ffn_split, glanes), BF16)] * 2
    out, *g_ffn, dmid, ggain, gp = call(
        functools.partial(
            ffn_kernel, (shards, fsdp, cq, cg, feat, ffr, ffn_split, packed)
        ),
        [arr((rows, width), BF16), *parts]
        + [arr((rows, width), F32), arr((8, width), F32), arr((hrows, 128), BF16)],
        [
            pltpu.VMEM((shards, rows, cgl), F32), pltpu.VMEM((rows, ff), F32),
            pltpu.VMEM((rows, ff), F32), pltpu.VMEM((rows, cgl), F32), pltpu.VMEM((rows, 768), F32),
            pltpu.VMEM((rows, width), F32), pltpu.VMEM((shards, width, cgl) if packed else (1, 16, 128), BF16),
            pltpu.VMEM((fsdp, width, ffr), BF16),
        ],
        18 * rows * width * ff, 14_000_000,
        meta, att, x, dy, a_nat if packed else a_nat[:, :, 128:], gain_second, *ffn_in,
    )
    ffn_sum = Scatter(*g_ffn, shards)
    ffn_sum.second()

    dq, dkv_near, dkv_far = call(
        functools.partial(attend_back_kernel, (shards, chunks, blk)),
        [arr((rows, width), BF16)] + [arr((shards // 2, rows, kvl), BF16)] * 2,
        [pltpu.VMEM((hrows, 128), F32)],
        10 * hrows * shards * rows * 128, 5_000_000,
        meta, qp, gp, kv_near, kv_far, ot, lse, cos_t, sin_t,
    )
    dkv_far = after(dkv_far, *ffn_sum.out)
    dkv_terms = scatter_outer(add_low(dkv_near, swap(dkv_far, "ctx", 1)), shards)
    ffn_sum.third()
    dkv = add_terms(dkv_terms, *ffn_sum.out)[0]

    grad_input, *g_attn = call(
        functools.partial(qkv_back_kernel, (shards, fsdp, cq, ck, split, feat)),
        [arr((rows, width), F32)]
        + [arr((2 * shards, split, lanes), BF16)] * 2
        + [arr((2 * shards, feat + 8 - split, lanes), BF16)] * 2,
        [
            pltpu.VMEM((rows, width), F32), pltpu.VMEM((rows, kvl), F32),
            pltpu.VMEM((rows, lanes), F32), pltpu.VMEM((rows, width), F32),
            pltpu.VMEM((8, width), F32),
        ],
        6 * rows * width * 256 * shards, 6_000_000,
        meta, x, dq, dkv, att, dmid, a_nat, gain_first, ggain, cos_t, sin_t,
    )
    attn_sum = Scatter(*g_attn, shards, ffn_sum.got_a, ffn_sum.got_b)
    ffn_sum.outer()
    attn_sum.second()
    attn_sum.third()
    ffn_own = ffn_sum.total(*attn_sum.out)
    attn_sum.outer()
    attn_own = attn_sum.total()
    return (
        out[None],
        grad_input[None],
        attn_own[feat, :cq],
        attn_own[:feat, :cq],
        attn_own[:feat, cq : cq + ck],
        attn_own[:feat, cq + ck : cq + 2 * ck],
        attn_own[:feat, 128 : 128 + cq],
        attn_own[feat, 128 : 128 + cq],
        ffn_own[:feat, :cg],
        ffn_own[:feat, cg : 2 * cg],
        jnp.concatenate([ffn_own[feat + t * cq : feat + (t + 1) * cq] for t in range(tiles)], 1).T,
    )


def solution(mesh):
    weights = (P("fsdp", "ctx"),) * 4
    data = P("fsdp", "ctx", None)
    in_specs = (
        (data, P("fsdp", None), P("ctx")) + weights + (P("ctx"),) + weights[:3] + (data,)
    )
    out_specs = (data, data, P("ctx")) + weights + (P("ctx"),) + weights[:3]
    return jax.shard_map(
        on_device, mesh=mesh, in_specs=in_specs, out_specs=out_specs, check_vma=False
    )
```

```python
import functools
import math

import jax
import jax.numpy as jnp
from jax import lax
from jax.experimental import pallas as pl
from jax.experimental.pallas import tpu as pltpu
from jax.sharding import PartitionSpec as P

QUERY_HEADS = 9
KEY_VALUE_HEADS = 3
HEAD_DIM = 64
GROUP = QUERY_HEADS // KEY_VALUE_HEADS

THETA = 100000.0
EPS = 1e-05
MASKED = -1e30
SCALE = 1.0 / math.sqrt(HEAD_DIM)
F32 = jnp.float32
BF16 = jnp.bfloat16
VMEM_BYTES = 56 * 1024 * 1024
CHIP_BYTES = 24 * 1024 * 1024

K_TILE, K_HALF = (0, 0, 1), (0, 1, 0)
V_TILE, V_HALF = (1, 2, 2), (1, 0, 1)


def round_up(n, m):
    return -(-n // m) * m


def swap(x, axis, mask):
    size = lax.axis_size(axis)
    return lax.ppermute(x, axis, [(i, i ^ mask) for i in range(size)])


def add_low(a, b):
    return (a.astype(F32) + b.astype(F32)).astype(BF16)


def outer_digits(shards):
    bits = list(range(1, shards.bit_length() - 1))
    return [tuple(bits[i : i + 2]) for i in range(0, len(bits), 2)]


def masks_of(digit):
    return [sum(1 << b for k, b in enumerate(digit) if n >> k & 1) for n in range(1 << len(digit))]


def join(pieces, *before):
    held = lax.optimization_barrier((*pieces, *before))[: len(pieces)]
    return jnp.concatenate(held, 0)


def gather_outer(x, shards):
    pieces = [x]
    for digit in outer_digits(shards):
        x = jnp.concatenate(pieces, 0)
        pieces = [x] + [swap(x, "ctx", m) for m in masks_of(digit)[1:]]
    return pieces


def scatter_outer(x, shards):
    for digit in outer_digits(shards)[::-1]:
        masks = masks_of(digit)
        parts = x.reshape((len(masks), -1) + x.shape[1:])
        terms = [parts[0]] + [swap(parts[n + 1], "ctx", m) for n, m in enumerate(masks[1:])]
        x = add_terms(terms).astype(BF16)
    return terms


def add_terms(terms, *before):
    held = lax.optimization_barrier((*terms, *before))[: len(terms)]
    return functools.reduce(lambda a, b: a + b, [t.astype(F32) for t in held])


def after(x, *before):
    return lax.optimization_barrier((x, *before))[0]


class Gather:
    def __init__(self, block, rows, shards):
        self.block, self.rows, self.shards = block, rows, shards

    def outer(self, *before):
        pieces = gather_outer(after(self.block[None], *before), self.shards)
        self.a = [p[:, : self.rows] for p in pieces]
        self.b = [p[:, self.rows :] for p in pieces]

    def phase(self, axis_a, mask_a, axis_b, mask_b, *before):
        a, b = join(self.a, *before), join(self.b, *before)
        self.now = a, b
        self.a, self.b = [a, swap(a, axis_a, mask_a)], [b, swap(b, axis_b, mask_b)]

    def second(self, *before):
        self.phase("ctx", 1, "fsdp", 2, *before)

    def third(self, *before):
        self.phase("fsdp", 2, "ctx", 1, *before)

    def cores_apart(self, *before):
        near, far = lax.optimization_barrier((*self.a, *before))[:2]
        b = join(self.b, *before)
        return near, far, swap(near, "fsdp", 1), swap(far, "fsdp", 1), b, swap(b, "fsdp", 1)

    def cores(self, *before):
        self.phase("fsdp", 1, "fsdp", 1, *before)
        return *self.a, *self.b


class Scatter:
    def __init__(self, keep_a, send_a, keep_b, send_b, shards, *before):
        self.a, self.b, self.shards = keep_a, keep_b, shards
        send_a, send_b = after(send_a, *before), after(send_b, *before)
        self.got_a, self.got_b = swap(send_a, "fsdp", 1), swap(send_b, "fsdp", 1)

    def fold(self, size, *before):
        a, b, got_a, got_b = lax.optimization_barrier(
            (self.a, self.b, self.got_a, self.got_b, *before)
        )[:4]
        self.a, self.b = add_low(a[:size], got_a[:size]), add_low(b[:size], got_b[:size])
        self.out = add_low(a[size:], got_a[size:]), add_low(b[size:], got_b[size:])
        return self.out

    def second(self, *before):
        a, b = self.fold(self.shards, *before)
        self.got_a, self.got_b = swap(a, "fsdp", 2), swap(b, "ctx", 1)

    def third(self, *before):
        a, b = self.fold(self.shards // 2, *before)
        self.got_a, self.got_b = swap(a, "ctx", 1), swap(b, "fsdp", 2)

    def outer(self, *before):
        a, b, got_a, got_b = lax.optimization_barrier(
            (self.a, self.b, self.got_a, self.got_b, *before)
        )[:4]
        self.terms = scatter_outer(
            jnp.concatenate([add_low(a, got_a), add_low(b, got_b)], 1), self.shards
        )

    def total(self, *before):
        return add_terms(self.terms, *before)[0]


def ctx_place(mask, shards):
    return (mask >> 1) + (shards // 2) * (mask & 1)


def place_a(cm, x_bit, shards):
    return ctx_place(cm, shards) + shards * x_bit


def place_b(cm, x_bit, shards):
    return (cm >> 1) + (shards // 2) * x_bit + shards * (cm & 1)


def arrange(out_ref, value, mine, feat):
    for k in range(value.shape[1] // feat):

        @pl.when(mine == k)
        def _():
            for m in range(value.shape[1] // feat):
                out_ref[:, m * feat : (m + 1) * feat] = value[:, (m ^ k) * feat : ((m ^ k) + 1) * feat]


def chunk_rows(parts, c, mc, fsdp, split, feat, shards, lanes):
    pieces = []
    for m in range(fsdp):
        a_ref, b_ref = parts[m & 1], parts[2 + (m & 1)]
        pieces.append(a_ref[place_a(c ^ mc, m >> 1, shards), :, lanes])
        pieces.append(b_ref[place_b(c ^ mc, m >> 1, shards), : feat - split, lanes])
    return jnp.concatenate(pieces, 0)


def dot(a, b):
    return lax.dot_general(a, b, (((1,), (0,)), ((), ())), preferred_element_type=F32)


def dot_nt(a, b):
    return lax.dot_general(a, b, (((1,), (1,)), ((), ())), preferred_element_type=F32)


def dot_tn(a, b):
    return lax.dot_general(a, b, (((0,), (0,)), ((), ())), preferred_element_type=F32)


def lane_ids():
    return lax.broadcasted_iota(jnp.int32, (1, 128), 1)


def turned(u):
    lane = lane_ids()
    first = (lane & (HEAD_DIM - 1)) < HEAD_DIM // 2
    return jnp.where(first, pltpu.roll(u, 96, 1), pltpu.roll(u, 32, 1))


def to_half(tile, source, target):
    return tile if source == target else pltpu.roll(tile, 64, 1)


def only_half(tile, half):
    lane = lane_ids()
    keep = lane >= 64 if half else lane < 64
    return jnp.where(keep, tile, 0.0)


def head_rows(h):
    return slice(h * 128, (h + 1) * 128)


def qkv_kernel(
    dims, meta, x_ref, ao_ref, as_ref, bo_ref, bs_ref, cos_ref, sin_ref,
    qp_ref, kv_ref, gain_ref, q_s, kv_s, n_s,
):
    shards, fsdp, cq, ck, split, feat = dims
    mc, mf = meta[shards], meta[shards + 1]
    parts = ao_ref, as_ref, bo_ref, bs_ref
    kvw = KEY_VALUE_HEADS * HEAD_DIM
    for c in range(shards):
        row = bo_ref[place_b(c ^ mc, 0, shards)][feat - split :, :].astype(F32)
        gain_ref[:, c * cq : (c + 1) * cq] = row[:, :cq]
        gain_ref[:, 640 + c * cq : 640 + (c + 1) * cq] = row[:, 128 : 128 + cq]
    x = x_ref[...].astype(F32)
    width = x.shape[1]
    rr = lax.rsqrt(jnp.mean(x * x, axis=-1, keepdims=True) + EPS)
    arrange(n_s, x * rr * gain_ref[0:1, :width], mf, feat)
    normed = n_s[...].astype(BF16)
    for c in range(shards):
        w = chunk_rows(parts, c, mc, fsdp, split, feat, shards, slice(0, 128))
        y = dot(normed, w)
        q_s[:, c * cq : (c + 1) * cq] = y[:, :cq]
        kv_s[:, c * ck : (c + 1) * ck] = y[:, cq : cq + ck]
        kv_s[:, kvw + c * ck : kvw + (c + 1) * ck] = y[:, cq + ck : cq + 2 * ck]
    cos, sin = cos_ref[...], sin_ref[...]
    for t in range(5):
        u = q_s[:, t * 128 : (t + 1) * 128]
        u = u * cos + turned(u) * sin
        for h in (2 * t, 2 * t + 1):
            if h < QUERY_HEADS:
                half = K_HALF[h // GROUP]
                qp_ref[head_rows(h), :] = only_half(to_half(u, h % 2, half), half).astype(BF16)
    for t in range(3):
        u = kv_s[:, t * 128 : (t + 1) * 128]
        if t < 2:
            r = u * cos + turned(u) * sin
            u = r if t == 0 else jnp.where(lane_ids() < 64, r, u)
        kv_ref[:, t * 128 : (t + 1) * 128] = u.astype(BF16)


def score_mask(meta, shards, block, chunks, blk):
    mc = meta[shards]
    mine = meta[mc]
    r = lax.broadcasted_iota(jnp.int32, (blk, GROUP * 2 * blk), 1) & (2 * blk - 1)
    qpos = jnp.where(r < blk, mine * blk + r, (2 * shards - 1 - mine) * blk + r - blk)
    gap = qpos - lax.broadcasted_iota(jnp.int32, qpos.shape, 0)
    out = []
    for i in range(chunks):
        pair = meta[mc ^ (2 * (block * (chunks // 2) + i % (chunks // 2)) + i // (chunks // 2))]
        out.append(gap >= pair * blk)
        out.append(gap >= (2 * shards - 1 - pair) * blk)
    return out


def block_rows(refs, block, chunks, blocks):
    if blocks == 1:
        values = [r[...] for r in refs]
    else:
        values = [r[pl.ds(block * (chunks // 2), chunks // 2)] for r in refs]
    return jnp.concatenate([v.reshape(-1, v.shape[2]) for v in values], 0)


def masked(s, mask, blk):
    return jnp.concatenate(
        [jnp.where(m, s[i * blk : (i + 1) * blk], MASKED) for i, m in enumerate(mask)], 0
    )


def attend_kernel(dims, meta, qp_ref, *refs):
    *kv_refs, att_ref, ot_ref, lse_ref, m_s, l_s = refs
    shards, chunks, blk = dims
    blocks = shards // chunks
    rows = chunks * 2 * blk
    span = GROUP * 2 * blk

    def block_step(b, first):
        mask = score_mask(meta, shards, b, chunks, blk)
        kv = block_rows(kv_refs, b, chunks, blocks)
        for g in range(KEY_VALUE_HEADS):
            keys = kv[:, K_TILE[g] * 128 : (K_TILE[g] + 1) * 128]
            vals = kv[:, V_TILE[g] * 128 : (V_TILE[g] + 1) * 128]
            s = masked(dot_nt(keys, qp_ref[g * span : (g + 1) * span, :]) * SCALE, mask, blk)
            top = jnp.max(s, axis=0, keepdims=True)
            if not first:
                top = jnp.maximum(top, m_s[g : g + 1, :])
            p = jnp.exp(s - top)
            total = jnp.sum(p, axis=0, keepdims=True)
            out = dot_tn(vals, p.astype(BF16))
            if not first:
                fade = jnp.exp(m_s[g : g + 1, :] - top)
                total = total + l_s[g : g + 1, :] * fade
                out = out + ot_ref[g] * fade
            m_s[g : g + 1, :] = top
            l_s[g : g + 1, :] = total
            ot_ref[g] = out

    block_step(0, True)
    if blocks > 1:

        @pl.loop(1, blocks)
        def _(b):
            block_step(b, False)

    tiles = {}
    for g in range(KEY_VALUE_HEADS):
        o = ot_ref[g] / l_s[g : g + 1, :]
        ot_ref[g] = o
        lse_ref[g : g + 1, :] = m_s[g : g + 1, :] + jnp.log(l_s[g : g + 1, :])
        for j in range(GROUP):
            h = g * GROUP + j
            tile = jnp.transpose(o[:, j * 128 : (j + 1) * 128])
            tiles[h] = to_half(tile, V_HALF[g], h % 2)
    for t in range(5):
        if 2 * t + 1 < QUERY_HEADS:
            tile = jnp.where(lane_ids() < 64, tiles[2 * t], tiles[2 * t + 1])
            att_ref[:, t * 128 : (t + 1) * 128] = tile.astype(BF16)
        else:
            att_ref[:, t * 128 : t * 128 + 64] = tiles[2 * t][:, :64].astype(BF16)


def ffn_kernel(
    dims, meta, att_ref, x_ref, dy_ref, gain_ref, *refs
):
    shards, fsdp, cq, cg, feat, ffr, fsplit, split, packed, asplit = dims
    ins, refs = (refs[:6], refs[6:]) if packed else (refs[:2], refs[2:])
    parts, refs = refs[:4], refs[4:]
    (
        out_ref, ak_ref, as_ref, bk_ref, bs_ref, dmid_ref, ggain_ref, gp_ref,
        gu_s, hid_s, dh_s, dgu_s, wide_s, p_s, dt_s,
    ) = refs
    mc, mf = meta[shards], meta[shards + 1]
    lanes = ak_ref.shape[2]
    if packed:
        for c in range(0, shards, 2):
            for m in range(fsdp):
                b_ref = ins[4 + (m & 1)]
                pair = [b_ref[place_b(d ^ mc, m >> 1, shards)][feat - fsplit :] for d in (c, c + 1)]
                dt_s[m, c * cq : (c + 2) * cq, :] = jnp.concatenate(
                    [p.astype(F32) for p in pair], 0
                ).astype(BF16)
    else:
        for m in range(fsdp):
            dt_s[m] = ins[1][mf ^ m]

    def weights(c):
        if packed:
            pieces = []
            for m in range(fsdp):
                pieces.append(ins[2 * (m & 1) + (m >> 1)][ctx_place(c ^ mc, shards)])
                if fsplit < feat:
                    b_ref = ins[4 + (m & 1)]
                    pieces.append(b_ref[place_b(c ^ mc, m >> 1, shards), : feat - fsplit, :])
            return jnp.concatenate(pieces, 0)
        return jnp.concatenate([ins[0][c, mf ^ m] for m in range(fsdp)], 0)

    def outer(c):
        return chunk_rows(parts, c, mc, fsdp, asplit, feat, shards, slice(-128, None))

    x = x_ref[...].astype(F32)
    width = x.shape[1]
    dy_t = dy_ref[...]
    dyf = jnp.transpose(dy_t.astype(F32))
    dyl = dyf.astype(BF16)
    gain = gain_ref[0:1, 640 : 640 + width]
    arrange(p_s, att_ref[...].astype(F32), mf, feat)
    attp = p_s[...].astype(BF16)
    for c in range(shards):
        wide_s[:, c * cq : (c + 1) * cq] = dot(attp, outer(c))[:, :cq]
    mid = x + wide_s[:, :width]
    rr = lax.rsqrt(jnp.mean(mid * mid, axis=-1, keepdims=True) + EPS)
    z = mid * rr
    arrange(p_s, z * gain, mf, feat)
    normed = p_s[...].astype(BF16)
    normed_t = jnp.transpose(p_s[...]).astype(BF16)

    def store_grad(c, m, row, value):
        end = row + value.shape[0]
        here = slice(0, value.shape[1])
        if row < split:
            stop = min(end, split)
            ref = (ak_ref, as_ref)[m & 1]
            ref[place_a(c ^ mc, m >> 1, shards), row:stop, here] = value[: stop - row]
        if end > split:
            start = max(row, split)
            ref = (bk_ref, bs_ref)[m & 1]
            ref[place_b(c ^ mc, m >> 1, shards), start - split : end - split, here] = value[start - row :]

    for c in range(shards):
        gu = dot(normed, weights(c))
        gu_s[c] = gu
        gate, up = gu[:, :cg], gu[:, cg : 2 * cg]
        hid_s[:, c * cg : (c + 1) * cg] = gate * jax.nn.sigmoid(gate) * up
    out = mid
    for m in range(fsdp):
        here = pl.ds(pl.multiple_of((mf ^ m) * ffr, 128), ffr)
        hid = hid_s[:, here].astype(BF16)
        out = out + dot_nt(hid, dt_s[m])
        dh_s[:, here] = dot(dyl, dt_s[m])
        g = dot(dy_t, hid)
        for c in range(shards):
            piece = g[c * cq : (c + 1) * cq, :].astype(BF16)
            for t in range(ffr // lanes):
                store_grad(c, m, feat + t * cq, piece[:, t * lanes : (t + 1) * lanes])
    out_ref[...] = jnp.transpose(out).astype(BF16)
    dn = jnp.zeros_like(mid)
    for c in range(shards):
        gu = gu_s[c]
        gate, up = gu[:, :cg], gu[:, cg : 2 * cg]
        dh = dh_s[:, c * cg : (c + 1) * cg]
        sg = jax.nn.sigmoid(gate)
        if 2 * cg < dgu_s.shape[1]:
            dgu_s[...] = jnp.zeros_like(dgu_s)
        dgu_s[:, :cg] = dh * up * sg * (1.0 + gate * (1.0 - sg))
        dgu_s[:, cg : 2 * cg] = dh * gate * sg
        dgu = dgu_s[...].astype(BF16)
        g = dot(normed_t, dgu)
        for m in range(fsdp):
            store_grad(c, m, 0, g[m * feat : (m + 1) * feat, :].astype(BF16))
        dn = dn + dot_nt(dgu, weights(c))
    arrange(p_s, dn, mf, feat)
    dn = p_s[...]
    e = dn * gain
    dmid = dyf + rr * (e - z * jnp.mean(e * z, axis=-1, keepdims=True))
    dmid_ref[...] = dmid
    ggain_ref[...] = jnp.broadcast_to(jnp.sum(dn * z, axis=0, keepdims=True), ggain_ref.shape)
    wide_s[...] = jnp.zeros_like(wide_s)
    wide_s[:, :width] = dmid
    ga = jnp.zeros_like(mid)
    for c in range(shards):
        gb = wide_s[:, c * cq : c * cq + 128].astype(BF16)
        ga = ga + dot_nt(gb, outer(c))
    arrange(p_s, ga, mf, feat)
    wide_s[:, :width] = p_s[...]
    for h in range(QUERY_HEADS):
        half = V_HALF[h // GROUP]
        tile = wide_s[:, (h // 2) * 128 : (h // 2 + 1) * 128]
        gp_ref[head_rows(h), :] = only_half(to_half(tile, h % 2, half), half).astype(BF16)


def attend_back_kernel(
    dims, meta, qp_ref, gp_ref, ot_ref, lse_ref, cos_ref, sin_ref, *refs
):
    *kv_refs, dq_ref, dnear_ref, dfar_ref, dq_s = refs
    shards, chunks, blk = dims
    blocks = shards // chunks
    rows = chunks * 2 * blk
    span = GROUP * 2 * blk
    deltas = []
    for g in range(KEY_VALUE_HEADS):
        gt = jnp.transpose(gp_ref[g * span : (g + 1) * span, :].astype(F32))
        deltas.append(jnp.sum(gt * ot_ref[g], axis=0, keepdims=True))

    def block_step(b, first):
        mask = score_mask(meta, shards, b, chunks, blk)
        kv = block_rows(kv_refs, b, chunks, blocks)
        tiles = [None, None, None]

        def put(t, value):
            tiles[t] = value if tiles[t] is None else tiles[t] + value

        for g in range(KEY_VALUE_HEADS):
            keys = kv[:, K_TILE[g] * 128 : (K_TILE[g] + 1) * 128]
            vals = kv[:, V_TILE[g] * 128 : (V_TILE[g] + 1) * 128]
            qg = qp_ref[g * span : (g + 1) * span, :]
            gg = gp_ref[g * span : (g + 1) * span, :]
            s = masked(dot_nt(keys, qg) * SCALE, mask, blk)
            p = jnp.exp(s - lse_ref[g : g + 1, :])
            ds = (p * (dot_nt(vals, gg) - deltas[g]) * SCALE).astype(BF16)
            put(V_TILE[g], dot(p.astype(BF16), gg))
            put(K_TILE[g], dot(ds, qg))
            dq = dot_tn(ds, keys)
            if first:
                dq_s[g * span : (g + 1) * span, :] = dq
            else:
                dq_s[g * span : (g + 1) * span, :] += dq
        for t in range(3):
            tile = tiles[t].astype(BF16).reshape(2, chunks // 2, 2 * blk, 128)
            for n, ref in enumerate((dnear_ref, dfar_ref)):
                ref[pl.ds(b * (chunks // 2), chunks // 2), :, t * 128 : (t + 1) * 128] = tile[n]

    block_step(0, True)
    if blocks > 1:

        @pl.loop(1, blocks)
        def _(b):
            block_step(b, False)

    cos, sin = cos_ref[...], sin_ref[...]
    tiles = {}
    for h in range(QUERY_HEADS):
        u = dq_s[head_rows(h), :]
        tiles[h] = to_half(u * cos - turned(u) * sin, K_HALF[h // GROUP], h % 2)
    for t in range(5):
        if 2 * t + 1 < QUERY_HEADS:
            tile = jnp.where(lane_ids() < 64, tiles[2 * t], tiles[2 * t + 1])
            dq_ref[:, t * 128 : (t + 1) * 128] = tile.astype(BF16)
        else:
            dq_ref[:, t * 128 : t * 128 + 64] = tiles[2 * t][:, :64].astype(BF16)


def qkv_back_kernel(
    dims, meta, x_ref, dq_ref, dkv_ref, att_ref, dmid_ref, gain_ref, gg_ref,
    cos_ref, sin_ref, ao_ref, as_in, bo_ref, bs_in, gin_ref, ak_ref, as_ref, bk_ref, bs_ref,
    dq_s, dkv_s, d_s, p_s, gg_s,
):
    shards, fsdp, cq, ck, split, feat = dims
    mc, mf = meta[shards], meta[shards + 1]
    parts = ao_ref, as_in, bo_ref, bs_in
    kvw = KEY_VALUE_HEADS * HEAD_DIM
    x = x_ref[...].astype(F32)
    width = x.shape[1]
    gain = gain_ref[0:1, :width]
    rr = lax.rsqrt(jnp.mean(x * x, axis=-1, keepdims=True) + EPS)
    z = x * rr
    arrange(p_s, z * gain, mf, feat)
    normed_t = jnp.transpose(p_s[...]).astype(BF16)
    arrange(p_s, att_ref[...].astype(F32), mf, feat)
    att_t = jnp.transpose(p_s[...]).astype(BF16)
    cos, sin = cos_ref[...], sin_ref[...]
    for t in range(3):
        u = dkv_ref[:, t * 128 : (t + 1) * 128]
        if t < 2:
            r = u * cos - turned(u) * sin
            u = r if t == 0 else jnp.where(lane_ids() < 64, r, u)
        dkv_s[:, t * 128 : (t + 1) * 128] = u
    dq_s[...] = dq_ref[...].astype(F32)
    d_s[...] = jnp.zeros_like(d_s)
    dn = jnp.zeros_like(x)
    for c in range(shards):
        d_s[:, :cq] = dq_s[:, c * cq : (c + 1) * cq]
        d_s[:, cq : cq + ck] = dkv_s[:, c * ck : (c + 1) * ck]
        d_s[:, cq + ck : cq + 2 * ck] = dkv_s[:, kvw + c * ck : kvw + (c + 1) * ck]
        d_s[:, 128 : 128 + cq] = dmid_ref[:, c * cq : (c + 1) * cq]
        d = d_s[...].astype(BF16)
        w = chunk_rows(parts, c, mc, fsdp, split, feat, shards, slice(0, 128))
        dn = dn + dot_nt(d[:, :128], w)
        g = jnp.concatenate([dot(normed_t, d[:, :128]), dot(att_t, d[:, 128:])], 1).astype(BF16)
        for m in range(fsdp):
            part = g[m * feat : (m + 1) * feat, :]
            (ak_ref, as_ref)[m & 1][place_a(c ^ mc, m >> 1, shards)] = part[:split]
            (bk_ref, bs_ref)[m & 1][place_b(c ^ mc, m >> 1, shards), : feat - split] = part[split:]
    arrange(p_s, dn, mf, feat)
    dn = p_s[...]
    e = dn * gain
    gin = dmid_ref[...] + rr * (e - z * jnp.mean(e * z, axis=-1, keepdims=True))
    gin_ref[...] = jnp.transpose(gin)
    gg_s[...] = jnp.broadcast_to(jnp.sum(dn * z, axis=0, keepdims=True), gg_s.shape)
    for c in range(shards):
        d_s[0:8, 0:cq] = gg_s[:, c * cq : (c + 1) * cq]
        d_s[0:8, 128 : 128 + cq] = gg_ref[:, c * cq : (c + 1) * cq]
        gains = d_s[0:8, :].astype(BF16)
        for m in range(fsdp):
            (bk_ref, bs_ref)[m & 1][place_b(c ^ mc, m >> 1, shards), feat - split :] = gains


def call(kernel, outs, scratch, flops, moved, *args, on_chip=False, leave=()):
    smem = pl.BlockSpec(memory_space=pltpu.SMEM)
    vmem = pl.BlockSpec(memory_space=pltpu.VMEM)
    if on_chip:
        args = args[:1] + tuple(pltpu.with_memory_space_constraint(a, pltpu.VMEM) for a in args[1:])
        outs = [
            o if n in leave else pltpu.VMEM(o.shape, o.dtype) for n, o in enumerate(outs)
        ]
    return pl.pallas_call(
        kernel,
        out_shape=outs,
        in_specs=[smem] + [vmem] * (len(args) - 1),
        out_specs=[vmem] * len(outs),
        scratch_shapes=scratch,
        cost_estimate=pl.CostEstimate(flops=flops, bytes_accessed=moved, transcendentals=0),
        compiler_params=pltpu.CompilerParams(vmem_limit_bytes=CHIP_BYTES if on_chip else VMEM_BYTES),
    )(*args)


def arr(shape, dtype):
    return jax.ShapeDtypeStruct(shape, dtype)


def on_device(
    tokens, pair_of, gain_attn, w_query, key_weight, value_weight, w_out, gain_ffn,
    w_gate, w_up, w_down, cotangent,
):
    rows, width = tokens.shape[1:]
    blk = rows // 2
    shards, fsdp = lax.axis_size("ctx"), lax.axis_size("fsdp")
    feat, cq = w_query.shape
    ck, cg, ffr = key_weight.shape[1], w_gate.shape[1], w_down.shape[0]
    ff = cg * shards
    x, dy = tokens[0], cotangent[0]
    meta = jnp.concatenate(
        [pair_of[0], jnp.stack([lax.axis_index("ctx"), lax.axis_index("fsdp")]).astype(jnp.int32)]
    )

    def fill(parts, total):
        used = sum(p.shape[1] for p in parts)
        return parts + [jnp.zeros((parts[0].shape[0], total - used), BF16)]

    lanes = 256
    body = jnp.concatenate(
        fill([w_query, key_weight, value_weight], 128) + fill([w_out], 128), 1
    )
    gains_row = jnp.concatenate(fill([gain_attn[None]], 128) + fill([gain_ffn[None]], 128), 1)
    own = jnp.concatenate([body, jnp.broadcast_to(gains_row, (8, lanes))], 0)
    split = 80

    cgl = round_up(2 * cg, 128)
    gu_own = jnp.concatenate(fill([w_gate, w_up], cgl), 1)
    dt_own = w_down.T
    packed = cgl == ffr and cq % 8 == 0
    ffn_split = feat
    if packed:
        ffn = Gather(jnp.concatenate([gu_own, dt_own], 0), ffn_split, shards)
    else:
        gu_all = lax.all_gather(gu_own, ("ctx", "fsdp"), axis=0).reshape(shards, fsdp, feat, cgl)
        dt_all = lax.all_gather(dt_own, ("ctx", "fsdp"), axis=0).reshape(shards, fsdp, cq, ffr)
        ffn_in = (gu_all, dt_all.transpose(1, 0, 2, 3).reshape(fsdp, width, ffr))

    attn = Gather(own, split, shards)
    attn.outer()
    if packed:
        ffn.outer(*attn.a, *attn.b)
    attn.second()
    attn.third()
    if packed:
        attn_in = attn.cores(*ffn.a, *ffn.b)
        ffn.second()
    else:
        attn_in = attn.cores()

    my_pair = pair_of[0, lax.axis_index("ctx")]
    offsets = jnp.arange(blk, dtype=jnp.int32)
    pos = jnp.concatenate([my_pair * blk + offsets, (2 * shards - 1 - my_pair) * blk + offsets])
    freq = THETA ** (-jnp.arange(HEAD_DIM // 2, dtype=F32) * 2.0 / HEAD_DIM)
    angles = pos.astype(F32)[:, None] * freq[None, :]
    cos, sin = jnp.cos(angles), jnp.sin(angles)
    cos_t = jnp.concatenate([cos] * 4, 1)
    sin_t = jnp.concatenate([-sin, sin] * 2, 1)

    kvl = 2 * KEY_VALUE_HEADS * HEAD_DIM
    hrows = QUERY_HEADS * rows
    qp, kv, gains = call(
        functools.partial(qkv_kernel, (shards, fsdp, cq, ck, split, feat)),
        [
            arr((hrows, 128), BF16), arr((rows, kvl), BF16),
            arr((8, 1280), F32),
        ],
        [
            pltpu.VMEM((rows, 640), F32), pltpu.VMEM((rows, kvl), F32),
            pltpu.VMEM((rows, width), F32),
        ],
        2 * rows * width * 128 * shards, 6_000_000,
        meta, x, *attn_in, cos_t, sin_t, on_chip=packed,
    )

    kv_pieces = gather_outer(kv[None], shards)
    kv_near = join(kv_pieces)
    if packed:
        cut = kv_near.shape[0] * 3 // 4
        kv_far = [swap(kv_near[:cut], "ctx", 1), swap(kv_near[cut:], "ctx", 1)]
        ffn.third(kv_pieces[1])
        ffn_in = ffn.cores_apart(kv_far[0])
    else:
        kv_far = [swap(kv_near, "ctx", 1)]
    chunks = min(8, shards)
    span = GROUP * rows
    att, ot, lse = call(
        functools.partial(attend_kernel, (shards, chunks, blk)),
        [arr((rows, width), BF16), arr((KEY_VALUE_HEADS, 128, span), F32), arr((8, span), F32)],
        [pltpu.VMEM((8, span), F32), pltpu.VMEM((8, span), F32)],
        4 * hrows * shards * rows * 128, 3_000_000,
        meta, qp, kv_near, *kv_far, on_chip=packed,
    )

    glanes = cgl
    tiles = ffr // glanes
    parts = [arr((2 * shards, feat, glanes), BF16)] * 2
    parts += [arr((2 * shards, tiles * cq, glanes), BF16)] * 2
    out, *g_ffn, dmid, ggain, gp = call(
        functools.partial(
            ffn_kernel, (shards, fsdp, cq, cg, feat, ffr, ffn_split, feat, packed, split)
        ),
        [arr((width, rows), BF16), *parts]
        + [arr((rows, width), F32), arr((8, width), F32), arr((hrows, 128), BF16)],
        [
            pltpu.VMEM((shards, rows, cgl), F32), pltpu.VMEM((rows, ff), F32),
            pltpu.VMEM((rows, ff), F32), pltpu.VMEM((rows, cgl), F32), pltpu.VMEM((rows, 768), F32),
            pltpu.VMEM((rows, width), F32), pltpu.VMEM((fsdp, width, ffr), BF16),
        ],
        18 * rows * width * ff, 14_000_000,
        meta, att, x, dy.T, gains, *ffn_in, *(attn_in if packed else [p[:, :, 128:] for p in attn_in]),
        on_chip=packed, leave=(0,),
    )
    ffn_sum = Scatter(*g_ffn, shards)
    ffn_sum.second()

    dq, dkv_near, dkv_far = call(
        functools.partial(attend_back_kernel, (shards, chunks, blk)),
        [arr((rows, width), BF16)] + [arr((shards // 2, rows, kvl), BF16)] * 2,
        [pltpu.VMEM((hrows, 128), F32)],
        10 * hrows * shards * rows * 128, 5_000_000,
        meta, qp, gp, ot, lse, cos_t, sin_t, kv_near, *kv_far, on_chip=packed,
    )
    dkv_far = after(dkv_far, *ffn_sum.out)
    dkv_terms = scatter_outer(add_low(dkv_near, swap(dkv_far, "ctx", 1)), shards)
    ffn_sum.third()
    dkv = add_terms(dkv_terms, *ffn_sum.out)[0]

    grad_input, *g_attn = call(
        functools.partial(qkv_back_kernel, (shards, fsdp, cq, ck, split, feat)),
        [arr((width, rows), F32)]
        + [arr((2 * shards, split, lanes), BF16)] * 2
        + [arr((2 * shards, feat + 8 - split, lanes), BF16)] * 2,
        [
            pltpu.VMEM((rows, width), F32), pltpu.VMEM((rows, kvl), F32),
            pltpu.VMEM((rows, lanes), F32), pltpu.VMEM((rows, width), F32),
            pltpu.VMEM((8, width), F32),
        ],
        6 * rows * width * 256 * shards, 6_000_000,
        meta, x, dq, dkv, att, dmid, gains, ggain, cos_t, sin_t, *attn_in,
        on_chip=packed, leave=(0,),
    )
    attn_sum = Scatter(*g_attn, shards, ffn_sum.got_a, ffn_sum.got_b)
    ffn_sum.outer()
    attn_sum.second()
    attn_sum.third()
    ffn_own = ffn_sum.total(*attn_sum.out)
    attn_sum.outer()
    attn_own = attn_sum.total()
    return (
        out.T[None],
        grad_input.T[None],
        attn_own[feat, :cq],
        attn_own[:feat, :cq],
        attn_own[:feat, cq : cq + ck],
        attn_own[:feat, cq + ck : cq + 2 * ck],
        attn_own[:feat, 128 : 128 + cq],
        attn_own[feat, 128 : 128 + cq],
        ffn_own[:feat, :cg],
        ffn_own[:feat, cg : 2 * cg],
        jnp.concatenate([ffn_own[feat + t * cq : feat + (t + 1) * cq] for t in range(tiles)], 1).T,
    )


def solution(mesh):
    weights = (P("fsdp", "ctx"),) * 4
    data = P("fsdp", "ctx", None)
    in_specs = (
        (data, P("fsdp", None), P("ctx")) + weights + (P("ctx"),) + weights[:3] + (data,)
    )
    out_specs = (data, data, P("ctx")) + weights + (P("ctx"),) + weights[:3]
    return jax.shard_map(
        on_device, mesh=mesh, in_specs=in_specs, out_specs=out_specs, check_vma=False
    )
```

```python
import functools
import math

import jax
import jax.numpy as jnp
from jax import lax
from jax.experimental import pallas as pl
from jax.experimental.pallas import tpu as pltpu
from jax.sharding import PartitionSpec as P

QUERY_HEADS = 9
KEY_VALUE_HEADS = 3
HEAD_DIM = 64
GROUP = QUERY_HEADS // KEY_VALUE_HEADS

THETA = 100000.0
EPS = 1e-05
MASKED = -1e30
SCALE = 1.0 / math.sqrt(HEAD_DIM)
F32 = jnp.float32
BF16 = jnp.bfloat16
VMEM_BYTES = 56 * 1024 * 1024
CHIP_BYTES = 24 * 1024 * 1024

K_TILE, K_HALF = (0, 0, 1), (0, 1, 0)
V_TILE, V_HALF = (1, 2, 2), (1, 0, 1)


def round_up(n, m):
    return -(-n // m) * m


def swap(x, axis, mask):
    size = lax.axis_size(axis)
    return lax.ppermute(x, axis, [(i, i ^ mask) for i in range(size)])


def add_low(a, b):
    return (a.astype(F32) + b.astype(F32)).astype(BF16)


def outer_digits(shards):
    bits = list(range(1, shards.bit_length() - 1))
    return [tuple(bits[i : i + 2]) for i in range(0, len(bits), 2)]


def masks_of(digit):
    return [sum(1 << b for k, b in enumerate(digit) if n >> k & 1) for n in range(1 << len(digit))]


def join(pieces, *before):
    held = lax.optimization_barrier((*pieces, *before))[: len(pieces)]
    return jnp.concatenate(held, 0)


def gather_outer(x, shards):
    pieces = [x]
    for digit in outer_digits(shards):
        x = jnp.concatenate(pieces, 0)
        pieces = [x] + [swap(x, "ctx", m) for m in masks_of(digit)[1:]]
    return pieces


def scatter_outer(x, shards):
    for digit in outer_digits(shards)[::-1]:
        masks = masks_of(digit)
        parts = x.reshape((len(masks), -1) + x.shape[1:])
        terms = [parts[0]] + [swap(parts[n + 1], "ctx", m) for n, m in enumerate(masks[1:])]
        x = add_terms(terms).astype(BF16)
    return terms


def add_terms(terms, *before):
    held = lax.optimization_barrier((*terms, *before))[: len(terms)]
    return functools.reduce(lambda a, b: a + b, [t.astype(F32) for t in held])


def after(x, *before):
    return lax.optimization_barrier((x, *before))[0]


class Gather:
    def __init__(self, block, rows, shards):
        self.block, self.rows, self.shards = block, rows, shards

    def outer(self, *before):
        pieces = gather_outer(after(self.block[None], *before), self.shards)
        self.a = [p[:, : self.rows] for p in pieces]
        self.b = [p[:, self.rows :] for p in pieces]

    def phase(self, axis_a, mask_a, axis_b, mask_b, *before):
        a, b = join(self.a, *before), join(self.b, *before)
        self.now = a, b
        self.a, self.b = [a, swap(a, axis_a, mask_a)], [b, swap(b, axis_b, mask_b)]

    def second(self, *before):
        self.phase("ctx", 1, "fsdp", 2, *before)

    def third(self, *before):
        self.phase("fsdp", 2, "ctx", 1, *before)

    def cores_apart(self, *before):
        near, far = lax.optimization_barrier((*self.a, *before))[:2]
        b = join(self.b, *before)
        return near, far, swap(near, "fsdp", 1), swap(far, "fsdp", 1), b, swap(b, "fsdp", 1)

    def cores(self, *before):
        self.phase("fsdp", 1, "fsdp", 1, *before)
        return *self.a, *self.b


class Scatter:
    def __init__(self, keep_a, send_a, keep_b, send_b, shards, *before):
        self.a, self.b, self.shards = keep_a, keep_b, shards
        send_a, send_b = after(send_a, *before), after(send_b, *before)
        self.got_a, self.got_b = swap(send_a, "fsdp", 1), swap(send_b, "fsdp", 1)

    def fold(self, size, *before):
        a, b, got_a, got_b = lax.optimization_barrier(
            (self.a, self.b, self.got_a, self.got_b, *before)
        )[:4]
        self.a, self.b = add_low(a[:size], got_a[:size]), add_low(b[:size], got_b[:size])
        self.out = add_low(a[size:], got_a[size:]), add_low(b[size:], got_b[size:])
        return self.out

    def second(self, *before, late=None):
        a, b = self.fold(self.shards, *before)
        wait = () if late is None else late(a, b)
        self.got_a, self.got_b = swap(a, "fsdp", 2), swap(after(b, *wait), "ctx", 1)

    def third(self, *before):
        a, b = self.fold(self.shards // 2, *before)
        self.got_a, self.got_b = swap(a, "ctx", 1), swap(b, "fsdp", 2)

    def outer(self, *before):
        a, b, got_a, got_b = lax.optimization_barrier(
            (self.a, self.b, self.got_a, self.got_b, *before)
        )[:4]
        self.last = jnp.concatenate([add_low(a, got_a), add_low(b, got_b)], 1)
        self.terms = scatter_outer(self.last, self.shards)

    def total(self, *before):
        return add_terms(self.terms, *before)[0]


def ctx_place(mask, shards):
    return (mask >> 1) + (shards // 2) * (mask & 1)


def place_a(cm, x_bit, shards):
    return ctx_place(cm, shards) + shards * x_bit


def place_b(cm, x_bit, shards):
    return (cm >> 1) + (shards // 2) * x_bit + shards * (cm & 1)


def arrange(out_ref, value, mine, feat):
    for k in range(value.shape[1] // feat):

        @pl.when(mine == k)
        def _():
            for m in range(value.shape[1] // feat):
                out_ref[:, m * feat : (m + 1) * feat] = value[:, (m ^ k) * feat : ((m ^ k) + 1) * feat]


def chunk_rows(parts, c, mc, fsdp, split, feat, shards, lanes):
    pieces = []
    for m in range(fsdp):
        a_ref, b_ref = parts[m & 1], parts[2 + (m & 1)]
        pieces.append(a_ref[place_a(c ^ mc, m >> 1, shards), :, lanes])
        pieces.append(b_ref[place_b(c ^ mc, m >> 1, shards), : feat - split, lanes])
    return jnp.concatenate(pieces, 0)


def dot(a, b):
    return lax.dot_general(a, b, (((1,), (0,)), ((), ())), preferred_element_type=F32)


def dot_nt(a, b):
    return lax.dot_general(a, b, (((1,), (1,)), ((), ())), preferred_element_type=F32)


def dot_tn(a, b):
    return lax.dot_general(a, b, (((0,), (0,)), ((), ())), preferred_element_type=F32)


def lane_ids():
    return lax.broadcasted_iota(jnp.int32, (1, 128), 1)


def turned(u):
    lane = lane_ids()
    first = (lane & (HEAD_DIM - 1)) < HEAD_DIM // 2
    return jnp.where(first, pltpu.roll(u, 96, 1), pltpu.roll(u, 32, 1))


def to_half(tile, source, target):
    return tile if source == target else pltpu.roll(tile, 64, 1)


def only_half(tile, half):
    lane = lane_ids()
    keep = lane >= 64 if half else lane < 64
    return jnp.where(keep, tile, 0.0)


def head_rows(h):
    return slice(h * 128, (h + 1) * 128)


def qkv_kernel(
    dims, meta, x_ref, ao_ref, as_ref, bo_ref, bs_ref, cos_ref, sin_ref,
    qp_ref, kv_ref, gain_ref, q_s, kv_s, n_s,
):
    shards, fsdp, cq, ck, split, feat = dims
    mc, mf = meta[shards], meta[shards + 1]
    parts = ao_ref, as_ref, bo_ref, bs_ref
    kvw = KEY_VALUE_HEADS * HEAD_DIM
    for c in range(shards):
        row = bo_ref[place_b(c ^ mc, 0, shards)][feat - split :, :].astype(F32)
        gain_ref[:, c * cq : (c + 1) * cq] = row[:, :cq]
        gain_ref[:, 640 + c * cq : 640 + (c + 1) * cq] = row[:, 128 : 128 + cq]
    x = x_ref[...].astype(F32)
    width = x.shape[1]
    rr = lax.rsqrt(jnp.mean(x * x, axis=-1, keepdims=True) + EPS)
    arrange(n_s, x * rr * gain_ref[0:1, :width], mf, feat)
    normed = n_s[...].astype(BF16)
    for c in range(shards):
        w = chunk_rows(parts, c, mc, fsdp, split, feat, shards, slice(0, 128))
        y = dot(normed, w)
        q_s[:, c * cq : (c + 1) * cq] = y[:, :cq]
        kv_s[:, c * ck : (c + 1) * ck] = y[:, cq : cq + ck]
        kv_s[:, kvw + c * ck : kvw + (c + 1) * ck] = y[:, cq + ck : cq + 2 * ck]
    cos, sin = cos_ref[...], sin_ref[...]
    for t in range(5):
        u = q_s[:, t * 128 : (t + 1) * 128]
        u = u * cos + turned(u) * sin
        for h in (2 * t, 2 * t + 1):
            if h < QUERY_HEADS:
                half = K_HALF[h // GROUP]
                qp_ref[head_rows(h), :] = only_half(to_half(u, h % 2, half), half).astype(BF16)
    for t in range(3):
        u = kv_s[:, t * 128 : (t + 1) * 128]
        if t < 2:
            r = u * cos + turned(u) * sin
            u = r if t == 0 else jnp.where(lane_ids() < 64, r, u)
        kv_ref[:, t * 128 : (t + 1) * 128] = u.astype(BF16)


def score_mask(meta, shards, block, chunks, blk):
    mc = meta[shards]
    mine = meta[mc]
    r = lax.broadcasted_iota(jnp.int32, (blk, GROUP * 2 * blk), 1) & (2 * blk - 1)
    qpos = jnp.where(r < blk, mine * blk + r, (2 * shards - 1 - mine) * blk + r - blk)
    gap = qpos - lax.broadcasted_iota(jnp.int32, qpos.shape, 0)
    out = []
    for i in range(chunks):
        pair = meta[mc ^ (2 * (block * (chunks // 2) + i % (chunks // 2)) + i // (chunks // 2))]
        out.append(gap >= pair * blk)
        out.append(gap >= (2 * shards - 1 - pair) * blk)
    return out


def block_rows(refs, block, chunks, blocks):
    if blocks == 1:
        values = [r[...] for r in refs]
    else:
        values = [r[pl.ds(block * (chunks // 2), chunks // 2)] for r in refs]
    return jnp.concatenate([v.reshape(-1, v.shape[2]) for v in values], 0)


def masked(s, mask, blk):
    return jnp.concatenate(
        [jnp.where(m, s[i * blk : (i + 1) * blk], MASKED) for i, m in enumerate(mask)], 0
    )


def attend_kernel(dims, meta, qp_ref, *refs):
    *kv_refs, att_ref, ot_ref, lse_ref, m_s, l_s = refs
    shards, chunks, blk = dims
    blocks = shards // chunks
    rows = chunks * 2 * blk
    span = GROUP * 2 * blk

    def block_step(b, first):
        mask = score_mask(meta, shards, b, chunks, blk)
        kv = block_rows(kv_refs, b, chunks, blocks)
        for g in range(KEY_VALUE_HEADS):
            keys = kv[:, K_TILE[g] * 128 : (K_TILE[g] + 1) * 128]
            vals = kv[:, V_TILE[g] * 128 : (V_TILE[g] + 1) * 128]
            s = masked(dot_nt(keys, qp_ref[g * span : (g + 1) * span, :]) * SCALE, mask, blk)
            top = jnp.max(s, axis=0, keepdims=True)
            if not first:
                top = jnp.maximum(top, m_s[g : g + 1, :])
            p = jnp.exp(s - top)
            total = jnp.sum(p, axis=0, keepdims=True)
            out = dot_tn(vals, p.astype(BF16))
            if not first:
                fade = jnp.exp(m_s[g : g + 1, :] - top)
                total = total + l_s[g : g + 1, :] * fade
                out = out + ot_ref[g] * fade
            m_s[g : g + 1, :] = top
            l_s[g : g + 1, :] = total
            ot_ref[g] = out

    block_step(0, True)
    if blocks > 1:

        @pl.loop(1, blocks)
        def _(b):
            block_step(b, False)

    tiles = {}
    for g in range(KEY_VALUE_HEADS):
        o = ot_ref[g] / l_s[g : g + 1, :]
        ot_ref[g] = o
        lse_ref[g : g + 1, :] = m_s[g : g + 1, :] + jnp.log(l_s[g : g + 1, :])
        for j in range(GROUP):
            h = g * GROUP + j
            tile = jnp.transpose(o[:, j * 128 : (j + 1) * 128])
            tiles[h] = to_half(tile, V_HALF[g], h % 2)
    for t in range(5):
        if 2 * t + 1 < QUERY_HEADS:
            tile = jnp.where(lane_ids() < 64, tiles[2 * t], tiles[2 * t + 1])
            att_ref[:, t * 128 : (t + 1) * 128] = tile.astype(BF16)
        else:
            att_ref[:, t * 128 : t * 128 + 64] = tiles[2 * t][:, :64].astype(BF16)


def ffn_kernel(
    dims, meta, att_ref, x_ref, dy_ref, gain_ref, *refs
):
    shards, fsdp, cq, cg, feat, ffr, fsplit, split, packed, asplit = dims
    ins, refs = (refs[:6], refs[6:]) if packed else (refs[:2], refs[2:])
    parts, refs = refs[:4], refs[4:]
    (
        out_ref, ak_ref, as_ref, bk_ref, bs_ref, dmid_ref, ggain_ref, gp_ref,
        gu_s, hid_s, dh_s, dgu_s, wide_s, p_s, dt_s,
    ) = refs
    mc, mf = meta[shards], meta[shards + 1]
    lanes = ak_ref.shape[2]
    if packed:
        for c in range(0, shards, 2):
            for m in range(fsdp):
                b_ref = ins[4 + (m & 1)]
                pair = [b_ref[place_b(d ^ mc, m >> 1, shards)][feat - fsplit :] for d in (c, c + 1)]
                dt_s[m, c * cq : (c + 2) * cq, :] = jnp.concatenate(
                    [p.astype(F32) for p in pair], 0
                ).astype(BF16)
    else:
        for m in range(fsdp):
            dt_s[m] = ins[1][mf ^ m]

    def weights(c):
        if packed:
            pieces = []
            for m in range(fsdp):
                pieces.append(ins[2 * (m & 1) + (m >> 1)][ctx_place(c ^ mc, shards)])
                if fsplit < feat:
                    b_ref = ins[4 + (m & 1)]
                    pieces.append(b_ref[place_b(c ^ mc, m >> 1, shards), : feat - fsplit, :])
            return jnp.concatenate(pieces, 0)
        return jnp.concatenate([ins[0][c, mf ^ m] for m in range(fsdp)], 0)

    def outer(c):
        return chunk_rows(parts, c, mc, fsdp, asplit, feat, shards, slice(-128, None))

    x = x_ref[...].astype(F32)
    width = x.shape[1]
    dy_t = dy_ref[...]
    dyf = jnp.transpose(dy_t.astype(F32))
    dyl = dyf.astype(BF16)
    gain = gain_ref[0:1, 640 : 640 + width]
    arrange(p_s, att_ref[...].astype(F32), mf, feat)
    attp = p_s[...].astype(BF16)
    for c in range(shards):
        wide_s[:, c * cq : (c + 1) * cq] = dot(attp, outer(c))[:, :cq]
    mid = x + wide_s[:, :width]
    rr = lax.rsqrt(jnp.mean(mid * mid, axis=-1, keepdims=True) + EPS)
    z = mid * rr
    arrange(p_s, z * gain, mf, feat)
    normed = p_s[...].astype(BF16)
    normed_t = jnp.transpose(p_s[...]).astype(BF16)

    def store_grad(c, m, row, value):
        end = row + value.shape[0]
        here = slice(0, value.shape[1])
        if row < split:
            stop = min(end, split)
            ref = (ak_ref, as_ref)[m & 1]
            ref[place_a(c ^ mc, m >> 1, shards), row:stop, here] = value[: stop - row]
        if end > split:
            start = max(row, split)
            ref = (bk_ref, bs_ref)[m & 1]
            ref[place_b(c ^ mc, m >> 1, shards), start - split : end - split, here] = value[start - row :]

    for c in range(shards):
        gu = dot(normed, weights(c))
        gu_s[c] = gu
        gate, up = gu[:, :cg], gu[:, cg : 2 * cg]
        hid_s[:, c * cg : (c + 1) * cg] = gate * jax.nn.sigmoid(gate) * up
    out = mid
    for m in range(fsdp):
        here = pl.ds(pl.multiple_of((mf ^ m) * ffr, 128), ffr)
        hid = hid_s[:, here].astype(BF16)
        out = out + dot_nt(hid, dt_s[m])
        dh_s[:, here] = dot(dyl, dt_s[m])
        g = dot(dy_t, hid)
        for c in range(shards):
            piece = g[c * cq : (c + 1) * cq, :].astype(BF16)
            for t in range(ffr // lanes):
                store_grad(c, m, feat + t * cq, piece[:, t * lanes : (t + 1) * lanes])
    out_ref[...] = jnp.transpose(out).astype(BF16)
    dn = jnp.zeros_like(mid)
    for c in range(shards):
        gu = gu_s[c]
        gate, up = gu[:, :cg], gu[:, cg : 2 * cg]
        dh = dh_s[:, c * cg : (c + 1) * cg]
        sg = jax.nn.sigmoid(gate)
        if 2 * cg < dgu_s.shape[1]:
            dgu_s[...] = jnp.zeros_like(dgu_s)
        dgu_s[:, :cg] = dh * up * sg * (1.0 + gate * (1.0 - sg))
        dgu_s[:, cg : 2 * cg] = dh * gate * sg
        dgu = dgu_s[...].astype(BF16)
        g = dot(normed_t, dgu)
        for m in range(fsdp):
            store_grad(c, m, 0, g[m * feat : (m + 1) * feat, :].astype(BF16))
        dn = dn + dot_nt(dgu, weights(c))
    arrange(p_s, dn, mf, feat)
    dn = p_s[...]
    e = dn * gain
    dmid = dyf + rr * (e - z * jnp.mean(e * z, axis=-1, keepdims=True))
    dmid_ref[...] = dmid
    ggain_ref[...] = jnp.broadcast_to(jnp.sum(dn * z, axis=0, keepdims=True), ggain_ref.shape)
    wide_s[...] = jnp.zeros_like(wide_s)
    wide_s[:, :width] = dmid
    ga = jnp.zeros_like(mid)
    for c in range(shards):
        gb = wide_s[:, c * cq : c * cq + 128].astype(BF16)
        ga = ga + dot_nt(gb, outer(c))
    arrange(p_s, ga, mf, feat)
    wide_s[:, :width] = p_s[...]
    for h in range(QUERY_HEADS):
        half = V_HALF[h // GROUP]
        tile = wide_s[:, (h // 2) * 128 : (h // 2 + 1) * 128]
        gp_ref[head_rows(h), :] = only_half(to_half(tile, h % 2, half), half).astype(BF16)


def attend_back_kernel(
    dims, meta, qp_ref, gp_ref, ot_ref, lse_ref, cos_ref, sin_ref, *refs
):
    *kv_refs, dq_ref, dnear_ref, dfar_ref, dq_s = refs
    shards, chunks, blk = dims
    blocks = shards // chunks
    rows = chunks * 2 * blk
    span = GROUP * 2 * blk
    deltas = []
    for g in range(KEY_VALUE_HEADS):
        gt = jnp.transpose(gp_ref[g * span : (g + 1) * span, :].astype(F32))
        deltas.append(jnp.sum(gt * ot_ref[g], axis=0, keepdims=True))

    def block_step(b, first):
        mask = score_mask(meta, shards, b, chunks, blk)
        kv = block_rows(kv_refs, b, chunks, blocks)
        tiles = [None, None, None]

        def put(t, value):
            tiles[t] = value if tiles[t] is None else tiles[t] + value

        for g in range(KEY_VALUE_HEADS):
            keys = kv[:, K_TILE[g] * 128 : (K_TILE[g] + 1) * 128]
            vals = kv[:, V_TILE[g] * 128 : (V_TILE[g] + 1) * 128]
            qg = qp_ref[g * span : (g + 1) * span, :]
            gg = gp_ref[g * span : (g + 1) * span, :]
            s = masked(dot_nt(keys, qg) * SCALE, mask, blk)
            p = jnp.exp(s - lse_ref[g : g + 1, :])
            ds = (p * (dot_nt(vals, gg) - deltas[g]) * SCALE).astype(BF16)
            put(V_TILE[g], dot(p.astype(BF16), gg))
            put(K_TILE[g], dot(ds, qg))
            dq = dot_tn(ds, keys)
            if first:
                dq_s[g * span : (g + 1) * span, :] = dq
            else:
                dq_s[g * span : (g + 1) * span, :] += dq
        for t in range(3):
            tile = tiles[t].astype(BF16).reshape(2, chunks // 2, 2 * blk, 128)
            for n, ref in enumerate((dnear_ref, dfar_ref)):
                ref[pl.ds(b * (chunks // 2), chunks // 2), :, t * 128 : (t + 1) * 128] = tile[n]

    block_step(0, True)
    if blocks > 1:

        @pl.loop(1, blocks)
        def _(b):
            block_step(b, False)

    cos, sin = cos_ref[...], sin_ref[...]
    tiles = {}
    for h in range(QUERY_HEADS):
        u = dq_s[head_rows(h), :]
        tiles[h] = to_half(u * cos - turned(u) * sin, K_HALF[h // GROUP], h % 2)
    for t in range(5):
        if 2 * t + 1 < QUERY_HEADS:
            tile = jnp.where(lane_ids() < 64, tiles[2 * t], tiles[2 * t + 1])
            dq_ref[:, t * 128 : (t + 1) * 128] = tile.astype(BF16)
        else:
            dq_ref[:, t * 128 : t * 128 + 64] = tiles[2 * t][:, :64].astype(BF16)


def qkv_back_kernel(
    dims, meta, x_ref, dq_ref, dkv_ref, att_ref, dmid_ref, gain_ref, gg_ref,
    cos_ref, sin_ref, ao_ref, as_in, bo_ref, bs_in, gin_ref, ak_ref, as_ref, bk_ref, bs_ref,
    dq_s, dkv_s, d_s, p_s, gg_s,
):
    shards, fsdp, cq, ck, split, feat = dims
    mc, mf = meta[shards], meta[shards + 1]
    parts = ao_ref, as_in, bo_ref, bs_in
    kvw = KEY_VALUE_HEADS * HEAD_DIM
    x = x_ref[...].astype(F32)
    width = x.shape[1]
    gain = gain_ref[0:1, :width]
    rr = lax.rsqrt(jnp.mean(x * x, axis=-1, keepdims=True) + EPS)
    z = x * rr
    arrange(p_s, z * gain, mf, feat)
    normed_t = jnp.transpose(p_s[...]).astype(BF16)
    arrange(p_s, att_ref[...].astype(F32), mf, feat)
    att_t = jnp.transpose(p_s[...]).astype(BF16)
    cos, sin = cos_ref[...], sin_ref[...]
    for t in range(3):
        u = dkv_ref[:, t * 128 : (t + 1) * 128]
        if t < 2:
            r = u * cos - turned(u) * sin
            u = r if t == 0 else jnp.where(lane_ids() < 64, r, u)
        dkv_s[:, t * 128 : (t + 1) * 128] = u
    dq_s[...] = dq_ref[...].astype(F32)
    d_s[...] = jnp.zeros_like(d_s)
    dn = jnp.zeros_like(x)
    for c in range(shards):
        d_s[:, :cq] = dq_s[:, c * cq : (c + 1) * cq]
        d_s[:, cq : cq + ck] = dkv_s[:, c * ck : (c + 1) * ck]
        d_s[:, cq + ck : cq + 2 * ck] = dkv_s[:, kvw + c * ck : kvw + (c + 1) * ck]
        d_s[:, 128 : 128 + cq] = dmid_ref[:, c * cq : (c + 1) * cq]
        d = d_s[...].astype(BF16)
        w = chunk_rows(parts, c, mc, fsdp, split, feat, shards, slice(0, 128))
        dn = dn + dot_nt(d[:, :128], w)
        g = jnp.concatenate([dot(normed_t, d[:, :128]), dot(att_t, d[:, 128:])], 1).astype(BF16)
        for m in range(fsdp):
            part = g[m * feat : (m + 1) * feat, :]
            (ak_ref, as_ref)[m & 1][place_a(c ^ mc, m >> 1, shards)] = part[:split]
            (bk_ref, bs_ref)[m & 1][place_b(c ^ mc, m >> 1, shards), : feat - split] = part[split:]
    arrange(p_s, dn, mf, feat)
    dn = p_s[...]
    e = dn * gain
    gin = dmid_ref[...] + rr * (e - z * jnp.mean(e * z, axis=-1, keepdims=True))
    gin_ref[...] = jnp.transpose(gin)
    gg_s[...] = jnp.broadcast_to(jnp.sum(dn * z, axis=0, keepdims=True), gg_s.shape)
    for c in range(shards):
        d_s[0:8, 0:cq] = gg_s[:, c * cq : (c + 1) * cq]
        d_s[0:8, 128 : 128 + cq] = gg_ref[:, c * cq : (c + 1) * cq]
        gains = d_s[0:8, :].astype(BF16)
        for m in range(fsdp):
            (bk_ref, bs_ref)[m & 1][place_b(c ^ mc, m >> 1, shards), feat - split :] = gains


def pack_kernel(wq_ref, wkt_ref, wvt_ref, wo_ref, ga_ref, gf_ref, own_ref, t_s):
    feat, cq = wq_ref.shape
    ck = wkt_ref.shape[0]
    t_s[...] = jnp.zeros_like(t_s)
    t_s[:feat, :cq] = wq_ref[...].astype(F32)
    t_s[:feat, cq : cq + ck] = jnp.transpose(wkt_ref[...].astype(F32))
    t_s[:feat, cq + ck : cq + 2 * ck] = jnp.transpose(wvt_ref[...].astype(F32))
    t_s[:feat, 128 : 128 + cq] = wo_ref[...].astype(F32)
    t_s[feat : feat + 1, :cq] = ga_ref[...].astype(F32)
    t_s[feat : feat + 1, 128 : 128 + cq] = gf_ref[...].astype(F32)
    own_ref[...] = t_s[...].astype(BF16)


def finish_kernel(ck, *refs):
    *terms, gq_ref, gkt_ref, gvt_ref, go_ref, ga_ref, gf_ref = refs
    feat, cq = gq_ref.shape
    total = functools.reduce(lambda a, b: a + b, [t[...].astype(F32) for t in terms])
    gq_ref[...] = total[:feat, :cq]
    turned_round = jnp.transpose(total[:feat, :128])
    gkt_ref[...] = turned_round[cq : cq + ck]
    gvt_ref[...] = turned_round[cq + ck : cq + 2 * ck]
    go_ref[...] = total[:feat, 128 : 128 + cq]
    ga_ref[...] = total[feat : feat + 1, :cq]
    gf_ref[...] = total[feat : feat + 1, 128 : 128 + cq]


def call(kernel, outs, scratch, flops, moved, *args, on_chip=False, leave=(), scalars=1):
    smem = pl.BlockSpec(memory_space=pltpu.SMEM)
    vmem = pl.BlockSpec(memory_space=pltpu.VMEM)
    if on_chip:
        held = [pltpu.with_memory_space_constraint(a, pltpu.VMEM) for a in args[scalars:]]
        args = (*args[:scalars], *held)
        outs = [
            o if n in leave else pltpu.VMEM(o.shape, o.dtype) for n, o in enumerate(outs)
        ]
    return pl.pallas_call(
        kernel,
        out_shape=outs,
        in_specs=[smem] * scalars + [vmem] * (len(args) - scalars),
        out_specs=[vmem] * len(outs),
        scratch_shapes=scratch,
        cost_estimate=pl.CostEstimate(flops=flops, bytes_accessed=moved, transcendentals=0),
        compiler_params=pltpu.CompilerParams(vmem_limit_bytes=CHIP_BYTES if on_chip else VMEM_BYTES),
    )(*args)


def arr(shape, dtype):
    return jax.ShapeDtypeStruct(shape, dtype)


def on_device(
    tokens, pair_of, gain_attn, w_query, key_weight, value_weight, w_out, gain_ffn,
    w_gate, w_up, w_down, cotangent,
):
    rows, width = tokens.shape[1:]
    blk = rows // 2
    shards, fsdp = lax.axis_size("ctx"), lax.axis_size("fsdp")
    feat, cq = w_query.shape
    ck, cg, ffr = key_weight.shape[1], w_gate.shape[1], w_down.shape[0]
    ff = cg * shards
    x, dy = tokens[0], cotangent[0]
    meta = jnp.concatenate(
        [pair_of[0], jnp.stack([lax.axis_index("ctx"), lax.axis_index("fsdp")]).astype(jnp.int32)]
    )

    def fill(parts, total):
        used = sum(p.shape[1] for p in parts)
        return parts + [jnp.zeros((parts[0].shape[0], total - used), BF16)]

    lanes = 256
    if cq % 8 == 0 and ck % 8 == 0:
        (own,) = call(
            pack_kernel, [pltpu.VMEM((feat + 8, lanes), BF16)], [pltpu.VMEM((feat + 8, lanes), F32)],
            0, 200_000,
            w_query, key_weight.T, value_weight.T, w_out, gain_attn[None], gain_ffn[None],
            scalars=0,
        )
    else:
        body = jnp.concatenate(
            fill([w_query, key_weight, value_weight], 128) + fill([w_out], 128), 1
        )
        gains_row = jnp.concatenate(fill([gain_attn[None]], 128) + fill([gain_ffn[None]], 128), 1)
        own = jnp.concatenate([body, jnp.broadcast_to(gains_row, (8, lanes))], 0)
    split = 80

    cgl = round_up(2 * cg, 128)
    gu_own = jnp.concatenate(fill([w_gate, w_up], cgl), 1)
    dt_own = w_down.T
    packed = cgl == ffr and cq % 8 == 0
    ffn_split = feat
    if packed:
        ffn = Gather(jnp.concatenate([gu_own, dt_own], 0), ffn_split, shards)
    else:
        gu_all = lax.all_gather(gu_own, ("ctx", "fsdp"), axis=0).reshape(shards, fsdp, feat, cgl)
        dt_all = lax.all_gather(dt_own, ("ctx", "fsdp"), axis=0).reshape(shards, fsdp, cq, ffr)
        ffn_in = (gu_all, dt_all.transpose(1, 0, 2, 3).reshape(fsdp, width, ffr))

    attn = Gather(own, split, shards)
    attn.outer()
    if packed:
        ffn.outer(*attn.a, *attn.b)
    attn.second()
    attn.third()
    if packed:
        attn_in = attn.cores(*ffn.a, *ffn.b)
        ffn.second()
    else:
        attn_in = attn.cores()

    my_pair = pair_of[0, lax.axis_index("ctx")]
    offsets = jnp.arange(blk, dtype=jnp.int32)
    pos = jnp.concatenate([my_pair * blk + offsets, (2 * shards - 1 - my_pair) * blk + offsets])
    freq = THETA ** (-jnp.arange(HEAD_DIM // 2, dtype=F32) * 2.0 / HEAD_DIM)
    angles = pos.astype(F32)[:, None] * freq[None, :]
    cos, sin = jnp.cos(angles), jnp.sin(angles)
    cos_t = jnp.concatenate([cos] * 4, 1)
    sin_t = jnp.concatenate([-sin, sin] * 2, 1)

    kvl = 2 * KEY_VALUE_HEADS * HEAD_DIM
    hrows = QUERY_HEADS * rows
    qp, kv, gains = call(
        functools.partial(qkv_kernel, (shards, fsdp, cq, ck, split, feat)),
        [
            arr((hrows, 128), BF16), arr((rows, kvl), BF16),
            arr((8, 1280), F32),
        ],
        [
            pltpu.VMEM((rows, 640), F32), pltpu.VMEM((rows, kvl), F32),
            pltpu.VMEM((rows, width), F32),
        ],
        2 * rows * width * 128 * shards, 6_000_000,
        meta, x, *attn_in, cos_t, sin_t, on_chip=packed,
    )

    kv_pieces = gather_outer(kv[None], shards)
    kv_near = join(kv_pieces)
    if packed:
        cut = kv_near.shape[0] * 3 // 4
        kv_far = [swap(kv_near[:cut], "ctx", 1), swap(kv_near[cut:], "ctx", 1)]
        ffn.third(kv_pieces[1])
        ffn_in = ffn.cores_apart(kv_far[0])
    else:
        kv_far = [swap(kv_near, "ctx", 1)]
    chunks = min(8, shards)
    span = GROUP * rows
    att, ot, lse = call(
        functools.partial(attend_kernel, (shards, chunks, blk)),
        [arr((rows, width), BF16), arr((KEY_VALUE_HEADS, 128, span), F32), arr((8, span), F32)],
        [pltpu.VMEM((8, span), F32), pltpu.VMEM((8, span), F32)],
        4 * hrows * shards * rows * 128, 3_000_000,
        meta, qp, kv_near, *kv_far, on_chip=packed,
    )

    glanes = cgl
    tiles = ffr // glanes
    parts = [arr((2 * shards, feat, glanes), BF16)] * 2
    parts += [arr((2 * shards, tiles * cq, glanes), BF16)] * 2
    out, *g_ffn, dmid, ggain, gp = call(
        functools.partial(
            ffn_kernel, (shards, fsdp, cq, cg, feat, ffr, ffn_split, feat, packed, split)
        ),
        [arr((width, rows), BF16), *parts]
        + [arr((rows, width), F32), arr((8, width), F32), arr((hrows, 128), BF16)],
        [
            pltpu.VMEM((shards, rows, cgl), F32), pltpu.VMEM((rows, ff), F32),
            pltpu.VMEM((rows, ff), F32), pltpu.VMEM((rows, cgl), F32), pltpu.VMEM((rows, 768), F32),
            pltpu.VMEM((rows, width), F32), pltpu.VMEM((fsdp, width, ffr), BF16),
        ],
        18 * rows * width * ff, 14_000_000,
        meta, att, x, dy.T, gains, *ffn_in, *(attn_in if packed else [p[:, :, 128:] for p in attn_in]),
        on_chip=packed, leave=(0,),
    )
    ffn_sum = Scatter(*g_ffn, shards)
    dq, dkv_near, dkv_far = call(
        functools.partial(attend_back_kernel, (shards, chunks, blk)),
        [arr((rows, width), BF16)] + [arr((shards // 2, rows, kvl), BF16)] * 2,
        [pltpu.VMEM((hrows, 128), F32)],
        10 * hrows * shards * rows * 128, 5_000_000,
        meta, qp, gp, ot, lse, cos_t, sin_t, kv_near, *kv_far, on_chip=packed,
    )
    dkv_got = []

    def send_far(*sent):
        dkv_got.append(swap(after(dkv_far, *sent), "ctx", 1))
        return dkv_got

    ffn_sum.second(late=send_far)
    dkv_terms = scatter_outer(add_low(dkv_near, dkv_got[0]), shards)
    ffn_sum.third()
    dkv = add_terms(dkv_terms, *ffn_sum.out)[0]

    grad_input, *g_attn = call(
        functools.partial(qkv_back_kernel, (shards, fsdp, cq, ck, split, feat)),
        [arr((width, rows), F32)]
        + [arr((2 * shards, split, lanes), BF16)] * 2
        + [arr((2 * shards, feat + 8 - split, lanes), BF16)] * 2,
        [
            pltpu.VMEM((rows, width), F32), pltpu.VMEM((rows, kvl), F32),
            pltpu.VMEM((rows, lanes), F32), pltpu.VMEM((rows, width), F32),
            pltpu.VMEM((8, width), F32),
        ],
        6 * rows * width * 256 * shards, 6_000_000,
        meta, x, dq, dkv, att, dmid, gains, ggain, cos_t, sin_t, *attn_in,
        on_chip=packed, leave=(0,),
    )
    attn_sum = Scatter(*g_attn, shards)
    attn_sum.second(ffn_sum.got_a, ffn_sum.got_b)
    ffn_sum.outer()
    attn_sum.third()
    attn_sum.outer()
    ffn_own = ffn_sum.total(attn_sum.last)
    if packed:
        gq, gkt, gvt, go, gain_a, gain_f = call(
            functools.partial(finish_kernel, ck),
            [arr((feat, cq), F32)] + [arr((ck, feat), F32)] * 2
            + [arr((feat, cq), F32)] + [arr((1, cq), F32)] * 2,
            [], 0, 400_000, *[t[0] for t in attn_sum.terms],
            on_chip=True, leave=range(6), scalars=0,
        )
        attn_grads = gq, gkt.T, gvt.T, go
        gain_grads = gain_a[0], gain_f[0]
    else:
        attn_own = attn_sum.total()
        attn_grads = (
            attn_own[:feat, :cq], attn_own[:feat, cq : cq + ck],
            attn_own[:feat, cq + ck : cq + 2 * ck], attn_own[:feat, 128 : 128 + cq],
        )
        gain_grads = attn_own[feat, :cq], attn_own[feat, 128 : 128 + cq]
    down_rows = ffn_own[feat:]
    grad_down = jnp.concatenate([down_rows[t * cq : (t + 1) * cq] for t in range(tiles)], 1).T
    return (
        out.T[None], grad_input.T[None], gain_grads[0], *attn_grads, gain_grads[1],
        ffn_own[:feat, :cg], ffn_own[:feat, cg : 2 * cg], grad_down,
    )


def solution(mesh):
    weights = (P("fsdp", "ctx"),) * 4
    data = P("fsdp", "ctx", None)
    in_specs = (
        (data, P("fsdp", None), P("ctx")) + weights + (P("ctx"),) + weights[:3] + (data,)
    )
    out_specs = (data, data, P("ctx")) + weights + (P("ctx"),) + weights[:3]
    return jax.shard_map(
        on_device, mesh=mesh, in_specs=in_specs, out_specs=out_specs, check_vma=False
    )
```

```python
import functools
import math

import jax
import jax.numpy as jnp
from jax import lax
from jax.experimental import pallas as pl
from jax.experimental.pallas import tpu as pltpu
from jax.sharding import PartitionSpec as P

QUERY_HEADS = 9
KEY_VALUE_HEADS = 3
HEAD_DIM = 64
GROUP = QUERY_HEADS // KEY_VALUE_HEADS

THETA = 100000.0
EPS = 1e-05
MASKED = -1e30
SCALE = 1.0 / math.sqrt(HEAD_DIM)
F32 = jnp.float32
BF16 = jnp.bfloat16
VMEM_BYTES = 56 * 1024 * 1024
CHIP_BYTES = 24 * 1024 * 1024

K_TILE, K_HALF = (0, 0, 1), (0, 1, 0)
V_TILE, V_HALF = (1, 2, 2), (1, 0, 1)


def round_up(n, m):
    return -(-n // m) * m


def swap(x, axis, mask):
    size = lax.axis_size(axis)
    return lax.ppermute(x, axis, [(i, i ^ mask) for i in range(size)])


def add_low(a, b):
    return (a.astype(F32) + b.astype(F32)).astype(BF16)


def outer_digits(shards):
    bits = list(range(1, shards.bit_length() - 1))
    return [tuple(bits[i : i + 2]) for i in range(0, len(bits), 2)]


def masks_of(digit):
    return [sum(1 << b for k, b in enumerate(digit) if n >> k & 1) for n in range(1 << len(digit))]


def join(pieces, *before):
    held = lax.optimization_barrier((*pieces, *before))[: len(pieces)]
    return jnp.concatenate(held, 0)


def gather_outer(x, shards):
    pieces = [x]
    for digit in outer_digits(shards):
        x = jnp.concatenate(pieces, 0)
        pieces = [x] + [swap(x, "ctx", m) for m in masks_of(digit)[1:]]
    return pieces


def scatter_outer(x, shards):
    for digit in outer_digits(shards)[::-1]:
        masks = masks_of(digit)
        parts = x.reshape((len(masks), -1) + x.shape[1:])
        terms = [parts[0]] + [swap(parts[n + 1], "ctx", m) for n, m in enumerate(masks[1:])]
        x = add_terms(terms).astype(BF16)
    return terms


def add_terms(terms, *before):
    held = lax.optimization_barrier((*terms, *before))[: len(terms)]
    return functools.reduce(lambda a, b: a + b, [t.astype(F32) for t in held])


def after(x, *before):
    return lax.optimization_barrier((x, *before))[0]


class Gather:
    def __init__(self, block, rows, shards):
        self.block, self.rows, self.shards = block, rows, shards

    def outer(self, *before):
        pieces = gather_outer(after(self.block[None], *before), self.shards)
        self.a = [p[:, : self.rows] for p in pieces]
        self.b = [p[:, self.rows :] for p in pieces]

    def phase(self, axis_a, mask_a, axis_b, mask_b, *before):
        a, b = join(self.a, *before), join(self.b, *before)
        self.now = a, b
        self.a, self.b = [a, swap(a, axis_a, mask_a)], [b, swap(b, axis_b, mask_b)]

    def second(self, *before):
        self.phase("ctx", 1, "fsdp", 2, *before)

    def third(self, *before):
        self.phase("fsdp", 2, "ctx", 1, *before)

    def cores_apart(self, *before):
        near, far = lax.optimization_barrier((*self.a, *before))[:2]
        b = join(self.b, *before)
        return near, far, swap(near, "fsdp", 1), swap(far, "fsdp", 1), b, swap(b, "fsdp", 1)

    def cores(self, *before):
        self.phase("fsdp", 1, "fsdp", 1, *before)
        return *self.a, *self.b


class Scatter:
    def __init__(self, keep_a, send_a, keep_b, send_b, shards, *before):
        self.a, self.b, self.shards = keep_a, keep_b, shards
        send_a, send_b = after(send_a, *before), after(send_b, *before)
        self.got_a, self.got_b = swap(send_a, "fsdp", 1), swap(send_b, "fsdp", 1)

    def fold(self, size, *before):
        a, b, got_a, got_b = lax.optimization_barrier(
            (self.a, self.b, self.got_a, self.got_b, *before)
        )[:4]
        self.a, self.b = add_low(a[:size], got_a[:size]), add_low(b[:size], got_b[:size])
        self.out = add_low(a[size:], got_a[size:]), add_low(b[size:], got_b[size:])
        return self.out

    def second(self, *before, late=None):
        a, b = self.fold(self.shards, *before)
        wait = () if late is None else late(a, b)
        self.got_a, self.got_b = swap(a, "fsdp", 2), swap(after(b, *wait), "ctx", 1)

    def third(self, *before):
        a, b = self.fold(self.shards // 2, *before)
        self.got_a, self.got_b = swap(a, "ctx", 1), swap(b, "fsdp", 2)

    def outer(self, *before):
        a, b, got_a, got_b = lax.optimization_barrier(
            (self.a, self.b, self.got_a, self.got_b, *before)
        )[:4]
        self.last = jnp.concatenate([add_low(a, got_a), add_low(b, got_b)], 1)
        self.terms = scatter_outer(self.last, self.shards)

    def total(self, *before):
        return add_terms(self.terms, *before)[0]


def ctx_place(mask, shards):
    return (mask >> 1) + (shards // 2) * (mask & 1)


def place_a(cm, x_bit, shards):
    return ctx_place(cm, shards) + shards * x_bit


def place_b(cm, x_bit, shards):
    return (cm >> 1) + (shards // 2) * x_bit + shards * (cm & 1)


def arrange(out_ref, value, mine, feat):
    for k in range(value.shape[1] // feat):

        @pl.when(mine == k)
        def _():
            for m in range(value.shape[1] // feat):
                out_ref[:, m * feat : (m + 1) * feat] = value[:, (m ^ k) * feat : ((m ^ k) + 1) * feat]


def chunk_rows(parts, c, mc, fsdp, split, feat, shards, lanes):
    pieces = []
    for m in range(fsdp):
        a_ref, b_ref = parts[m & 1], parts[2 + (m & 1)]
        pieces.append(a_ref[place_a(c ^ mc, m >> 1, shards), :, lanes])
        pieces.append(b_ref[place_b(c ^ mc, m >> 1, shards), : feat - split, lanes])
    return jnp.concatenate(pieces, 0)


def dot(a, b):
    return lax.dot_general(a, b, (((1,), (0,)), ((), ())), preferred_element_type=F32)


def dot_nt(a, b):
    return lax.dot_general(a, b, (((1,), (1,)), ((), ())), preferred_element_type=F32)


def dot_tn(a, b):
    return lax.dot_general(a, b, (((0,), (0,)), ((), ())), preferred_element_type=F32)


def lane_ids():
    return lax.broadcasted_iota(jnp.int32, (1, 128), 1)


def turned(u):
    lane = lane_ids()
    first = (lane & (HEAD_DIM - 1)) < HEAD_DIM // 2
    return jnp.where(first, pltpu.roll(u, 96, 1), pltpu.roll(u, 32, 1))


def to_half(tile, source, target):
    return tile if source == target else pltpu.roll(tile, 64, 1)


def only_half(tile, half):
    lane = lane_ids()
    keep = lane >= 64 if half else lane < 64
    return jnp.where(keep, tile, 0.0)


def head_rows(h):
    return slice(h * 128, (h + 1) * 128)


def qkv_kernel(
    dims, meta, x_ref, ao_ref, as_ref, bo_ref, bs_ref, cos_ref, sin_ref,
    qp_ref, kv_ref, gain_ref, q_s, kv_s, n_s,
):
    shards, fsdp, cq, ck, split, feat = dims
    mc, mf = meta[shards], meta[shards + 1]
    parts = ao_ref, as_ref, bo_ref, bs_ref
    kvw = KEY_VALUE_HEADS * HEAD_DIM
    for c in range(shards):
        row = bo_ref[place_b(c ^ mc, 0, shards)][feat - split :, :].astype(F32)
        gain_ref[:, c * cq : (c + 1) * cq] = row[:, :cq]
        gain_ref[:, 640 + c * cq : 640 + (c + 1) * cq] = row[:, 128 : 128 + cq]
    x = x_ref[...].astype(F32)
    width = x.shape[1]
    rr = lax.rsqrt(jnp.mean(x * x, axis=-1, keepdims=True) + EPS)
    arrange(n_s, x * rr * gain_ref[0:1, :width], mf, feat)
    normed = n_s[...].astype(BF16)
    for c in range(shards):
        w = chunk_rows(parts, c, mc, fsdp, split, feat, shards, slice(0, 128))
        y = dot(normed, w)
        q_s[:, c * cq : (c + 1) * cq] = y[:, :cq]
        kv_s[:, c * ck : (c + 1) * ck] = y[:, cq : cq + ck]
        kv_s[:, kvw + c * ck : kvw + (c + 1) * ck] = y[:, cq + ck : cq + 2 * ck]
    cos, sin = cos_ref[...], sin_ref[...]
    for t in range(5):
        u = q_s[:, t * 128 : (t + 1) * 128]
        u = u * cos + turned(u) * sin
        for h in (2 * t, 2 * t + 1):
            if h < QUERY_HEADS:
                half = K_HALF[h // GROUP]
                qp_ref[head_rows(h), :] = only_half(to_half(u, h % 2, half), half).astype(BF16)
    for t in range(3):
        u = kv_s[:, t * 128 : (t + 1) * 128]
        if t < 2:
            r = u * cos + turned(u) * sin
            u = r if t == 0 else jnp.where(lane_ids() < 64, r, u)
        kv_ref[:, t * 128 : (t + 1) * 128] = u.astype(BF16)


def score_mask(meta, shards, block, chunks, blk):
    mc = meta[shards]
    mine = meta[mc]
    r = lax.broadcasted_iota(jnp.int32, (blk, GROUP * 2 * blk), 1) & (2 * blk - 1)
    qpos = jnp.where(r < blk, mine * blk + r, (2 * shards - 1 - mine) * blk + r - blk)
    gap = qpos - lax.broadcasted_iota(jnp.int32, qpos.shape, 0)
    out = []
    for i in range(chunks):
        pair = meta[mc ^ (2 * (block * (chunks // 2) + i % (chunks // 2)) + i // (chunks // 2))]
        out.append(gap >= pair * blk)
        out.append(gap >= (2 * shards - 1 - pair) * blk)
    return out


def block_rows(refs, block, chunks, blocks):
    if blocks == 1:
        values = [r[...] for r in refs]
    else:
        values = [r[pl.ds(block * (chunks // 2), chunks // 2)] for r in refs]
    return jnp.concatenate([v.reshape(-1, v.shape[2]) for v in values], 0)


def masked(s, mask, blk):
    return jnp.concatenate(
        [jnp.where(m, s[i * blk : (i + 1) * blk], MASKED) for i, m in enumerate(mask)], 0
    )


def attend_kernel(dims, meta, qp_ref, *refs):
    *kv_refs, att_ref, ot_ref, lse_ref, m_s, l_s = refs
    shards, chunks, blk = dims
    blocks = shards // chunks
    rows = chunks * 2 * blk
    span = GROUP * 2 * blk

    def block_step(b, first):
        mask = score_mask(meta, shards, b, chunks, blk)
        kv = block_rows(kv_refs, b, chunks, blocks)
        for g in range(KEY_VALUE_HEADS):
            keys = kv[:, K_TILE[g] * 128 : (K_TILE[g] + 1) * 128]
            vals = kv[:, V_TILE[g] * 128 : (V_TILE[g] + 1) * 128]
            s = masked(dot_nt(keys, qp_ref[g * span : (g + 1) * span, :]) * SCALE, mask, blk)
            top = jnp.max(s, axis=0, keepdims=True)
            if not first:
                top = jnp.maximum(top, m_s[g : g + 1, :])
            p = jnp.exp(s - top)
            total = jnp.sum(p, axis=0, keepdims=True)
            out = dot_tn(vals, p.astype(BF16))
            if not first:
                fade = jnp.exp(m_s[g : g + 1, :] - top)
                total = total + l_s[g : g + 1, :] * fade
                out = out + ot_ref[g] * fade
            m_s[g : g + 1, :] = top
            l_s[g : g + 1, :] = total
            ot_ref[g] = out

    block_step(0, True)
    if blocks > 1:

        @pl.loop(1, blocks)
        def _(b):
            block_step(b, False)

    tiles = {}
    for g in range(KEY_VALUE_HEADS):
        o = ot_ref[g] / l_s[g : g + 1, :]
        ot_ref[g] = o
        lse_ref[g : g + 1, :] = m_s[g : g + 1, :] + jnp.log(l_s[g : g + 1, :])
        for j in range(GROUP):
            h = g * GROUP + j
            tile = jnp.transpose(o[:, j * 128 : (j + 1) * 128])
            tiles[h] = to_half(tile, V_HALF[g], h % 2)
    for t in range(5):
        if 2 * t + 1 < QUERY_HEADS:
            tile = jnp.where(lane_ids() < 64, tiles[2 * t], tiles[2 * t + 1])
            att_ref[:, t * 128 : (t + 1) * 128] = tile.astype(BF16)
        else:
            att_ref[:, t * 128 : t * 128 + 64] = tiles[2 * t][:, :64].astype(BF16)


def ffn_kernel(
    dims, meta, att_ref, x_ref, dy_ref, gain_ref, *refs
):
    shards, fsdp, cq, cg, feat, ffr, fsplit, split, packed, asplit = dims
    ins, refs = (refs[:6], refs[6:]) if packed else (refs[:2], refs[2:])
    parts, refs = refs[:4], refs[4:]
    (
        out_ref, ak_ref, as_ref, bk_ref, bs_ref, dmid_ref, ggain_ref, gp_ref,
        gu_s, hid_s, dh_s, dgu_s, wide_s, p_s, dt_s,
    ) = refs
    mc, mf = meta[shards], meta[shards + 1]
    lanes = ak_ref.shape[2]
    if packed:
        for c in range(0, shards, 2):
            for m in range(fsdp):
                b_ref = ins[4 + (m & 1)]
                pair = [b_ref[place_b(d ^ mc, m >> 1, shards)][feat - fsplit :] for d in (c, c + 1)]
                dt_s[m, c * cq : (c + 2) * cq, :] = jnp.concatenate(
                    [p.astype(F32) for p in pair], 0
                ).astype(BF16)
    else:
        for m in range(fsdp):
            dt_s[m] = ins[1][mf ^ m]

    def weights(c):
        if packed:
            pieces = []
            for m in range(fsdp):
                pieces.append(ins[2 * (m & 1) + (m >> 1)][ctx_place(c ^ mc, shards)])
                if fsplit < feat:
                    b_ref = ins[4 + (m & 1)]
                    pieces.append(b_ref[place_b(c ^ mc, m >> 1, shards), : feat - fsplit, :])
            return jnp.concatenate(pieces, 0)
        return jnp.concatenate([ins[0][c, mf ^ m] for m in range(fsdp)], 0)

    def outer(c):
        return chunk_rows(parts, c, mc, fsdp, asplit, feat, shards, slice(-128, None))

    x = x_ref[...].astype(F32)
    width = x.shape[1]
    dy_t = dy_ref[...]
    dyf = jnp.transpose(dy_t.astype(F32))
    dyl = dyf.astype(BF16)
    gain = gain_ref[0:1, 640 : 640 + width]
    arrange(p_s, att_ref[...].astype(F32), mf, feat)
    attp = p_s[...].astype(BF16)
    for c in range(shards):
        wide_s[:, c * cq : (c + 1) * cq] = dot(attp, outer(c))[:, :cq]
    mid = x + wide_s[:, :width]
    rr = lax.rsqrt(jnp.mean(mid * mid, axis=-1, keepdims=True) + EPS)
    z = mid * rr
    arrange(p_s, z * gain, mf, feat)
    normed = p_s[...].astype(BF16)
    normed_t = jnp.transpose(p_s[...]).astype(BF16)

    def store_grad(c, m, row, value):
        end = row + value.shape[0]
        here = slice(0, value.shape[1])
        if row < split:
            stop = min(end, split)
            ref = (ak_ref, as_ref)[m & 1]
            ref[place_a(c ^ mc, m >> 1, shards), row:stop, here] = value[: stop - row]
        if end > split:
            start = max(row, split)
            ref = (bk_ref, bs_ref)[m & 1]
            ref[place_b(c ^ mc, m >> 1, shards), start - split : end - split, here] = value[start - row :]

    for c in range(shards):
        gu = dot(normed, weights(c))
        gu_s[c] = gu
        gate, up = gu[:, :cg], gu[:, cg : 2 * cg]
        hid_s[:, c * cg : (c + 1) * cg] = gate * jax.nn.sigmoid(gate) * up
    out = mid
    for m in range(fsdp):
        here = pl.ds(pl.multiple_of((mf ^ m) * ffr, 128), ffr)
        hid = hid_s[:, here].astype(BF16)
        out = out + dot_nt(hid, dt_s[m])
        dh_s[:, here] = dot(dyl, dt_s[m])
        g = dot(dy_t, hid)
        for c in range(shards):
            piece = g[c * cq : (c + 1) * cq, :].astype(BF16)
            for t in range(ffr // lanes):
                store_grad(c, m, feat + t * cq, piece[:, t * lanes : (t + 1) * lanes])
    out_ref[...] = jnp.transpose(out).astype(BF16)
    dn = jnp.zeros_like(mid)
    for c in range(shards):
        gu = gu_s[c]
        gate, up = gu[:, :cg], gu[:, cg : 2 * cg]
        dh = dh_s[:, c * cg : (c + 1) * cg]
        sg = jax.nn.sigmoid(gate)
        if 2 * cg < dgu_s.shape[1]:
            dgu_s[...] = jnp.zeros_like(dgu_s)
        dgu_s[:, :cg] = dh * up * sg * (1.0 + gate * (1.0 - sg))
        dgu_s[:, cg : 2 * cg] = dh * gate * sg
        dgu = dgu_s[...].astype(BF16)
        g = dot(normed_t, dgu)
        for m in range(fsdp):
            store_grad(c, m, 0, g[m * feat : (m + 1) * feat, :].astype(BF16))
        dn = dn + dot_nt(dgu, weights(c))
    arrange(p_s, dn, mf, feat)
    dn = p_s[...]
    e = dn * gain
    dmid = dyf + rr * (e - z * jnp.mean(e * z, axis=-1, keepdims=True))
    dmid_ref[...] = dmid
    ggain_ref[...] = jnp.broadcast_to(jnp.sum(dn * z, axis=0, keepdims=True), ggain_ref.shape)
    wide_s[...] = jnp.zeros_like(wide_s)
    wide_s[:, :width] = dmid
    ga = jnp.zeros_like(mid)
    for c in range(shards):
        gb = wide_s[:, c * cq : c * cq + 128].astype(BF16)
        ga = ga + dot_nt(gb, outer(c))
    arrange(p_s, ga, mf, feat)
    wide_s[:, :width] = p_s[...]
    for h in range(QUERY_HEADS):
        half = V_HALF[h // GROUP]
        tile = wide_s[:, (h // 2) * 128 : (h // 2 + 1) * 128]
        gp_ref[head_rows(h), :] = only_half(to_half(tile, h % 2, half), half).astype(BF16)


def attend_back_kernel(
    dims, meta, qp_ref, gp_ref, ot_ref, lse_ref, cos_ref, sin_ref, *refs
):
    *kv_refs, dq_ref, dnear_ref, dfar_ref, dq_s = refs
    shards, chunks, blk = dims
    blocks = shards // chunks
    rows = chunks * 2 * blk
    span = GROUP * 2 * blk
    deltas = []
    for g in range(KEY_VALUE_HEADS):
        gt = jnp.transpose(gp_ref[g * span : (g + 1) * span, :].astype(F32))
        deltas.append(jnp.sum(gt * ot_ref[g], axis=0, keepdims=True))

    def block_step(b, first):
        mask = score_mask(meta, shards, b, chunks, blk)
        kv = block_rows(kv_refs, b, chunks, blocks)
        tiles = [None, None, None]

        def put(t, value):
            tiles[t] = value if tiles[t] is None else tiles[t] + value

        for g in range(KEY_VALUE_HEADS):
            keys = kv[:, K_TILE[g] * 128 : (K_TILE[g] + 1) * 128]
            vals = kv[:, V_TILE[g] * 128 : (V_TILE[g] + 1) * 128]
            qg = qp_ref[g * span : (g + 1) * span, :]
            gg = gp_ref[g * span : (g + 1) * span, :]
            s = masked(dot_nt(keys, qg) * SCALE, mask, blk)
            p = jnp.exp(s - lse_ref[g : g + 1, :])
            ds = (p * (dot_nt(vals, gg) - deltas[g]) * SCALE).astype(BF16)
            put(V_TILE[g], dot(p.astype(BF16), gg))
            put(K_TILE[g], dot(ds, qg))
            dq = dot_tn(ds, keys)
            if first:
                dq_s[g * span : (g + 1) * span, :] = dq
            else:
                dq_s[g * span : (g + 1) * span, :] += dq
        for t in range(3):
            tile = tiles[t].astype(BF16).reshape(2, chunks // 2, 2 * blk, 128)
            for n, ref in enumerate((dnear_ref, dfar_ref)):
                ref[pl.ds(b * (chunks // 2), chunks // 2), :, t * 128 : (t + 1) * 128] = tile[n]

    block_step(0, True)
    if blocks > 1:

        @pl.loop(1, blocks)
        def _(b):
            block_step(b, False)

    cos, sin = cos_ref[...], sin_ref[...]
    tiles = {}
    for h in range(QUERY_HEADS):
        u = dq_s[head_rows(h), :]
        tiles[h] = to_half(u * cos - turned(u) * sin, K_HALF[h // GROUP], h % 2)
    for t in range(5):
        if 2 * t + 1 < QUERY_HEADS:
            tile = jnp.where(lane_ids() < 64, tiles[2 * t], tiles[2 * t + 1])
            dq_ref[:, t * 128 : (t + 1) * 128] = tile.astype(BF16)
        else:
            dq_ref[:, t * 128 : t * 128 + 64] = tiles[2 * t][:, :64].astype(BF16)


def qkv_back_kernel(
    dims, meta, x_ref, dq_ref, dkv_ref, att_ref, dmid_ref, gain_ref, gg_ref,
    cos_ref, sin_ref, ao_ref, as_in, bo_ref, bs_in, gin_ref, ak_ref, as_ref, bk_ref, bs_ref,
    dq_s, dkv_s, d_s, p_s, gg_s,
):
    shards, fsdp, cq, ck, split, feat = dims
    mc, mf = meta[shards], meta[shards + 1]
    parts = ao_ref, as_in, bo_ref, bs_in
    kvw = KEY_VALUE_HEADS * HEAD_DIM
    x = x_ref[...].astype(F32)
    width = x.shape[1]
    gain = gain_ref[0:1, :width]
    rr = lax.rsqrt(jnp.mean(x * x, axis=-1, keepdims=True) + EPS)
    z = x * rr
    arrange(p_s, z * gain, mf, feat)
    normed_t = jnp.transpose(p_s[...]).astype(BF16)
    arrange(p_s, att_ref[...].astype(F32), mf, feat)
    att_t = jnp.transpose(p_s[...]).astype(BF16)
    cos, sin = cos_ref[...], sin_ref[...]
    for t in range(3):
        u = dkv_ref[:, t * 128 : (t + 1) * 128]
        if t < 2:
            r = u * cos - turned(u) * sin
            u = r if t == 0 else jnp.where(lane_ids() < 64, r, u)
        dkv_s[:, t * 128 : (t + 1) * 128] = u
    dq_s[...] = dq_ref[...].astype(F32)
    d_s[...] = jnp.zeros_like(d_s)
    dn = jnp.zeros_like(x)
    for c in range(shards):
        d_s[:, :cq] = dq_s[:, c * cq : (c + 1) * cq]
        d_s[:, cq : cq + ck] = dkv_s[:, c * ck : (c + 1) * ck]
        d_s[:, cq + ck : cq + 2 * ck] = dkv_s[:, kvw + c * ck : kvw + (c + 1) * ck]
        d_s[:, 128 : 128 + cq] = dmid_ref[:, c * cq : (c + 1) * cq]
        d = d_s[...].astype(BF16)
        w = chunk_rows(parts, c, mc, fsdp, split, feat, shards, slice(0, 128))
        dn = dn + dot_nt(d[:, :128], w)
        g = jnp.concatenate([dot(normed_t, d[:, :128]), dot(att_t, d[:, 128:])], 1).astype(BF16)
        for m in range(fsdp):
            part = g[m * feat : (m + 1) * feat, :]
            (ak_ref, as_ref)[m & 1][place_a(c ^ mc, m >> 1, shards)] = part[:split]
            (bk_ref, bs_ref)[m & 1][place_b(c ^ mc, m >> 1, shards), : feat - split] = part[split:]
    arrange(p_s, dn, mf, feat)
    dn = p_s[...]
    e = dn * gain
    gin = dmid_ref[...] + rr * (e - z * jnp.mean(e * z, axis=-1, keepdims=True))
    gin_ref[...] = jnp.transpose(gin)
    gg_s[...] = jnp.broadcast_to(jnp.sum(dn * z, axis=0, keepdims=True), gg_s.shape)
    for c in range(shards):
        d_s[0:8, 0:cq] = gg_s[:, c * cq : (c + 1) * cq]
        d_s[0:8, 128 : 128 + cq] = gg_ref[:, c * cq : (c + 1) * cq]
        gains = d_s[0:8, :].astype(BF16)
        for m in range(fsdp):
            (bk_ref, bs_ref)[m & 1][place_b(c ^ mc, m >> 1, shards), feat - split :] = gains


def pack_kernel(wq_ref, wkt_ref, wvt_ref, wo_ref, ga_ref, gf_ref, own_ref, t_s):
    feat, cq = wq_ref.shape
    ck = wkt_ref.shape[0]
    t_s[...] = jnp.zeros_like(t_s)
    t_s[:feat, :cq] = wq_ref[...].astype(F32)
    t_s[:feat, cq : cq + ck] = jnp.transpose(wkt_ref[...].astype(F32))
    t_s[:feat, cq + ck : cq + 2 * ck] = jnp.transpose(wvt_ref[...].astype(F32))
    t_s[:feat, 128 : 128 + cq] = wo_ref[...].astype(F32)
    t_s[feat : feat + 1, :cq] = ga_ref[...].astype(F32)
    t_s[feat : feat + 1, 128 : 128 + cq] = gf_ref[...].astype(F32)
    own_ref[...] = t_s[...].astype(BF16)


def finish_kernel(ck, *refs):
    *terms, gq_ref, gkt_ref, gvt_ref, go_ref, ga_ref, gf_ref = refs
    feat, cq = gq_ref.shape
    total = functools.reduce(lambda a, b: a + b, [t[...].astype(F32) for t in terms])
    gq_ref[...] = total[:feat, :cq]
    turned_round = jnp.transpose(total[:feat, :128])
    gkt_ref[...] = turned_round[cq : cq + ck]
    gvt_ref[...] = turned_round[cq + ck : cq + 2 * ck]
    go_ref[...] = total[:feat, 128 : 128 + cq]
    ga_ref[...] = total[feat : feat + 1, :cq]
    gf_ref[...] = total[feat : feat + 1, 128 : 128 + cq]


def call(kernel, outs, scratch, flops, moved, *args, on_chip=False, leave=(), scalars=1):
    smem = pl.BlockSpec(memory_space=pltpu.SMEM)
    vmem = pl.BlockSpec(memory_space=pltpu.VMEM)
    if on_chip:
        held = [pltpu.with_memory_space_constraint(a, pltpu.VMEM) for a in args[scalars:]]
        args = (*args[:scalars], *held)
        outs = [
            o if n in leave else pltpu.VMEM(o.shape, o.dtype) for n, o in enumerate(outs)
        ]
    return pl.pallas_call(
        kernel,
        out_shape=outs,
        in_specs=[smem] * scalars + [vmem] * (len(args) - scalars),
        out_specs=[vmem] * len(outs),
        scratch_shapes=scratch,
        cost_estimate=pl.CostEstimate(flops=flops, bytes_accessed=moved, transcendentals=0),
        compiler_params=pltpu.CompilerParams(vmem_limit_bytes=CHIP_BYTES if on_chip else VMEM_BYTES),
    )(*args)


def arr(shape, dtype):
    return jax.ShapeDtypeStruct(shape, dtype)


def on_device(
    tokens, pair_of, gain_attn, w_query, key_weight, value_weight, w_out, gain_ffn,
    w_gate, w_up, w_down, cotangent,
):
    rows, width = tokens.shape[1:]
    blk = rows // 2
    shards, fsdp = lax.axis_size("ctx"), lax.axis_size("fsdp")
    feat, cq = w_query.shape
    ck, cg, ffr = key_weight.shape[1], w_gate.shape[1], w_down.shape[0]
    ff = cg * shards
    x, dy = tokens[0], cotangent[0]
    meta = jnp.concatenate(
        [pair_of[0], jnp.stack([lax.axis_index("ctx"), lax.axis_index("fsdp")]).astype(jnp.int32)]
    )

    def fill(parts, total):
        used = sum(p.shape[1] for p in parts)
        return parts + [jnp.zeros((parts[0].shape[0], total - used), BF16)]

    lanes = 256
    if cq % 8 == 0 and ck % 8 == 0:
        (own,) = call(
            pack_kernel, [pltpu.VMEM((feat + 8, lanes), BF16)], [pltpu.VMEM((feat + 8, lanes), F32)],
            0, 200_000,
            w_query, key_weight.T, value_weight.T, w_out, gain_attn[None], gain_ffn[None],
            scalars=0,
        )
    else:
        body = jnp.concatenate(
            fill([w_query, key_weight, value_weight], 128) + fill([w_out], 128), 1
        )
        gains_row = jnp.concatenate(fill([gain_attn[None]], 128) + fill([gain_ffn[None]], 128), 1)
        own = jnp.concatenate([body, jnp.broadcast_to(gains_row, (8, lanes))], 0)
    split = 80

    cgl = round_up(2 * cg, 128)
    gu_own = jnp.concatenate(fill([w_gate, w_up], cgl), 1)
    dt_own = w_down.T
    packed = cgl == ffr and cq % 8 == 0
    ffn_split = feat
    if packed:
        ffn = Gather(jnp.concatenate([gu_own, dt_own], 0), ffn_split, shards)
    else:
        gu_all = lax.all_gather(gu_own, ("ctx", "fsdp"), axis=0).reshape(shards, fsdp, feat, cgl)
        dt_all = lax.all_gather(dt_own, ("ctx", "fsdp"), axis=0).reshape(shards, fsdp, cq, ffr)
        ffn_in = (gu_all, dt_all.transpose(1, 0, 2, 3).reshape(fsdp, width, ffr))

    attn = Gather(own, split, shards)
    attn.outer()
    attn.second()
    if packed:
        ffn.outer(*attn.now)
    attn.third()
    if packed:
        attn_in = attn.cores(ffn.a[3], ffn.b[3])
        ffn.second()
    else:
        attn_in = attn.cores()

    my_pair = pair_of[0, lax.axis_index("ctx")]
    offsets = jnp.arange(blk, dtype=jnp.int32)
    pos = jnp.concatenate([my_pair * blk + offsets, (2 * shards - 1 - my_pair) * blk + offsets])
    freq = THETA ** (-jnp.arange(HEAD_DIM // 2, dtype=F32) * 2.0 / HEAD_DIM)
    angles = pos.astype(F32)[:, None] * freq[None, :]
    cos, sin = jnp.cos(angles), jnp.sin(angles)
    cos_t = jnp.concatenate([cos] * 4, 1)
    sin_t = jnp.concatenate([-sin, sin] * 2, 1)

    kvl = 2 * KEY_VALUE_HEADS * HEAD_DIM
    hrows = QUERY_HEADS * rows
    qp, kv, gains = call(
        functools.partial(qkv_kernel, (shards, fsdp, cq, ck, split, feat)),
        [
            arr((hrows, 128), BF16), arr((rows, kvl), BF16),
            arr((8, 1280), F32),
        ],
        [
            pltpu.VMEM((rows, 640), F32), pltpu.VMEM((rows, kvl), F32),
            pltpu.VMEM((rows, width), F32),
        ],
        2 * rows * width * 128 * shards, 6_000_000,
        meta, x, *attn_in, cos_t, sin_t, on_chip=packed,
    )

    kv_pieces = gather_outer(kv[None], shards)
    kv_near = join(kv_pieces)
    if packed:
        cut = kv_near.shape[0] * 3 // 4
        kv_far = [swap(kv_near[:cut], "ctx", 1), swap(kv_near[cut:], "ctx", 1)]
        ffn.third(kv_pieces[1])
        ffn_in = ffn.cores_apart(kv_far[0])
    else:
        kv_far = [swap(kv_near, "ctx", 1)]
    chunks = min(8, shards)
    span = GROUP * rows
    att, ot, lse = call(
        functools.partial(attend_kernel, (shards, chunks, blk)),
        [arr((rows, width), BF16), arr((KEY_VALUE_HEADS, 128, span), F32), arr((8, span), F32)],
        [pltpu.VMEM((8, span), F32), pltpu.VMEM((8, span), F32)],
        4 * hrows * shards * rows * 128, 3_000_000,
        meta, qp, kv_near, *kv_far, on_chip=packed,
    )

    glanes = cgl
    tiles = ffr // glanes
    parts = [arr((2 * shards, feat, glanes), BF16)] * 2
    parts += [arr((2 * shards, tiles * cq, glanes), BF16)] * 2
    out, *g_ffn, dmid, ggain, gp = call(
        functools.partial(
            ffn_kernel, (shards, fsdp, cq, cg, feat, ffr, ffn_split, feat, packed, split)
        ),
        [arr((width, rows), BF16), *parts]
        + [arr((rows, width), F32), arr((8, width), F32), arr((hrows, 128), BF16)],
        [
            pltpu.VMEM((shards, rows, cgl), F32), pltpu.VMEM((rows, ff), F32),
            pltpu.VMEM((rows, ff), F32), pltpu.VMEM((rows, cgl), F32), pltpu.VMEM((rows, 768), F32),
            pltpu.VMEM((rows, width), F32), pltpu.VMEM((fsdp, width, ffr), BF16),
        ],
        18 * rows * width * ff, 14_000_000,
        meta, att, x, dy.T, gains, *ffn_in, *(attn_in if packed else [p[:, :, 128:] for p in attn_in]),
        on_chip=packed, leave=(0,),
    )
    ffn_sum = Scatter(*g_ffn, shards)
    dq, dkv_near, dkv_far = call(
        functools.partial(attend_back_kernel, (shards, chunks, blk)),
        [arr((rows, width), BF16)] + [arr((shards // 2, rows, kvl), BF16)] * 2,
        [pltpu.VMEM((hrows, 128), F32)],
        10 * hrows * shards * rows * 128, 5_000_000,
        meta, qp, gp, ot, lse, cos_t, sin_t, kv_near, *kv_far, on_chip=packed,
    )
    dkv_got = []

    def send_far(*sent):
        dkv_got.append(swap(after(dkv_far, *sent), "ctx", 1))
        return dkv_got

    ffn_sum.second(late=send_far)
    dkv_terms = scatter_outer(add_low(dkv_near, dkv_got[0]), shards)
    ffn_sum.third()
    dkv = add_terms(dkv_terms, *ffn_sum.out)[0]

    grad_input, *g_attn = call(
        functools.partial(qkv_back_kernel, (shards, fsdp, cq, ck, split, feat)),
        [arr((width, rows), F32)]
        + [arr((2 * shards, split, lanes), BF16)] * 2
        + [arr((2 * shards, feat + 8 - split, lanes), BF16)] * 2,
        [
            pltpu.VMEM((rows, width), F32), pltpu.VMEM((rows, kvl), F32),
            pltpu.VMEM((rows, lanes), F32), pltpu.VMEM((rows, width), F32),
            pltpu.VMEM((8, width), F32),
        ],
        6 * rows * width * 256 * shards, 6_000_000,
        meta, x, dq, dkv, att, dmid, gains, ggain, cos_t, sin_t, *attn_in,
        on_chip=packed, leave=(0,),
    )
    attn_sum = Scatter(*g_attn, shards)
    attn_sum.second(ffn_sum.got_a, ffn_sum.got_b)
    ffn_sum.outer()
    attn_sum.third()
    attn_sum.outer()
    ffn_own = ffn_sum.total(attn_sum.last)
    if packed:
        gq, gkt, gvt, go, gain_a, gain_f = call(
            functools.partial(finish_kernel, ck),
            [arr((feat, cq), F32)] + [arr((ck, feat), F32)] * 2
            + [arr((feat, cq), F32)] + [arr((1, cq), F32)] * 2,
            [], 0, 400_000, *[t[0] for t in attn_sum.terms],
            on_chip=True, leave=range(6), scalars=0,
        )
        attn_grads = gq, gkt.T, gvt.T, go
        gain_grads = gain_a[0], gain_f[0]
    else:
        attn_own = attn_sum.total()
        attn_grads = (
            attn_own[:feat, :cq], attn_own[:feat, cq : cq + ck],
            attn_own[:feat, cq + ck : cq + 2 * ck], attn_own[:feat, 128 : 128 + cq],
        )
        gain_grads = attn_own[feat, :cq], attn_own[feat, 128 : 128 + cq]
    down_rows = ffn_own[feat:]
    grad_down = jnp.concatenate([down_rows[t * cq : (t + 1) * cq] for t in range(tiles)], 1).T
    return (
        out.T[None], grad_input.T[None], gain_grads[0], *attn_grads, gain_grads[1],
        ffn_own[:feat, :cg], ffn_own[:feat, cg : 2 * cg], grad_down,
    )


def solution(mesh):
    weights = (P("fsdp", "ctx"),) * 4
    data = P("fsdp", "ctx", None)
    in_specs = (
        (data, P("fsdp", None), P("ctx")) + weights + (P("ctx"),) + weights[:3] + (data,)
    )
    out_specs = (data, data, P("ctx")) + weights + (P("ctx"),) + weights[:3]
    return jax.shard_map(
        on_device, mesh=mesh, in_specs=in_specs, out_specs=out_specs, check_vma=False
    )
```

```python
import functools
import math

import jax
import jax.numpy as jnp
from jax import lax
from jax.experimental import pallas as pl
from jax.experimental.pallas import tpu as pltpu
from jax.sharding import PartitionSpec as P

QUERY_HEADS = 9
KEY_VALUE_HEADS = 3
HEAD_DIM = 64
GROUP = QUERY_HEADS // KEY_VALUE_HEADS

THETA = 100000.0
EPS = 1e-05
MASKED = -1e30
SCALE = 1.0 / math.sqrt(HEAD_DIM)
F32 = jnp.float32
BF16 = jnp.bfloat16
VMEM_BYTES = 56 * 1024 * 1024
CHIP_BYTES = 24 * 1024 * 1024

K_TILE, K_HALF = (0, 0, 1), (0, 1, 0)
V_TILE, V_HALF = (1, 2, 2), (1, 0, 1)


def round_up(n, m):
    return -(-n // m) * m


def swap(x, axis, mask):
    size = lax.axis_size(axis)
    return lax.ppermute(x, axis, [(i, i ^ mask) for i in range(size)])


def add_low(a, b):
    return (a.astype(F32) + b.astype(F32)).astype(BF16)


def outer_digits(shards):
    bits = list(range(1, shards.bit_length() - 1))
    return [tuple(bits[i : i + 2]) for i in range(0, len(bits), 2)]


def masks_of(digit):
    return [sum(1 << b for k, b in enumerate(digit) if n >> k & 1) for n in range(1 << len(digit))]


def join(pieces, *before):
    held = lax.optimization_barrier((*pieces, *before))[: len(pieces)]
    return jnp.concatenate(held, 0)


def gather_outer(x, shards):
    pieces = [x]
    for digit in outer_digits(shards):
        x = jnp.concatenate(pieces, 0)
        pieces = [x] + [swap(x, "ctx", m) for m in masks_of(digit)[1:]]
    return pieces


def scatter_outer(x, shards):
    for digit in outer_digits(shards)[::-1]:
        masks = masks_of(digit)
        parts = x.reshape((len(masks), -1) + x.shape[1:])
        terms = [parts[0]] + [swap(parts[n + 1], "ctx", m) for n, m in enumerate(masks[1:])]
        x = add_terms(terms).astype(BF16)
    return terms


def add_terms(terms, *before):
    held = lax.optimization_barrier((*terms, *before))[: len(terms)]
    return functools.reduce(lambda a, b: a + b, [t.astype(F32) for t in held])


def after(x, *before):
    return lax.optimization_barrier((x, *before))[0]


class Gather:
    def __init__(self, block, rows, shards):
        self.block, self.rows, self.shards = block, rows, shards

    def outer(self, *before):
        pieces = gather_outer(after(self.block[None], *before), self.shards)
        self.a = [p[:, : self.rows] for p in pieces]
        self.b = [p[:, self.rows :] for p in pieces]

    def phase(self, axis_a, mask_a, axis_b, mask_b, *before):
        a, b = join(self.a, *before), join(self.b, *before)
        self.now = a, b
        self.a, self.b = [a, swap(a, axis_a, mask_a)], [b, swap(b, axis_b, mask_b)]

    def second(self, *before):
        self.phase("ctx", 1, "fsdp", 2, *before)

    def third(self, *before):
        self.phase("fsdp", 2, "ctx", 1, *before)

    def cores_apart(self, *before):
        near, far = lax.optimization_barrier((*self.a, *before))[:2]
        b = join(self.b, *before)
        return near, far, swap(near, "fsdp", 1), swap(far, "fsdp", 1), b, swap(b, "fsdp", 1)

    def cores(self, *before):
        self.phase("fsdp", 1, "fsdp", 1, *before)
        return *self.a, *self.b


class Scatter:
    def __init__(self, keep_a, send_a, keep_b, send_b, shards, *before):
        self.a, self.b, self.shards = keep_a, keep_b, shards
        send_a, send_b = after(send_a, *before), after(send_b, *before)
        self.got_a, self.got_b = swap(send_a, "fsdp", 1), swap(send_b, "fsdp", 1)

    def fold(self, size, *before):
        a, b, got_a, got_b = lax.optimization_barrier(
            (self.a, self.b, self.got_a, self.got_b, *before)
        )[:4]
        self.a, self.b = add_low(a[:size], got_a[:size]), add_low(b[:size], got_b[:size])
        self.out = add_low(a[size:], got_a[size:]), add_low(b[size:], got_b[size:])
        return self.out

    def second(self, *before, late=None):
        a, b = self.fold(self.shards, *before)
        wait = () if late is None else late(a, b)
        self.got_a, self.got_b = swap(a, "fsdp", 2), swap(after(b, *wait), "ctx", 1)

    def third(self, *before):
        a, b = self.fold(self.shards // 2, *before)
        self.got_a, self.got_b = swap(a, "ctx", 1), swap(b, "fsdp", 2)

    def outer(self, *before):
        a, b, got_a, got_b = lax.optimization_barrier(
            (self.a, self.b, self.got_a, self.got_b, *before)
        )[:4]
        self.last = jnp.concatenate([add_low(a, got_a), add_low(b, got_b)], 1)
        self.terms = scatter_outer(self.last, self.shards)

    def total(self, *before):
        return add_terms(self.terms, *before)[0]


def ctx_place(mask, shards):
    return (mask >> 1) + (shards // 2) * (mask & 1)


def place_a(cm, x_bit, shards):
    return ctx_place(cm, shards) + shards * x_bit


def place_b(cm, x_bit, shards):
    return (cm >> 1) + (shards // 2) * x_bit + shards * (cm & 1)


def arrange(out_ref, value, mine, feat):
    for k in range(value.shape[1] // feat):

        @pl.when(mine == k)
        def _():
            for m in range(value.shape[1] // feat):
                out_ref[:, m * feat : (m + 1) * feat] = value[:, (m ^ k) * feat : ((m ^ k) + 1) * feat]


def chunk_rows(parts, c, mc, fsdp, split, feat, shards, lanes):
    pieces = []
    for m in range(fsdp):
        a_ref, b_ref = parts[m & 1], parts[2 + (m & 1)]
        pieces.append(a_ref[place_a(c ^ mc, m >> 1, shards), :, lanes])
        pieces.append(b_ref[place_b(c ^ mc, m >> 1, shards), : feat - split, lanes])
    return jnp.concatenate(pieces, 0)


def dot(a, b):
    return lax.dot_general(a, b, (((1,), (0,)), ((), ())), preferred_element_type=F32)


def dot_nt(a, b):
    return lax.dot_general(a, b, (((1,), (1,)), ((), ())), preferred_element_type=F32)


def dot_tn(a, b):
    return lax.dot_general(a, b, (((0,), (0,)), ((), ())), preferred_element_type=F32)


def lane_ids():
    return lax.broadcasted_iota(jnp.int32, (1, 128), 1)


def turned(u):
    lane = lane_ids()
    first = (lane & (HEAD_DIM - 1)) < HEAD_DIM // 2
    return jnp.where(first, pltpu.roll(u, 96, 1), pltpu.roll(u, 32, 1))


def to_half(tile, source, target):
    return tile if source == target else pltpu.roll(tile, 64, 1)


def only_half(tile, half):
    lane = lane_ids()
    keep = lane >= 64 if half else lane < 64
    return jnp.where(keep, tile, 0.0)


def head_rows(h):
    return slice(h * 128, (h + 1) * 128)


def qkv_kernel(
    dims, meta, x_ref, ao_ref, as_ref, bo_ref, bs_ref, cos_ref, sin_ref,
    qp_ref, kv_ref, gain_ref, q_s, kv_s, n_s,
):
    shards, fsdp, cq, ck, split, feat = dims
    mc, mf = meta[shards], meta[shards + 1]
    parts = ao_ref, as_ref, bo_ref, bs_ref
    kvw = KEY_VALUE_HEADS * HEAD_DIM
    for c in range(shards):
        row = bo_ref[place_b(c ^ mc, 0, shards)][feat - split :, :].astype(F32)
        gain_ref[:, c * cq : (c + 1) * cq] = row[:, :cq]
        gain_ref[:, 640 + c * cq : 640 + (c + 1) * cq] = row[:, 128 : 128 + cq]
    x = x_ref[...].astype(F32)
    width = x.shape[1]
    rr = lax.rsqrt(jnp.mean(x * x, axis=-1, keepdims=True) + EPS)
    arrange(n_s, x * rr * gain_ref[0:1, :width], mf, feat)
    normed = n_s[...].astype(BF16)
    for c in range(shards):
        w = chunk_rows(parts, c, mc, fsdp, split, feat, shards, slice(0, 128))
        y = dot(normed, w)
        q_s[:, c * cq : (c + 1) * cq] = y[:, :cq]
        kv_s[:, c * ck : (c + 1) * ck] = y[:, cq : cq + ck]
        kv_s[:, kvw + c * ck : kvw + (c + 1) * ck] = y[:, cq + ck : cq + 2 * ck]
    cos, sin = cos_ref[...], sin_ref[...]
    for t in range(5):
        u = q_s[:, t * 128 : (t + 1) * 128]
        u = u * cos + turned(u) * sin
        for h in (2 * t, 2 * t + 1):
            if h < QUERY_HEADS:
                half = K_HALF[h // GROUP]
                qp_ref[head_rows(h), :] = (only_half(to_half(u, h % 2, half), half) * SCALE).astype(BF16)
    for t in range(3):
        u = kv_s[:, t * 128 : (t + 1) * 128]
        if t < 2:
            r = u * cos + turned(u) * sin
            u = r if t == 0 else jnp.where(lane_ids() < 64, r, u)
        kv_ref[:, t * 128 : (t + 1) * 128] = u.astype(BF16)


def score_mask(meta, shards, block, chunks, blk):
    mc = meta[shards]
    mine = meta[mc]
    r = lax.broadcasted_iota(jnp.int32, (blk, GROUP * 2 * blk), 1) & (2 * blk - 1)
    qpos = jnp.where(r < blk, mine * blk + r, (2 * shards - 1 - mine) * blk + r - blk)
    gap = qpos - lax.broadcasted_iota(jnp.int32, qpos.shape, 0)
    out = []
    for i in range(chunks):
        pair = meta[mc ^ (2 * (block * (chunks // 2) + i % (chunks // 2)) + i // (chunks // 2))]
        out.append(gap >= pair * blk)
        out.append(gap >= (2 * shards - 1 - pair) * blk)
    return out


def block_rows(refs, block, chunks, blocks):
    if blocks == 1:
        values = [r[...] for r in refs]
    else:
        values = [r[pl.ds(block * (chunks // 2), chunks // 2)] for r in refs]
    return jnp.concatenate([v.reshape(-1, v.shape[2]) for v in values], 0)


def masked(s, mask, blk):
    return jnp.concatenate(
        [jnp.where(m, s[i * blk : (i + 1) * blk], MASKED) for i, m in enumerate(mask)], 0
    )


def attend_kernel(dims, meta, qp_ref, *refs):
    *kv_refs, att_ref, ot_ref, lse_ref, m_s, l_s = refs
    shards, chunks, blk = dims
    blocks = shards // chunks
    rows = chunks * 2 * blk
    span = GROUP * 2 * blk

    def block_step(b, first):
        mask = score_mask(meta, shards, b, chunks, blk)
        kv = block_rows(kv_refs, b, chunks, blocks)
        for g in range(KEY_VALUE_HEADS):
            keys = kv[:, K_TILE[g] * 128 : (K_TILE[g] + 1) * 128]
            vals = kv[:, V_TILE[g] * 128 : (V_TILE[g] + 1) * 128]
            s = masked(dot_nt(keys, qp_ref[g * span : (g + 1) * span, :]), mask, blk)
            top = jnp.max(s, axis=0, keepdims=True)
            if not first:
                top = jnp.maximum(top, m_s[g : g + 1, :])
            p = jnp.exp(s - top)
            total = jnp.sum(p, axis=0, keepdims=True)
            out = dot_tn(vals, p.astype(BF16))
            if not first:
                fade = jnp.exp(m_s[g : g + 1, :] - top)
                total = total + l_s[g : g + 1, :] * fade
                out = out + ot_ref[g] * fade
            m_s[g : g + 1, :] = top
            l_s[g : g + 1, :] = total
            ot_ref[g] = out

    block_step(0, True)
    if blocks > 1:

        @pl.loop(1, blocks)
        def _(b):
            block_step(b, False)

    tiles = {}
    for g in range(KEY_VALUE_HEADS):
        o = ot_ref[g] / l_s[g : g + 1, :]
        ot_ref[g] = o
        lse_ref[g : g + 1, :] = m_s[g : g + 1, :] + jnp.log(l_s[g : g + 1, :])
        for j in range(GROUP):
            h = g * GROUP + j
            tile = jnp.transpose(o[:, j * 128 : (j + 1) * 128])
            tiles[h] = to_half(tile, V_HALF[g], h % 2)
    for t in range(5):
        if 2 * t + 1 < QUERY_HEADS:
            tile = jnp.where(lane_ids() < 64, tiles[2 * t], tiles[2 * t + 1])
            att_ref[:, t * 128 : (t + 1) * 128] = tile.astype(BF16)
        else:
            att_ref[:, t * 128 : t * 128 + 64] = tiles[2 * t][:, :64].astype(BF16)


def ffn_kernel(
    dims, meta, att_ref, x_ref, dy_ref, gain_ref, *refs
):
    shards, fsdp, cq, cg, feat, ffr, fsplit, split, packed, asplit = dims
    ins, refs = (refs[:6], refs[6:]) if packed else (refs[:2], refs[2:])
    parts, refs = refs[:4], refs[4:]
    (
        out_ref, ak_ref, as_ref, bk_ref, bs_ref, dmid_ref, ggain_ref, gp_ref,
        gu_s, hid_s, dh_s, dgu_s, wide_s, p_s, dt_s,
    ) = refs
    mc, mf = meta[shards], meta[shards + 1]
    lanes = ak_ref.shape[2]
    if packed:
        for c in range(0, shards, 2):
            for m in range(fsdp):
                b_ref = ins[4 + (m & 1)]
                pair = [b_ref[place_b(d ^ mc, m >> 1, shards)][feat - fsplit :] for d in (c, c + 1)]
                dt_s[m, c * cq : (c + 2) * cq, :] = jnp.concatenate(
                    [p.astype(F32) for p in pair], 0
                ).astype(BF16)
    else:
        for m in range(fsdp):
            dt_s[m] = ins[1][mf ^ m]

    def weights(c):
        if packed:
            pieces = []
            for m in range(fsdp):
                pieces.append(ins[2 * (m & 1) + (m >> 1)][ctx_place(c ^ mc, shards)])
                if fsplit < feat:
                    b_ref = ins[4 + (m & 1)]
                    pieces.append(b_ref[place_b(c ^ mc, m >> 1, shards), : feat - fsplit, :])
            return jnp.concatenate(pieces, 0)
        return jnp.concatenate([ins[0][c, mf ^ m] for m in range(fsdp)], 0)

    def outer(c):
        return chunk_rows(parts, c, mc, fsdp, asplit, feat, shards, slice(-128, None))

    x = x_ref[...].astype(F32)
    width = x.shape[1]
    dy_t = dy_ref[...]
    dyf = jnp.transpose(dy_t.astype(F32))
    dyl = dyf.astype(BF16)
    gain = gain_ref[0:1, 640 : 640 + width]
    arrange(p_s, att_ref[...].astype(F32), mf, feat)
    attp = p_s[...].astype(BF16)
    for c in range(shards):
        wide_s[:, c * cq : (c + 1) * cq] = dot(attp, outer(c))[:, :cq]
    mid = x + wide_s[:, :width]
    rr = lax.rsqrt(jnp.mean(mid * mid, axis=-1, keepdims=True) + EPS)
    z = mid * rr
    arrange(p_s, z * gain, mf, feat)
    normed = p_s[...].astype(BF16)
    normed_t = jnp.transpose(p_s[...]).astype(BF16)

    def store_grad(c, m, row, value):
        end = row + value.shape[0]
        here = slice(0, value.shape[1])
        if row < split:
            stop = min(end, split)
            ref = (ak_ref, as_ref)[m & 1]
            ref[place_a(c ^ mc, m >> 1, shards), row:stop, here] = value[: stop - row]
        if end > split:
            start = max(row, split)
            ref = (bk_ref, bs_ref)[m & 1]
            ref[place_b(c ^ mc, m >> 1, shards), start - split : end - split, here] = value[start - row :]

    for c in range(shards):
        gu = dot(normed, weights(c))
        gu_s[c] = gu
        gate, up = gu[:, :cg], gu[:, cg : 2 * cg]
        hid_s[:, c * cg : (c + 1) * cg] = gate * jax.nn.sigmoid(gate) * up
    out = mid
    for m in range(fsdp):
        here = pl.ds(pl.multiple_of((mf ^ m) * ffr, 128), ffr)
        hid = hid_s[:, here].astype(BF16)
        out = out + dot_nt(hid, dt_s[m])
        dh_s[:, here] = dot(dyl, dt_s[m])
        g = dot(dy_t, hid)
        for c in range(shards):
            piece = g[c * cq : (c + 1) * cq, :].astype(BF16)
            for t in range(ffr // lanes):
                store_grad(c, m, feat + t * cq, piece[:, t * lanes : (t + 1) * lanes])
    out_ref[...] = jnp.transpose(out).astype(BF16)
    dn = jnp.zeros_like(mid)
    for c in range(shards):
        gu = gu_s[c]
        gate, up = gu[:, :cg], gu[:, cg : 2 * cg]
        dh = dh_s[:, c * cg : (c + 1) * cg]
        sg = jax.nn.sigmoid(gate)
        if 2 * cg < dgu_s.shape[1]:
            dgu_s[...] = jnp.zeros_like(dgu_s)
        dgu_s[:, :cg] = dh * up * sg * (1.0 + gate * (1.0 - sg))
        dgu_s[:, cg : 2 * cg] = dh * gate * sg
        dgu = dgu_s[...].astype(BF16)
        g = dot(normed_t, dgu)
        for m in range(fsdp):
            store_grad(c, m, 0, g[m * feat : (m + 1) * feat, :].astype(BF16))
        dn = dn + dot_nt(dgu, weights(c))
    arrange(p_s, dn, mf, feat)
    dn = p_s[...]
    e = dn * gain
    dmid = dyf + rr * (e - z * jnp.mean(e * z, axis=-1, keepdims=True))
    dmid_ref[...] = dmid
    ggain_ref[...] = jnp.broadcast_to(jnp.sum(dn * z, axis=0, keepdims=True), ggain_ref.shape)
    wide_s[...] = jnp.zeros_like(wide_s)
    wide_s[:, :width] = dmid
    ga = jnp.zeros_like(mid)
    for c in range(shards):
        gb = wide_s[:, c * cq : c * cq + 128].astype(BF16)
        ga = ga + dot_nt(gb, outer(c))
    arrange(p_s, ga, mf, feat)
    wide_s[:, :width] = p_s[...]
    for h in range(QUERY_HEADS):
        half = V_HALF[h // GROUP]
        tile = wide_s[:, (h // 2) * 128 : (h // 2 + 1) * 128]
        gp_ref[head_rows(h), :] = only_half(to_half(tile, h % 2, half), half).astype(BF16)


def attend_back_kernel(
    dims, meta, qp_ref, gp_ref, ot_ref, lse_ref, cos_ref, sin_ref, *refs
):
    *kv_refs, dq_ref, dnear_ref, dfar_ref, dq_s = refs
    shards, chunks, blk = dims
    blocks = shards // chunks
    rows = chunks * 2 * blk
    span = GROUP * 2 * blk
    deltas = []
    for g in range(KEY_VALUE_HEADS):
        gt = jnp.transpose(gp_ref[g * span : (g + 1) * span, :].astype(F32))
        deltas.append(jnp.sum(gt * ot_ref[g], axis=0, keepdims=True))

    def block_step(b, first):
        mask = score_mask(meta, shards, b, chunks, blk)
        kv = block_rows(kv_refs, b, chunks, blocks)
        tiles = [None, None, None]

        def put(t, value):
            tiles[t] = value if tiles[t] is None else tiles[t] + value

        for g in range(KEY_VALUE_HEADS):
            keys = kv[:, K_TILE[g] * 128 : (K_TILE[g] + 1) * 128]
            vals = kv[:, V_TILE[g] * 128 : (V_TILE[g] + 1) * 128]
            qg = qp_ref[g * span : (g + 1) * span, :]
            gg = gp_ref[g * span : (g + 1) * span, :]
            s = masked(dot_nt(keys, qg), mask, blk)
            p = jnp.exp(s - lse_ref[g : g + 1, :])
            ds = (p * (dot_nt(vals, gg) - deltas[g])).astype(BF16)
            put(V_TILE[g], dot(p.astype(BF16), gg))
            put(K_TILE[g], dot(ds, qg))
            dq = dot_tn(ds, keys)
            if first:
                dq_s[g * span : (g + 1) * span, :] = dq
            else:
                dq_s[g * span : (g + 1) * span, :] += dq
        for t in range(3):
            tile = tiles[t].astype(BF16).reshape(2, chunks // 2, 2 * blk, 128)
            for n, ref in enumerate((dnear_ref, dfar_ref)):
                ref[pl.ds(b * (chunks // 2), chunks // 2), :, t * 128 : (t + 1) * 128] = tile[n]

    block_step(0, True)
    if blocks > 1:

        @pl.loop(1, blocks)
        def _(b):
            block_step(b, False)

    cos, sin = cos_ref[...], sin_ref[...]
    tiles = {}
    for h in range(QUERY_HEADS):
        u = dq_s[head_rows(h), :] * SCALE
        tiles[h] = to_half(u * cos - turned(u) * sin, K_HALF[h // GROUP], h % 2)
    for t in range(5):
        if 2 * t + 1 < QUERY_HEADS:
            tile = jnp.where(lane_ids() < 64, tiles[2 * t], tiles[2 * t + 1])
            dq_ref[:, t * 128 : (t + 1) * 128] = tile.astype(BF16)
        else:
            dq_ref[:, t * 128 : t * 128 + 64] = tiles[2 * t][:, :64].astype(BF16)


def qkv_back_kernel(
    dims, meta, x_ref, dq_ref, dkv_ref, att_ref, dmid_ref, gain_ref, gg_ref,
    cos_ref, sin_ref, ao_ref, as_in, bo_ref, bs_in, gin_ref, ak_ref, as_ref, bk_ref, bs_ref,
    dq_s, dkv_s, d_s, p_s, gg_s,
):
    shards, fsdp, cq, ck, split, feat = dims
    mc, mf = meta[shards], meta[shards + 1]
    parts = ao_ref, as_in, bo_ref, bs_in
    kvw = KEY_VALUE_HEADS * HEAD_DIM
    x = x_ref[...].astype(F32)
    width = x.shape[1]
    gain = gain_ref[0:1, :width]
    rr = lax.rsqrt(jnp.mean(x * x, axis=-1, keepdims=True) + EPS)
    z = x * rr
    arrange(p_s, z * gain, mf, feat)
    normed_t = jnp.transpose(p_s[...]).astype(BF16)
    arrange(p_s, att_ref[...].astype(F32), mf, feat)
    att_t = jnp.transpose(p_s[...]).astype(BF16)
    cos, sin = cos_ref[...], sin_ref[...]
    for t in range(3):
        u = dkv_ref[:, t * 128 : (t + 1) * 128]
        if t < 2:
            r = u * cos - turned(u) * sin
            u = r if t == 0 else jnp.where(lane_ids() < 64, r, u)
        dkv_s[:, t * 128 : (t + 1) * 128] = u
    dq_s[...] = dq_ref[...].astype(F32)
    d_s[...] = jnp.zeros_like(d_s)
    dn = jnp.zeros_like(x)
    for c in range(shards):
        d_s[:, :cq] = dq_s[:, c * cq : (c + 1) * cq]
        d_s[:, cq : cq + ck] = dkv_s[:, c * ck : (c + 1) * ck]
        d_s[:, cq + ck : cq + 2 * ck] = dkv_s[:, kvw + c * ck : kvw + (c + 1) * ck]
        d_s[:, 128 : 128 + cq] = dmid_ref[:, c * cq : (c + 1) * cq]
        d = d_s[...].astype(BF16)
        w = chunk_rows(parts, c, mc, fsdp, split, feat, shards, slice(0, 128))
        dn = dn + dot_nt(d[:, :128], w)
        g = jnp.concatenate([dot(normed_t, d[:, :128]), dot(att_t, d[:, 128:])], 1).astype(BF16)
        for m in range(fsdp):
            part = g[m * feat : (m + 1) * feat, :]
            (ak_ref, as_ref)[m & 1][place_a(c ^ mc, m >> 1, shards)] = part[:split]
            (bk_ref, bs_ref)[m & 1][place_b(c ^ mc, m >> 1, shards), : feat - split] = part[split:]
    arrange(p_s, dn, mf, feat)
    dn = p_s[...]
    e = dn * gain
    gin = dmid_ref[...] + rr * (e - z * jnp.mean(e * z, axis=-1, keepdims=True))
    gin_ref[...] = jnp.transpose(gin)
    gg_s[...] = jnp.broadcast_to(jnp.sum(dn * z, axis=0, keepdims=True), gg_s.shape)
    for c in range(shards):
        d_s[0:8, 0:cq] = gg_s[:, c * cq : (c + 1) * cq]
        d_s[0:8, 128 : 128 + cq] = gg_ref[:, c * cq : (c + 1) * cq]
        gains = d_s[0:8, :].astype(BF16)
        for m in range(fsdp):
            (bk_ref, bs_ref)[m & 1][place_b(c ^ mc, m >> 1, shards), feat - split :] = gains


def pack_kernel(wq_ref, wkt_ref, wvt_ref, wo_ref, ga_ref, gf_ref, own_ref, t_s):
    feat, cq = wq_ref.shape
    ck = wkt_ref.shape[0]
    t_s[...] = jnp.zeros_like(t_s)
    t_s[:feat, :cq] = wq_ref[...].astype(F32)
    t_s[:feat, cq : cq + ck] = jnp.transpose(wkt_ref[...].astype(F32))
    t_s[:feat, cq + ck : cq + 2 * ck] = jnp.transpose(wvt_ref[...].astype(F32))
    t_s[:feat, 128 : 128 + cq] = wo_ref[...].astype(F32)
    t_s[feat : feat + 1, :cq] = ga_ref[...].astype(F32)
    t_s[feat : feat + 1, 128 : 128 + cq] = gf_ref[...].astype(F32)
    own_ref[...] = t_s[...].astype(BF16)


def finish_kernel(ck, *refs):
    *terms, gq_ref, gkt_ref, gvt_ref, go_ref, ga_ref, gf_ref = refs
    feat, cq = gq_ref.shape
    total = functools.reduce(lambda a, b: a + b, [t[...].astype(F32) for t in terms])
    gq_ref[...] = total[:feat, :cq]
    turned_round = jnp.transpose(total[:feat, :128])
    gkt_ref[...] = turned_round[cq : cq + ck]
    gvt_ref[...] = turned_round[cq + ck : cq + 2 * ck]
    go_ref[...] = total[:feat, 128 : 128 + cq]
    ga_ref[...] = total[feat : feat + 1, :cq]
    gf_ref[...] = total[feat : feat + 1, 128 : 128 + cq]


def call(kernel, outs, scratch, flops, moved, *args, on_chip=False, leave=(), scalars=1):
    smem = pl.BlockSpec(memory_space=pltpu.SMEM)
    vmem = pl.BlockSpec(memory_space=pltpu.VMEM)
    if on_chip:
        held = [pltpu.with_memory_space_constraint(a, pltpu.VMEM) for a in args[scalars:]]
        args = (*args[:scalars], *held)
        outs = [
            o if n in leave else pltpu.VMEM(o.shape, o.dtype) for n, o in enumerate(outs)
        ]
    return pl.pallas_call(
        kernel,
        out_shape=outs,
        in_specs=[smem] * scalars + [vmem] * (len(args) - scalars),
        out_specs=[vmem] * len(outs),
        scratch_shapes=scratch,
        cost_estimate=pl.CostEstimate(flops=flops, bytes_accessed=moved, transcendentals=0),
        compiler_params=pltpu.CompilerParams(vmem_limit_bytes=CHIP_BYTES if on_chip else VMEM_BYTES),
    )(*args)


def arr(shape, dtype):
    return jax.ShapeDtypeStruct(shape, dtype)


def on_device(
    tokens, pair_of, gain_attn, w_query, key_weight, value_weight, w_out, gain_ffn,
    w_gate, w_up, w_down, cotangent,
):
    rows, width = tokens.shape[1:]
    blk = rows // 2
    shards, fsdp = lax.axis_size("ctx"), lax.axis_size("fsdp")
    feat, cq = w_query.shape
    ck, cg, ffr = key_weight.shape[1], w_gate.shape[1], w_down.shape[0]
    ff = cg * shards
    x, dy = tokens[0], cotangent[0]
    meta = jnp.concatenate(
        [pair_of[0], jnp.stack([lax.axis_index("ctx"), lax.axis_index("fsdp")]).astype(jnp.int32)]
    )

    def fill(parts, total):
        used = sum(p.shape[1] for p in parts)
        return parts + [jnp.zeros((parts[0].shape[0], total - used), BF16)]

    lanes = 256
    if cq % 8 == 0 and ck % 8 == 0:
        (own,) = call(
            pack_kernel, [pltpu.VMEM((feat + 8, lanes), BF16)], [pltpu.VMEM((feat + 8, lanes), F32)],
            0, 200_000,
            w_query, key_weight.T, value_weight.T, w_out, gain_attn[None], gain_ffn[None],
            scalars=0,
        )
    else:
        body = jnp.concatenate(
            fill([w_query, key_weight, value_weight], 128) + fill([w_out], 128), 1
        )
        gains_row = jnp.concatenate(fill([gain_attn[None]], 128) + fill([gain_ffn[None]], 128), 1)
        own = jnp.concatenate([body, jnp.broadcast_to(gains_row, (8, lanes))], 0)
    split = 80

    cgl = round_up(2 * cg, 128)
    gu_own = jnp.concatenate(fill([w_gate, w_up], cgl), 1)
    dt_own = w_down.T
    packed = cgl == ffr and cq % 8 == 0
    ffn_split = feat
    if packed:
        ffn = Gather(jnp.concatenate([gu_own, dt_own], 0), ffn_split, shards)
    else:
        gu_all = lax.all_gather(gu_own, ("ctx", "fsdp"), axis=0).reshape(shards, fsdp, feat, cgl)
        dt_all = lax.all_gather(dt_own, ("ctx", "fsdp"), axis=0).reshape(shards, fsdp, cq, ffr)
        ffn_in = (gu_all, dt_all.transpose(1, 0, 2, 3).reshape(fsdp, width, ffr))

    attn = Gather(own, split, shards)
    attn.outer()
    attn.second()
    if packed:
        ffn.outer(*attn.now)
    attn.third()
    if packed:
        attn_in = attn.cores(ffn.a[3], ffn.b[3])
        ffn.second()
    else:
        attn_in = attn.cores()

    my_pair = pair_of[0, lax.axis_index("ctx")]
    offsets = jnp.arange(blk, dtype=jnp.int32)
    pos = jnp.concatenate([my_pair * blk + offsets, (2 * shards - 1 - my_pair) * blk + offsets])
    freq = THETA ** (-jnp.arange(HEAD_DIM // 2, dtype=F32) * 2.0 / HEAD_DIM)
    angles = pos.astype(F32)[:, None] * freq[None, :]
    cos, sin = jnp.cos(angles), jnp.sin(angles)
    cos_t = jnp.concatenate([cos] * 4, 1)
    sin_t = jnp.concatenate([-sin, sin] * 2, 1)

    kvl = 2 * KEY_VALUE_HEADS * HEAD_DIM
    hrows = QUERY_HEADS * rows
    qp, kv, gains = call(
        functools.partial(qkv_kernel, (shards, fsdp, cq, ck, split, feat)),
        [
            arr((hrows, 128), BF16), arr((rows, kvl), BF16),
            arr((8, 1280), F32),
        ],
        [
            pltpu.VMEM((rows, 640), F32), pltpu.VMEM((rows, kvl), F32),
            pltpu.VMEM((rows, width), F32),
        ],
        2 * rows * width * 128 * shards, 6_000_000,
        meta, x, *attn_in, cos_t, sin_t, on_chip=packed,
    )

    kv_pieces = gather_outer(kv[None], shards)
    kv_near = join(kv_pieces)
    if packed:
        cut = kv_near.shape[0] * 3 // 4
        kv_far = [swap(kv_near[:cut], "ctx", 1), swap(kv_near[cut:], "ctx", 1)]
        ffn.third(kv_pieces[1])
        ffn_in = ffn.cores_apart(kv_far[0])
    else:
        kv_far = [swap(kv_near, "ctx", 1)]
    chunks = min(8, shards)
    span = GROUP * rows
    att, ot, lse = call(
        functools.partial(attend_kernel, (shards, chunks, blk)),
        [arr((rows, width), BF16), arr((KEY_VALUE_HEADS, 128, span), F32), arr((8, span), F32)],
        [pltpu.VMEM((8, span), F32), pltpu.VMEM((8, span), F32)],
        4 * hrows * shards * rows * 128, 3_000_000,
        meta, qp, kv_near, *kv_far, on_chip=packed,
    )

    glanes = cgl
    tiles = ffr // glanes
    parts = [arr((2 * shards, feat, glanes), BF16)] * 2
    parts += [arr((2 * shards, tiles * cq, glanes), BF16)] * 2
    out, *g_ffn, dmid, ggain, gp = call(
        functools.partial(
            ffn_kernel, (shards, fsdp, cq, cg, feat, ffr, ffn_split, feat, packed, split)
        ),
        [arr((width, rows), BF16), *parts]
        + [arr((rows, width), F32), arr((8, width), F32), arr((hrows, 128), BF16)],
        [
            pltpu.VMEM((shards, rows, cgl), F32), pltpu.VMEM((rows, ff), F32),
            pltpu.VMEM((rows, ff), F32), pltpu.VMEM((rows, cgl), F32), pltpu.VMEM((rows, 768), F32),
            pltpu.VMEM((rows, width), F32), pltpu.VMEM((fsdp, width, ffr), BF16),
        ],
        18 * rows * width * ff, 14_000_000,
        meta, att, x, dy.T, gains, *ffn_in, *(attn_in if packed else [p[:, :, 128:] for p in attn_in]),
        on_chip=packed, leave=(0,),
    )
    ffn_sum = Scatter(*g_ffn, shards)
    dq, dkv_near, dkv_far = call(
        functools.partial(attend_back_kernel, (shards, chunks, blk)),
        [arr((rows, width), BF16)] + [arr((shards // 2, rows, kvl), BF16)] * 2,
        [pltpu.VMEM((hrows, 128), F32)],
        10 * hrows * shards * rows * 128, 5_000_000,
        meta, qp, gp, ot, lse, cos_t, sin_t, kv_near, *kv_far, on_chip=packed,
    )
    dkv_got = []

    def send_far(*sent):
        dkv_got.append(swap(after(dkv_far, *sent), "ctx", 1))
        return dkv_got

    ffn_sum.second(late=send_far)
    dkv_terms = scatter_outer(add_low(dkv_near, dkv_got[0]), shards)
    ffn_sum.third()
    dkv = add_terms(dkv_terms, *ffn_sum.out)[0]

    grad_input, *g_attn = call(
        functools.partial(qkv_back_kernel, (shards, fsdp, cq, ck, split, feat)),
        [arr((width, rows), F32)]
        + [arr((2 * shards, split, lanes), BF16)] * 2
        + [arr((2 * shards, feat + 8 - split, lanes), BF16)] * 2,
        [
            pltpu.VMEM((rows, width), F32), pltpu.VMEM((rows, kvl), F32),
            pltpu.VMEM((rows, lanes), F32), pltpu.VMEM((rows, width), F32),
            pltpu.VMEM((8, width), F32),
        ],
        6 * rows * width * 256 * shards, 6_000_000,
        meta, x, dq, dkv, att, dmid, gains, ggain, cos_t, sin_t, *attn_in,
        on_chip=packed, leave=(0,),
    )
    attn_sum = Scatter(*g_attn, shards)
    attn_sum.second(ffn_sum.got_a, ffn_sum.got_b)
    ffn_sum.outer()
    attn_sum.third()
    attn_sum.outer()
    ffn_own = ffn_sum.total(attn_sum.last)
    if packed:
        gq, gkt, gvt, go, gain_a, gain_f = call(
            functools.partial(finish_kernel, ck),
            [arr((feat, cq), F32)] + [arr((ck, feat), F32)] * 2
            + [arr((feat, cq), F32)] + [arr((1, cq), F32)] * 2,
            [], 0, 400_000, *[t[0] for t in attn_sum.terms],
            on_chip=True, leave=range(6), scalars=0,
        )
        attn_grads = gq, gkt.T, gvt.T, go
        gain_grads = gain_a[0], gain_f[0]
    else:
        attn_own = attn_sum.total()
        attn_grads = (
            attn_own[:feat, :cq], attn_own[:feat, cq : cq + ck],
            attn_own[:feat, cq + ck : cq + 2 * ck], attn_own[:feat, 128 : 128 + cq],
        )
        gain_grads = attn_own[feat, :cq], attn_own[feat, 128 : 128 + cq]
    down_rows = ffn_own[feat:]
    grad_down = jnp.concatenate([down_rows[t * cq : (t + 1) * cq] for t in range(tiles)], 1).T
    return (
        out.T[None], grad_input.T[None], gain_grads[0], *attn_grads, gain_grads[1],
        ffn_own[:feat, :cg], ffn_own[:feat, cg : 2 * cg], grad_down,
    )


def solution(mesh):
    weights = (P("fsdp", "ctx"),) * 4
    data = P("fsdp", "ctx", None)
    in_specs = (
        (data, P("fsdp", None), P("ctx")) + weights + (P("ctx"),) + weights[:3] + (data,)
    )
    out_specs = (data, data, P("ctx")) + weights + (P("ctx"),) + weights[:3]
    return jax.shard_map(
        on_device, mesh=mesh, in_specs=in_specs, out_specs=out_specs, check_vma=False
    )
```
